32 devices in a mesh: dp: 8 (over z, x), tensor: 4 (over y, core).
Axes of the slice: x: 2, y: 2, z: 4, core: 2. Of those that a mesh axis runs over, the one named last changes fastest.
Arguments:
- tokens: bfloat16 [48, 260, 768], P('dp'), may hold values from -6 to 6
- cotangent: bfloat16 [48, 260, 768], P('dp'), may hold values from -6 to 6
- split_point: int32 [48], P('dp'), may hold values from 0 to 32
- w_qkv: bfloat16 [3, 768, 768], P(None, None, 'tensor'), may hold values from -0.21875 to 0.21875
- w_out: bfloat16 [768, 768], P('tensor'), may hold values from -0.75 to 0.75
- w_up: bfloat16 [768, 3072], P(None, 'tensor'), may hold values from -0.21875 to 0.21875
- w_down: bfloat16 [3072, 768], P('tensor'), may hold values from -0.109375 to 0.109375
- gain_one: float32 [768], replicated, may hold values from 0.1 to 1.9
- shift_one: float32 [768], replicated, may hold values from -3 to 3
- gain_two: float32 [768], replicated, may hold values from 0.1 to 1.9
- shift_two: float32 [768], replicated, may hold values from -3 to 3
Outputs:
- output: bfloat16 [48, 260, 768], P('dp')
- grad_tokens: bfloat16 [48, 260, 768], P('dp')
- grad_qkv: float32 [3, 768, 768], P(None, 'dp', 'tensor')
- grad_out: float32 [768, 768], P('tensor', 'dp')
- grad_up: float32 [768, 3072], P('dp', 'tensor')
- grad_down: float32 [3072, 768], P('tensor', 'dp')
- grad_gain_one: float32 [768], P('dp')
- grad_shift_one: float32 [768], P('dp')
- grad_gain_two: float32 [768], P('dp')
- grad_shift_two: float32 [768], P('dp')
The draws below stay inside these ranges and needn't reach their ends.
All inputs are finite; a program needn't handle non-finite values.
Results may differ from the reference program's by a relative error of at most 0.013.
Values sent between devices are 32-bit elements; how exact they have to be, the bound alone decides.
A program may use at most 128 MiB of HBM per device.

```python
import jax
import jax.numpy as jnp
from jax import lax

D = 768
HD = 64
FF = 3072
PATCHES = 196
MAXSPLIT = 32
B_DEV = 6
SEQ = 260
B = 48


def with_ends(drawn, stream_key, low, top_value):
    extent = drawn.shape
    place = [jax.random.randint(jax.random.fold_in(stream_key, axis), (), 0, extent[axis]) for axis in range(len(extent))]
    drawn = drawn.at[tuple(place)].set(low)
    longest = extent.index(max(extent))
    place[longest] = (place[longest] + 1) % extent[longest]
    return drawn.at[tuple(place)].set(top_value)


def spiked(entries, stream_key, source, target, parts, factor):
    def block_of(axis_at):
        return (jnp.arange(entries.shape[axis_at]) // (entries.shape[axis_at] // parts)).reshape((-1,) + (1,) * (entries.ndim - 1 - axis_at))

    first = jax.random.permutation(stream_key, parts)[block_of(target)]
    second = (block_of(target) + parts // 2) % parts
    return jnp.where((block_of(source) == first) | (block_of(source) == second), factor * entries, entries)


def block_levels(key, shape, pieces, smallest, high):
    def one(dim, blocks):
        heights = jax.random.uniform(jax.random.fold_in(jax.random.fold_in(key, 6), dim), (blocks,), jnp.float32, smallest / len(pieces), high / len(pieces))
        return jnp.repeat(jnp.exp(heights), shape[dim] // blocks).reshape((-1,) + (1,) * (len(shape) - dim - 1))

    level = one(*pieces[0])
    for cut in pieces[1:]:
        level = level * one(*cut)
    return level


def scatter_about(key, extent, scale, most, pieces=(), kind=jnp.bfloat16):
    entries = scale * jax.random.normal(key, extent, jnp.float32)
    if pieces:
        entries = entries * block_levels(key, extent, pieces, -0.22, 0.18)
    return jnp.clip(entries, -most, most).astype(kind)


def gaussian_with(own_key, shape, spread, bound, split, heavy, kind=jnp.bfloat16):
    array = spread * jax.random.normal(own_key, shape, jnp.float32)
    if split:
        array = array * block_levels(own_key, shape, split, -0.22, 0.18)
    return jnp.clip(spiked(array, jax.random.fold_in(own_key, 3), *heavy), -bound, bound).astype(kind)


def setup_inputs(seed: int = 0) -> dict:
    seeds = jax.random.split(jax.random.key(seed), 12)
    return {
        "tokens": scatter_about(seeds[0], (B, SEQ, D), 1.0, 6.0, ((0, 8),)),
        "cotangent": gaussian_with(seeds[1], (B, SEQ, D), 1.0, 6.0, ((0, 8),), (0, 2, 8, 2.0)),
        "split_point": with_ends(jax.random.randint(seeds[2], (B,), 0, MAXSPLIT + 1), jax.random.fold_in(seeds[2], 1), 0, MAXSPLIT).astype(jnp.int32),
        "w_qkv": scatter_about(seeds[3], (3, D, D), D ** -0.5, 0.21875, ((2, 4),)),
        "w_out": scatter_about(seeds[4], (D, D), HD ** -0.5, 0.75, ((0, 4),)),
        "w_up": scatter_about(seeds[5], (D, FF), D ** -0.5, 0.21875, ((1, 4),)),
        "w_down": scatter_about(seeds[6], (FF, D), FF ** -0.5, 0.109375, ((0, 4),)),
        "gain_one": jnp.clip(1.0 + 0.18 * jax.random.normal(seeds[7], (D,), jnp.float32), 0.1, 1.9),
        "shift_one": scatter_about(seeds[8], (D,), 0.5, 3.0, (), jnp.float32),
        "gain_two": jnp.clip(1.0 + 0.18 * jax.random.normal(seeds[9], (D,), jnp.float32), 0.1, 1.9),
        "shift_two": scatter_about(seeds[10], (D,), 0.5, 3.0, (), jnp.float32),
    }


EPSILON = 1e-05

@jax.custom_vjp
def low(v):
    return lax.optimization_barrier(v.astype(jnp.bfloat16)).astype(jnp.float32)

@jax.custom_vjp
def low_back(v):
    return v

def low_keep(v):
    return (low(v), None)

def low_pass(kept, grad):
    return (grad,)

def back_keep(v):
    return (v, None)

def back_low(kept, grad):
    return (low(grad),)
low.defvjp(low_keep, low_pass)
low_back.defvjp(back_keep, back_low)

def layer_norm(values, gain_vec, shift_vec):
    row_mean = lax.optimization_barrier(jnp.mean(values, axis=-1, keepdims=True))
    centered = values - row_mean
    variance = lax.optimization_barrier(jnp.mean(centered * centered, axis=-1, keepdims=True))
    return centered * lax.rsqrt(variance + EPSILON) * gain_vec + shift_vec

def matmul(left, right):
    return jnp.matmul(left, right, precision=lax.Precision.HIGHEST)

def forward(inputs, split_point, w_qkv, w_out, w_up, w_down, gain_one, shift_one, gain_two, shift_two):
    groups, length, width = inputs.shape
    head_count = width // HD
    score_scale = HD ** (-0.5)
    places = jnp.arange(length, dtype=jnp.int32)
    limit = jnp.maximum(places[None, :, None], PATCHES + split_point[:, None, None] - 1)
    allowed = places[None, None, :] <= limit
    normed = low(layer_norm(inputs, gain_one, shift_one))
    packed = jnp.einsum('gtd,cde->cgte', normed, w_qkv, precision=lax.Precision.HIGHEST)
    packed = low(low_back(packed))
    queries = packed[0].reshape(groups, length, head_count, HD)
    keys = packed[1].reshape(groups, length, head_count, HD)
    values = packed[2].reshape(groups, length, head_count, HD)
    scores = jnp.einsum('gqhe,gkhe->ghqk', queries, keys, precision=lax.Precision.HIGHEST) * score_scale
    scores = low_back(scores)
    scores = jnp.where(allowed[:, None], scores, -1e+30)
    log_total = jax.nn.logsumexp(scores, axis=-1, keepdims=True)
    attn_probs = low(jnp.exp(scores - log_total))
    mixed = jnp.einsum('ghqk,gkhe->gqhe', attn_probs, values, precision=lax.Precision.HIGHEST)
    mixed = low(low_back(mixed.reshape(groups, length, width)))
    middle = inputs + low_back(matmul(mixed, w_out))
    normed_two = low(layer_norm(middle, gain_two, shift_two))
    pre_act = low_back(matmul(normed_two, w_up))
    activated = low(jax.nn.gelu(pre_act, approximate=False))
    return middle + low_back(matmul(activated, w_down))

def reference(tokens, cotangent, split_point, w_qkv, w_out, w_up, w_down, gain_one, shift_one, gain_two, shift_two):
    params = (w_qkv.astype(jnp.float32), w_out.astype(jnp.float32), w_up.astype(jnp.float32), w_down.astype(jnp.float32), gain_one.astype(jnp.float32), shift_one.astype(jnp.float32), gain_two.astype(jnp.float32), shift_two.astype(jnp.float32))
    inputs = tokens.astype(jnp.float32).reshape(-1, B_DEV, SEQ, D)
    grads_in = cotangent.astype(jnp.float32).reshape(-1, B_DEV, SEQ, D)
    splits = split_point.reshape(-1, B_DEV)

    def group_step(totals, group_item):
        group_in, group_grad, group_split = group_item

        def apply(values, *weights):
            return forward(values, group_split, *weights)
        result, pullback = jax.vjp(apply, group_in, *params)
        pulled = pullback(group_grad)
        totals = jax.tree.map(jnp.add, totals, tuple(pulled[1:]))
        return (totals, (result.astype(jnp.bfloat16), pulled[0].astype(jnp.bfloat16)))
    start = tuple((jnp.zeros_like(weight) for weight in params))
    totals, outs = lax.scan(group_step, start, (inputs, grads_in, splits))
    results, grad_inputs = outs
    return (results.reshape(tokens.shape), grad_inputs.reshape(tokens.shape), totals[0], totals[1], totals[2], totals[3], totals[4], totals[5], totals[6], totals[7])
```

```python
from functools import partial

import jax
import jax.numpy as jnp
from jax import lax
from jax.experimental import pallas as pl
from jax.experimental.pallas import tpu as pltpu
from jax.sharding import PartitionSpec as P

HD = 64
PATCHES = 196
EPSILON = 1e-05
MESH = pl.DeviceIdType.MESH
F32 = jnp.float32
BF16 = jnp.bfloat16
ANY = pl.BlockSpec(memory_space=pl.ANY)
VM = pl.BlockSpec(memory_space=pltpu.VMEM)
SM = pl.BlockSpec(memory_space=pltpu.SMEM)
VLIM = 60 * 1024 * 1024
NT = (((1,), (1,)), ((), ()))


def mm(a, b):
    return jnp.dot(a, b, preferred_element_type=F32)


def mm_nt(a, b):
    return lax.dot_general(a, b, NT, preferred_element_type=F32)


def mm_tn(a, b):
    return lax.dot_general(a, b, (((0,), (0,)), ((), ())), preferred_element_type=F32)


class Place:
    def __init__(self):
        d, t = lax.axis_index("dp"), lax.axis_index("tensor")
        self.d, self.t = d, t
        self.z, self.x = d // 2, lax.rem(d, 2)
        self.y, self.c = t // 2, lax.rem(t, 2)
        self.sib = (d, self.y * 2 + 1 - self.c)
        self.ynb = (d, (1 - self.y) * 2 + self.c)
        self.xnb = (self.z * 2 + 1 - self.x, t)

    def zof(self, k):
        return lax.rem(self.z + k, 4)

    def znb(self, k):
        return (self.zof(k) * 2 + self.x, self.t)


def greet(place, with_y, with_dp):
    peers = [place.sib, place.xnb] + [place.znb(k) for k in (1, 2, 3)]
    if with_y:
        peers.append(place.ynb)
    if with_dp:
        peers += [(place.zof(k) * 2 + 1 - place.x, place.t) for k in (1, 2, 3)]
    barrier = pltpu.get_barrier_semaphore()
    for p in peers:
        pl.semaphore_signal(barrier, 1, device_id=p, device_id_type=MESH)
    pl.semaphore_wait(barrier, len(peers))


def rcopy(src, dst, ssem, rsem, dev):
    return pltpu.make_async_remote_copy(
        src_ref=src, dst_ref=dst, send_sem=ssem, recv_sem=rsem, device_id=dev, device_id_type=MESH
    )


def gather_kernel(own, wf, lsem, csend, crecv, ysend, yrecv, zsend, xsend, brecv):
    me = Place()
    greet(me, True, False)
    local = pltpu.make_async_copy(own, wf.at[0], lsem)
    local.start()
    sends = []

    def go(cp):
        cp.start()
        sends.append(cp)
        return cp

    d = me.d
    ysl = [go(rcopy(own.at[p, d], wf.at[2, p, d], ysend.at[p], yrecv.at[p], me.ynb)) for p in (0, 1)]
    c1 = [go(rcopy(own.at[p], wf.at[1, p], csend.at[p], crecv.at[p], me.sib)) for p in (0, 1, 2)]
    yd = go(rcopy(own.at[2], wf.at[2, 2], ysend.at[2], yrecv.at[2], me.ynb))
    c3 = []
    for p in (0, 1):
        ysl[p].wait_recv()
        src = wf.at[2, p, d]
        for k in (1, 2, 3):
            go(rcopy(src, src, zsend.at[p, k - 1], brecv.at[p, 3 - k], me.znb(k)))
        go(rcopy(src, src, xsend.at[p, 0], brecv.at[p, 3], me.xnb))
    for p in (0, 1):
        for k in (1, 2, 3):
            s = me.zof(k) * 2 + me.x
            blk = wf.at[2, p, s]
            rcopy(blk, blk, zsend.at[p, k - 1], brecv.at[p, k - 1], me.znb(k)).wait_recv()
            go(rcopy(blk, blk, xsend.at[p, k], brecv.at[p, 3 + k], me.xnb))
        for k in (0, 1, 2, 3):
            s = me.zof(k) * 2 + 1 - me.x
            blk = wf.at[2, p, s]
            rcopy(blk, blk, xsend.at[p, k], brecv.at[p, 3 + k], me.xnb).wait_recv()
        c3.append(go(rcopy(wf.at[2, p], wf.at[3, p], csend.at[3 + p], crecv.at[3 + p], me.sib)))
    yd.wait_recv()
    c3.append(go(rcopy(wf.at[2, 2], wf.at[3, 2], csend.at[5], crecv.at[5], me.sib)))
    for cp in c1 + c3:
        cp.wait_recv()
    for cp in sends:
        cp.wait_send()
    local.wait()


def gather(own):
    n = own.shape
    dma = pltpu.SemaphoreType.DMA
    return pl.pallas_call(
        gather_kernel,
        out_shape=jax.ShapeDtypeStruct((4,) + n, F32),
        in_specs=[ANY],
        out_specs=ANY,
        scratch_shapes=[
            dma, dma((6,)), dma((6,)), dma((3,)), dma((3,)), dma((2, 3)), dma((2, 4)), dma((2, 7)),
        ],
        compiler_params=pltpu.CompilerParams(collective_id=0, has_side_effects=True),
        name="gather",
    )(own)


def ln_stats(v):
    mean = jnp.mean(v, axis=-1, keepdims=True)
    cen = v - mean
    var = jnp.mean(cen * cen, axis=-1, keepdims=True)
    rstd = lax.rsqrt(var + EPSILON)
    return cen * rstd, rstd


def lanes(shape):
    return lax.broadcasted_iota(jnp.int32, shape, len(shape) - 1)


HEADS = ((0, 1, 2, False), (0, 1, 2, True), (3, 4, 3, False))


def attn_fwd_kernel(split, tok, g1, s1, g2, s2, wf, n1, qkv, prob, mx, mid, n2, wst, wbf, s_a, s_b, sem):
    ex, rows, rpad = tok.shape[0], tok.shape[1], n1.shape[1]

    def fetch(j):
        return pltpu.make_async_copy(wf.at[j, 0], wst.at[j % 2], sem.at[j % 2])

    fetch(0).start()
    n1[...] = jnp.zeros_like(n1)

    @pl.loop(0, ex)
    def _(e):
        xhat, _ = ln_stats(tok[e].astype(F32))
        n1[e, :rows, :] = (xhat * g1[...] + s1[...]).astype(BF16)

    low_half = lanes((rpad, 128)) < HD
    qi = lax.broadcasted_iota(jnp.int32, (rpad, rpad), 0)
    kj = lax.broadcasted_iota(jnp.int32, (rpad, rpad), 1)
    for j in range(4):
        if j < 3:
            fetch(j + 1).start()
        fetch(j).wait()
        wbf[...] = wst[j % 2].astype(BF16)
        n1f = n1[...].reshape(ex * rpad, -1)
        qkv[j] = mm(n1f, wbf[:, :640]).astype(BF16).reshape(ex, rpad, 640)

        @pl.loop(0, ex)
        def _(e):
            allowed = kj <= jnp.maximum(qi, PATCHES - 1 + split[e])
            outs = []
            for h, (gq, gk, gv, high) in enumerate(HEADS):
                q = qkv[j, e, :, gq * 128 : gq * 128 + 128]
                q = jnp.where(low_half != high, q, jnp.zeros_like(q))
                k = qkv[j, e, :, gk * 128 : gk * 128 + 128]
                s = mm_nt(q, k) * (HD ** -0.5)
                s = jnp.where(allowed, s, -1e30)
                top = jnp.max(s, axis=-1, keepdims=True)
                p = jnp.exp(s - top)
                p = (p * (1.0 / jnp.sum(p, axis=-1, keepdims=True))).astype(BF16)
                prob[j, e, h] = p
                outs.append(mm(p, qkv[j, e, :, gv * 128 : gv * 128 + 128]))
            zero = jnp.zeros((rpad, 128), F32)
            mx[j, e, :, :128] = jnp.where(low_half, zero, outs[2]).astype(BF16)
            mx[j, e, :, 128:] = jnp.where(low_half, outs[0], outs[1]).astype(BF16)

        s = mm_nt(mx[j].reshape(ex * rpad, 256), wbf[:, 512:]).reshape(ex, rpad, -1)
        acc = s_a if j < 2 else s_b
        if j % 2 == 0:
            acc[...] = s
        else:
            acc[...] += s
    mid[...] = jnp.zeros_like(mid)

    @pl.loop(0, ex)
    def _(e):
        mid[e, :rows, :] = tok[e].astype(F32) + (s_a[e, :rows, :] + s_b[e, :rows, :])
        xhat, _ = ln_stats(mid[e])
        n2[e] = (xhat * g2[...] + s2[...]).astype(BF16)


def attn_fwd(split, tok, g1, s1, g2, s2, wf):
    ex, rows, width = tok.shape
    rpad = -(-rows // 16) * 16
    sds = jax.ShapeDtypeStruct
    return pl.pallas_call(
        attn_fwd_kernel,
        out_shape=(
            sds((ex, rpad, width), BF16), sds((4, ex, rpad, 640), BF16), sds((4, ex, 3, rpad, rpad), BF16),
            sds((4, ex, rpad, 256), BF16), sds((ex, rpad, width), F32), sds((ex, rpad, width), BF16),
        ),
        in_specs=[SM, VM, VM, VM, VM, VM, ANY],
        out_specs=(VM,) * 6,
        scratch_shapes=[
            pltpu.VMEM((2, width, 768), F32), pltpu.VMEM((width, 768), BF16),
            pltpu.VMEM((ex, rpad, width), F32), pltpu.VMEM((ex, rpad, width), F32),
            pltpu.SemaphoreType.DMA((2,)),
        ],
        compiler_params=pltpu.CompilerParams(vmem_limit_bytes=VLIM),
        name="attn_fwd",
    )(split, tok, g1, s1, g2, s2, wf)


CH = 256


def mlp_kernel(cot, mid, n2, wf, out, gn2, gup, gdn, cotp, cot_t, n2_t, ust, dst, br_a, br_b, gn_b, gst_u, gst_d, sem, gsem):
    ex, rows, rpad = cot.shape[0], cot.shape[1], n2.shape[1]
    t = ex * rpad
    nch = wf.shape[3] // CH
    order = [(j, i) for j in (1, 0, 3, 2) for i in range(nch)]

    def fetch(n):
        j, i = order[n]
        b = n % 2
        return (
            pltpu.make_async_copy(wf.at[j, 1, :, pl.ds(i * CH, CH)], ust.at[b], sem.at[0, b]),
            pltpu.make_async_copy(wf.at[j, 2, pl.ds(i * CH, CH), :], dst.at[b], sem.at[1, b]),
        )

    for cp in fetch(0):
        cp.start()
    cotp[...] = jnp.zeros_like(cotp)

    @pl.loop(0, ex)
    def _(e):
        cotp[e, :rows, :] = cot[e]

    cot_t[...] = cotp[...].reshape(t, -1).T
    n2_t[...] = n2[...].reshape(t, -1).T

    def store(n):
        j, i = order[n]
        b = n % 2
        return (
            pltpu.make_async_copy(gst_u.at[b], gup.at[j, :, pl.ds(i * CH, CH)], gsem.at[0, b]),
            pltpu.make_async_copy(gst_d.at[b], gdn.at[j, :, pl.ds(i * CH, CH)], gsem.at[1, b]),
        )

    for n, (j, i) in enumerate(order):
        if n + 1 < len(order):
            for cp in fetch(n + 1):
                cp.start()
        for cp in fetch(n):
            cp.wait()
        u = ust[n % 2].astype(BF16)
        dn = dst[n % 2].astype(BF16)
        pre = mm(n2[...].reshape(t, -1), u)
        ga = mm_nt(cotp[...].reshape(t, -1), dn)
        phi = 0.5 * (1.0 + lax.erf(pre * (0.5 ** 0.5)))
        act = (pre * phi).astype(BF16)
        gpre = (ga * (phi + pre * jnp.exp(-0.5 * pre * pre) * 0.3989422804014327)).astype(BF16)
        br = br_a if j < 2 else br_b
        gn = gn2 if j < 2 else gn_b
        b2 = mm(act, dn).reshape(ex, rpad, -1)
        g2 = mm_nt(gpre, u).reshape(ex, rpad, -1)
        if n % (2 * nch) == 0:
            br[...] = b2
            gn[...] = g2
        else:
            br[...] += b2
            gn[...] += g2
        if j < 2:
            if n >= 2:
                for cp in store(n - 2):
                    cp.wait()
            gst_d[n % 2] = mm(cot_t[...], act)
            gst_u[n % 2] = mm(n2_t[...], gpre)
            for cp in store(n):
                cp.start()
    out[...] = mid[...] + (br_a[...] + br_b[...])
    gn2[...] += gn_b[...]
    for n in (2 * nch - 2, 2 * nch - 1):
        for cp in store(n):
            cp.wait()


def mlp(cot, mid, n2, wf):
    ex, rows, width = cot.shape
    rpad = n2.shape[1]
    t = ex * rpad
    sds = jax.ShapeDtypeStruct
    act = (ex, rpad, width)
    return pl.pallas_call(
        mlp_kernel,
        out_shape=(sds(act, F32), sds(act, F32), sds((2, width, 768), F32), sds((2, width, 768), F32)),
        in_specs=[VM, VM, VM, ANY],
        out_specs=(VM, VM, ANY, ANY),
        scratch_shapes=[
            pltpu.VMEM(act, BF16), pltpu.VMEM((width, t), BF16), pltpu.VMEM((width, t), BF16),
            pltpu.VMEM((2, width, CH), F32), pltpu.VMEM((2, CH, width), F32),
            pltpu.VMEM(act, F32), pltpu.VMEM(act, F32), pltpu.VMEM(act, F32),
            pltpu.VMEM((2, width, CH), F32), pltpu.VMEM((2, width, CH), F32),
            pltpu.SemaphoreType.DMA((2, 2)), pltpu.SemaphoreType.DMA((2, 2)),
        ],
        compiler_params=pltpu.CompilerParams(vmem_limit_bytes=VLIM),
        name="mlp",
    )(cot, mid, n2, wf)


def ln_back(v, gy, gain):
    xhat, rstd = ln_stats(v)
    gx = gy * gain
    m1 = jnp.mean(gx, axis=-1, keepdims=True)
    m2 = jnp.mean(gx * xhat, axis=-1, keepdims=True)
    return rstd * (gx - m1 - xhat * m2), jnp.sum(gy * xhat, axis=0, keepdims=True), jnp.sum(gy, axis=0, keepdims=True)


def attn_bwd_kernel(tok, cot, mid, gn2, n1, qkv, prob, mx, g1, g2, wf, gtok, ga, gv, wst, wbf, gm, gml, gml_t, n1_t, gp, gmix, gn_a, gn_b, sem):
    ex, rows, rpad = tok.shape[0], tok.shape[1], n1.shape[1]
    t = ex * rpad

    def fetch(n):
        return pltpu.make_async_copy(wf.at[(1, 0, 3, 2)[n], 0], wst.at[n % 2], sem.at[n % 2])

    fetch(0).start()
    gv[...] = jnp.zeros_like(gv)
    gm[...] = jnp.zeros_like(gm)

    @pl.loop(0, ex)
    def _(e):
        back, dg, ds = ln_back(mid[e], gn2[e], g2[...])
        gv[2:3, :] += dg
        gv[3:4, :] += ds
        gm[e, :rows, :] = cot[e].astype(F32) + back[:rows]
        gml[e] = gm[e].astype(BF16)

    gml_t[...] = gml[...].reshape(t, -1).T
    n1_t[...] = n1[...].reshape(t, -1).T
    low_half = lanes((rpad, 128)) < HD
    scale = HD ** -0.5
    for n, j in enumerate((1, 0, 3, 2)):
        if n < 3:
            fetch(n + 1).start()
        fetch(n).wait()
        wbf[...] = wst[n % 2].astype(BF16)
        gmix[...] = mm(gml[...].reshape(t, -1), wbf[:, 512:]).astype(BF16).reshape(ex, rpad, 256)

        @pl.loop(0, ex)
        def _(e):
            dq, dk, dv = [], [], []
            for h, (gq, gk, gv_, high) in enumerate(HEADS):
                gx = gmix[e, :, :128] if h == 2 else gmix[e, :, 128:]
                gx = jnp.where(low_half != (high or h == 2), gx, jnp.zeros_like(gx))
                p = prob[j, e, h]
                dp = mm_nt(gx, qkv[j, e, :, gv_ * 128 : gv_ * 128 + 128])
                pf = p.astype(F32)
                pd = pf * dp
                ds = (pd - pf * jnp.sum(pd, axis=-1, keepdims=True)).astype(BF16)
                dq.append(mm(ds, qkv[j, e, :, gk * 128 : gk * 128 + 128]) * scale)
                dk.append(mm_tn(ds, qkv[j, e, :, gq * 128 : gq * 128 + 128]) * scale)
                dv.append(mm_tn(p, gx))
            zero = jnp.zeros((rpad, 128), F32)
            gp[e, :, 0:128] = jnp.where(low_half, dq[0], dq[1]).astype(BF16)
            gp[e, :, 128:256] = jnp.where(low_half, dk[0], dk[1]).astype(BF16)
            gp[e, :, 256:384] = jnp.where(low_half, dv[0], dv[1]).astype(BF16)
            gp[e, :, 384:512] = jnp.where(low_half, dq[2], dv[2]).astype(BF16)
            gp[e, :, 512:640] = jnp.where(low_half, dk[2], zero).astype(BF16)

        gpf = gp[...].reshape(t, 640)
        gn = gn_a if j < 2 else gn_b
        g = mm_nt(gpf, wbf[:, :640]).reshape(ex, rpad, -1)
        if n % 2 == 0:
            gn[...] = g
        else:
            gn[...] += g
        if j < 2:
            ga[j, :, :512] = mm(n1_t[...], gpf[:, :512])
            og = mm(gml_t[...], mx[j].reshape(t, 256))
            ga[j, :, 512:640] = og[:, :128] + mm(n1_t[...], gpf[:, 512:640])
            ga[j, :, 640:] = og[:, 128:]

    @pl.loop(0, ex)
    def _(e):
        gy = gn_a[e, :rows, :] + gn_b[e, :rows, :]
        back, dg, ds = ln_back(tok[e].astype(F32), gy, g1[...])
        gv[0:1, :] += dg
        gv[1:2, :] += ds
        gtok[e] = gm[e, :rows, :] + back


def attn_bwd(tok, cot, mid, gn2, n1, qkv, prob, mx, g1, g2, wf):
    ex, rows, width = tok.shape
    rpad = n1.shape[1]
    t = ex * rpad
    act = (ex, rpad, width)
    sds = jax.ShapeDtypeStruct
    return pl.pallas_call(
        attn_bwd_kernel,
        out_shape=(sds((ex, rows, width), F32), sds((2, width, 768), F32), sds((8, width), F32)),
        in_specs=[VM] * 10 + [ANY],
        out_specs=(VM, VM, VM),
        scratch_shapes=[
            pltpu.VMEM((2, width, 768), F32), pltpu.VMEM((width, 768), BF16),
            pltpu.VMEM(act, F32), pltpu.VMEM(act, BF16), pltpu.VMEM((width, t), BF16), pltpu.VMEM((width, t), BF16),
            pltpu.VMEM((ex, rpad, 640), BF16), pltpu.VMEM((ex, rpad, 256), BF16),
            pltpu.VMEM(act, F32), pltpu.VMEM(act, F32),
            pltpu.SemaphoreType.DMA((2,)),
        ],
        compiler_params=pltpu.CompilerParams(vmem_limit_bytes=VLIM),
        name="attn_bwd",
    )(tok, cot, mid, gn2, n1, qkv, prob, mx, g1, g2, wf)


def reduce_kernel(ga, gu, gd, vec, out, gtok, res, vecs, outs, gtoks, po, cr, xr, zr, vown, vcr, vr,
                  lsem, csend, crecv, xsend, xrecv, zsend, zrecv, vsend, vrecv):
    me = Place()
    greet(me, False, True)
    sends = []

    def go(cp):
        cp.start()
        sends.append(cp)
        return cp

    parts = (gd, gu, ga)
    cc, ll = [], []
    for p, g in enumerate(parts):
        cc.append(go(rcopy(g.at[1], cr.at[p], csend.at[p], crecv.at[p], me.sib)))
        lc = pltpu.make_async_copy(g.at[0], po.at[p], lsem.at[p])
        lc.start()
        ll.append(lc)
    oc = go(rcopy(out, outs, csend.at[3], crecv.at[3], me.sib))
    gc = go(rcopy(gtok, gtoks, csend.at[4], crecv.at[4], me.sib))
    vc = go(rcopy(vec, vcr, csend.at[5], crecv.at[5], me.sib))
    d = me.d
    xs = []
    for p in range(3):
        cc[p].wait_recv()
        ll[p].wait()
        xp = []
        for k in (0, 1, 2, 3):
            s = me.zof(k) * 2 + 1 - me.x
            po[p, s] += cr[p, s]
            xp.append(go(rcopy(po.at[p, s], xr.at[p, me.zof(k)], xsend.at[p, k], xrecv.at[p, k], me.xnb)))
        xs.append(xp)
    for p in range(3):
        for k in (0, 1, 2, 3):
            s = me.zof(k) * 2 + me.x
            po[p, s] += cr[p, s]
    vc.wait_recv()
    vown[...] = vec[...] + vcr[...]
    vp = []
    for k in range(1, 8):
        to = lax.rem(d + k, 8)
        vp.append(go(rcopy(vown, vr.at[7 - k], vsend.at[k - 1], vrecv.at[7 - k], (to, me.t))))
    zs = []
    for p in range(3):
        for k in (1, 2, 3, 0):
            s = me.zof(k) * 2 + me.x
            xs[p][k].wait_recv()
            po[p, s] += xr[p, me.zof(k)]
            if k:
                zs.append(go(rcopy(po.at[p, s], zr.at[p, 3 - k], zsend.at[p, k - 1], zrecv.at[p, 3 - k], me.znb(k))))
    for p in range(3):
        for k in (1, 2, 3):
            rcopy(zr.at[p, k - 1], zr.at[p, k - 1], zsend.at[p, k - 1], zrecv.at[p, k - 1], me.znb(k)).wait_recv()
        res[p] = po[p, d] + zr[p, 0] + zr[p, 1] + zr[p, 2]
    for k in range(1, 8):
        rcopy(vown, vr.at[k - 1], vsend.at[k - 1], vrecv.at[k - 1], me.sib).wait_recv()
    acc = None
    for i in range(8):
        k = lax.rem(i - d + 8, 8)
        slot = jnp.maximum(k - 1, 0)
        term = jnp.where(k == 0, vown[...], vr[slot])
        acc = term if acc is None else acc + term
    vecs[...] = acc
    oc.wait_recv()
    gc.wait_recv()
    for cp in sends:
        cp.wait_send()


def reduce(ga, gu, gd, vec, out, gtok):
    sds = jax.ShapeDtypeStruct
    dma = pltpu.SemaphoreType.DMA
    blk = ga.shape[1:]
    return pl.pallas_call(
        reduce_kernel,
        out_shape=(sds((3,) + blk[1:], F32), sds(vec.shape, F32), sds(out.shape, F32), sds(gtok.shape, F32)),
        in_specs=[ANY] * 3 + [VM] + [ANY] * 2,
        out_specs=(VM, VM, ANY, ANY),
        scratch_shapes=[
            pltpu.VMEM((3,) + blk, F32), pltpu.VMEM((3,) + blk, F32), pltpu.VMEM((3, 4) + blk[1:], F32),
            pltpu.VMEM((3, 3) + blk[1:], F32), pltpu.VMEM(vec.shape, F32), pltpu.VMEM(vec.shape, F32),
            pltpu.VMEM((7,) + vec.shape, F32),
            dma((3,)), dma((6,)), dma((6,)), dma((3, 4)), dma((3, 4)), dma((3, 3)), dma((3, 3)), dma((7,)), dma((7,)),
        ],
        compiler_params=pltpu.CompilerParams(collective_id=1, has_side_effects=True, vmem_limit_bytes=VLIM),
        name="reduce",
    )(ga, gu, gd, vec, out, gtok)


def fast_device(tokens, cotangent, split_point, w_qkv, w_out, w_up, w_down, gain_one, shift_one, gain_two, shift_two):
    batch, length, width = tokens.shape
    c = lax.rem(lax.axis_index("tensor"), 2)
    d = lax.axis_index("dp")
    ex = batch // 2
    tok = lax.dynamic_slice_in_dim(tokens, c * ex, ex, 0)
    cot = lax.dynamic_slice_in_dim(cotangent, c * ex, ex, 0)
    split = lax.dynamic_slice_in_dim(split_point, c * ex, ex, 0)
    q, k, v, o = w_qkv[0], w_qkv[1], w_qkv[2], w_out.T
    attn = jnp.concatenate(
        [q[:, :128], k[:, :128], v[:, :128], q[:, 128:], v[:, 128:], k[:, 128:], o[:, 128:], o[:, :128]], axis=1
    )
    own = jnp.stack([attn, w_up, w_down]).astype(F32).reshape(3, 8, width // 8, 768)
    row = lambda v_: v_.reshape(1, -1)
    g1, s1, g2, s2 = row(gain_one), row(shift_one), row(gain_two), row(shift_two)
    wf = gather(own).reshape(4, 3, width, 768)
    n1, qkv, prob, mx, mid, n2 = attn_fwd(split, tok, g1, s1, g2, s2, wf)
    out, gn2, gup, gdn = mlp(cot, mid, n2, wf)
    gtok, ga, vec = attn_bwd(tok, cot, mid, gn2, n1, qkv, prob, mx, g1, g2, wf)
    blk = (2, 8, width // 8, 768)
    res, vecs, outs, gtoks = reduce(ga.reshape(blk), gup.reshape(blk), gdn.reshape(blk), vec, out, gtok)

    def both(mine, other):
        first = jnp.where(c == 0, mine, other)
        second = jnp.where(c == 0, other, mine)
        return jnp.concatenate([first, second], axis=0).astype(BF16)

    output = both(out[:, :length], outs[:, :length])
    grad_tokens = both(gtok, gtoks)
    rd, ru, ra = res[0], res[1], res[2]
    gq = jnp.concatenate([ra[:, 0:128], ra[:, 384:448]], axis=1)
    gk = jnp.concatenate([ra[:, 128:256], ra[:, 512:576]], axis=1)
    gv = jnp.concatenate([ra[:, 256:384], ra[:, 448:512]], axis=1)
    go = jnp.concatenate([ra[:, 640:768], ra[:, 576:640]], axis=1).T
    mine = lax.dynamic_slice_in_dim(vecs, d * (width // 8), width // 8, 1)
    return (
        output, grad_tokens, jnp.stack([gq, gk, gv]), go, ru, rd.T, mine[0], mine[1], mine[2], mine[3],
    )


def layer_norm(values, gain_vec, shift_vec):
    row_mean = jnp.mean(values, axis=-1, keepdims=True)
    centered = values - row_mean
    variance = jnp.mean(centered * centered, axis=-1, keepdims=True)
    return centered * lax.rsqrt(variance + EPSILON) * gain_vec + shift_vec


def attention_forward(inputs, allowed, w_qkv, w_out, gain_one, shift_one):
    batch, length, width = inputs.shape
    local = w_qkv.shape[2]
    head_count = local // HD
    normed = layer_norm(inputs, gain_one, shift_one).astype(jnp.bfloat16)
    packed = jnp.einsum("btd,cde->cbte", normed, w_qkv, preferred_element_type=jnp.float32).astype(
        jnp.bfloat16
    )
    queries = packed[0].reshape(batch, length, head_count, HD)
    keys = packed[1].reshape(batch, length, head_count, HD)
    values = packed[2].reshape(batch, length, head_count, HD)
    scores = jnp.einsum(
        "bqhe,bkhe->bhqk", queries, keys, preferred_element_type=jnp.float32
    ) * HD ** (-0.5)
    scores = jnp.where(allowed[:, None], scores, -1e30)
    log_total = jax.nn.logsumexp(scores, axis=-1, keepdims=True)
    attn_probs = jnp.exp(scores - log_total)
    probs_low = attn_probs.astype(jnp.bfloat16)
    mixed = jnp.einsum("bhqk,bkhe->bqhe", probs_low, values, preferred_element_type=jnp.float32)
    mixed = mixed.reshape(batch, length, local).astype(jnp.bfloat16)
    partial_out = jnp.einsum("btk,kd->btd", mixed, w_out, preferred_element_type=jnp.float32)
    return (normed, queries, keys, values, attn_probs, probs_low, mixed, partial_out)


def mlp_forward(middle, w_up, gain_two, shift_two):
    normed_two = layer_norm(middle, gain_two, shift_two).astype(jnp.bfloat16)
    pre_act = jnp.einsum("btd,df->btf", normed_two, w_up, preferred_element_type=jnp.float32)
    activated = jax.nn.gelu(pre_act, approximate=False).astype(jnp.bfloat16)
    return (normed_two, pre_act, activated)


def per_device(
    tokens,
    cotangent,
    split_point,
    w_qkv,
    w_out,
    w_up,
    w_down,
    gain_one,
    shift_one,
    gain_two,
    shift_two,
):
    inputs = tokens.astype(jnp.float32)
    batch, length, width = tokens.shape
    local = w_qkv.shape[2]
    head_count = local // HD
    score_scale = HD ** (-0.5)
    places = jnp.arange(length, dtype=jnp.int32)
    limit = jnp.maximum(places[None, :, None], PATCHES + split_point[:, None, None] - 1)
    allowed = places[None, None, :] <= limit
    normed, queries, keys, values, attn_probs, probs_low, mixed, partial_out = attention_forward(
        inputs, allowed, w_qkv, w_out, gain_one, shift_one
    )
    middle = inputs + lax.psum(partial_out, "tensor")
    normed_two, pre_act, activated = mlp_forward(middle, w_up, gain_two, shift_two)
    branch = jnp.einsum("btf,fd->btd", activated, w_down, preferred_element_type=jnp.float32)
    output = (middle + lax.psum(branch, "tensor")).astype(jnp.bfloat16)
    normed, queries, keys, values, attn_probs, probs_low, mixed, partial_out = attention_forward(
        inputs, allowed, w_qkv, w_out, gain_one, shift_one
    )
    middle = inputs + lax.psum(partial_out, "tensor")
    normed_two, pre_act, activated = mlp_forward(middle, w_up, gain_two, shift_two)
    grad_output = cotangent.astype(jnp.float32)
    grad_act = jnp.einsum("btd,fd->btf", cotangent, w_down, preferred_element_type=jnp.float32)
    gelu_pull = jax.vjp(partial(jax.nn.gelu, approximate=False), pre_act)[1]
    grad_pre = gelu_pull(grad_act)[0].astype(jnp.bfloat16)
    grad_down_local = jnp.einsum(
        "btf,btd->fd", activated, cotangent, preferred_element_type=jnp.float32
    )
    grad_up_local = jnp.einsum(
        "btd,btf->df", normed_two, grad_pre, preferred_element_type=jnp.float32
    )
    grad_normed_two = lax.psum(
        jnp.einsum("btf,df->btd", grad_pre, w_up, preferred_element_type=jnp.float32), "tensor"
    )
    norm_two_pull = jax.vjp(layer_norm, middle, gain_two, shift_two)[1]
    grad_mid_norm, grad_gain_two, grad_shift_two = norm_two_pull(grad_normed_two)
    grad_middle = grad_output + grad_mid_norm
    grad_mid_low = grad_middle.astype(jnp.bfloat16)
    grad_out_local = jnp.einsum(
        "btk,btd->kd", mixed, grad_mid_low, preferred_element_type=jnp.float32
    )
    grad_mix = jnp.einsum("btd,kd->btk", grad_mid_low, w_out, preferred_element_type=jnp.float32)
    grad_mix = grad_mix.astype(jnp.bfloat16).reshape(batch, length, head_count, HD)
    grad_probs = jnp.einsum("bqhe,bkhe->bhqk", grad_mix, values, preferred_element_type=jnp.float32)
    row_terms = jnp.sum(attn_probs * grad_probs, axis=-1, keepdims=True)
    grad_scores = (attn_probs * (grad_probs - row_terms)).astype(jnp.bfloat16)
    grad_query = (
        jnp.einsum("bhqk,bkhe->bqhe", grad_scores, keys, preferred_element_type=jnp.float32)
        * score_scale
    )
    grad_key = (
        jnp.einsum("bhqk,bqhe->bkhe", grad_scores, queries, preferred_element_type=jnp.float32)
        * score_scale
    )
    grad_value = jnp.einsum(
        "bhqk,bqhe->bkhe", probs_low, grad_mix, preferred_element_type=jnp.float32
    )
    grad_packed = (
        jnp.stack([grad_query, grad_key, grad_value])
        .reshape(3, batch, length, local)
        .astype(jnp.bfloat16)
    )
    grad_qkv_local = jnp.einsum(
        "btd,cbte->cde", normed, grad_packed, preferred_element_type=jnp.float32
    )
    grad_normed = lax.psum(
        jnp.einsum("cbte,cde->btd", grad_packed, w_qkv, preferred_element_type=jnp.float32),
        "tensor",
    )
    norm_one_pull = jax.vjp(layer_norm, inputs, gain_one, shift_one)[1]
    grad_in_norm, grad_gain_one, grad_shift_one = norm_one_pull(grad_normed)
    grad_tokens = (grad_middle + grad_in_norm).astype(jnp.bfloat16)
    (
        qkv_part,
        out_part,
        up_part,
        down_part,
        gain_one_part,
        shift_one_part,
        gain_two_part,
        shift_two_part,
    ) = (
        lax.psum_scatter(grad_qkv_local, "dp", scatter_dimension=1, tiled=True),
        lax.psum_scatter(grad_out_local, "dp", scatter_dimension=1, tiled=True),
        lax.psum_scatter(grad_up_local, "dp", scatter_dimension=0, tiled=True),
        lax.psum_scatter(grad_down_local, "dp", scatter_dimension=1, tiled=True),
        lax.psum_scatter(grad_gain_one, "dp", scatter_dimension=0, tiled=True),
        lax.psum_scatter(grad_shift_one, "dp", scatter_dimension=0, tiled=True),
        lax.psum_scatter(grad_gain_two, "dp", scatter_dimension=0, tiled=True),
        lax.psum_scatter(grad_shift_two, "dp", scatter_dimension=0, tiled=True),
    )
    return (
        output,
        grad_tokens,
        qkv_part,
        out_part,
        up_part,
        down_part,
        gain_one_part,
        shift_one_part,
        gain_two_part,
        shift_two_part,
    )


def solution(mesh):
    in_specs = (
        P("dp", None, None),
        P("dp", None, None),
        P("dp"),
        P(None, None, "tensor"),
        P("tensor", None),
        P(None, "tensor"),
        P("tensor", None),
        P(),
        P(),
        P(),
        P(),
    )
    out_specs = (
        P("dp", None, None),
        P("dp", None, None),
        P(None, "dp", "tensor"),
        P("tensor", "dp"),
        P("dp", "tensor"),
        P("tensor", "dp"),
        P("dp"),
        P("dp"),
        P("dp"),
        P("dp"),
    )
    fast = mesh.shape["dp"] == 8 and mesh.shape["tensor"] == 4
    return jax.shard_map(
        fast_device if fast else per_device, mesh=mesh, in_specs=in_specs, out_specs=out_specs, check_vma=False
    )
```

```python
from functools import partial

import jax
import jax.numpy as jnp
from jax import lax
from jax.experimental import pallas as pl
from jax.experimental.pallas import tpu as pltpu
from jax.sharding import PartitionSpec as P

HD = 64
PATCHES = 196
EPSILON = 1e-05
MESH = pl.DeviceIdType.MESH
F32 = jnp.float32
BF16 = jnp.bfloat16
CH = 256


def mm(a, b):
    return jnp.dot(a, b, preferred_element_type=F32)


def mm_nt(a, b):
    return lax.dot_general(a, b, (((1,), (1,)), ((), ())), preferred_element_type=F32)


def mm_tn(a, b):
    return lax.dot_general(a, b, (((0,), (0,)), ((), ())), preferred_element_type=F32)


def ln_stats(v):
    mean = jnp.mean(v, axis=-1, keepdims=True)
    cen = v - mean
    var = jnp.mean(cen * cen, axis=-1, keepdims=True)
    rstd = lax.rsqrt(var + EPSILON)
    return cen * rstd, rstd


def ln_back(v, gy, gain):
    xhat, rstd = ln_stats(v)
    gx = gy * gain
    m1 = jnp.mean(gx, axis=-1, keepdims=True)
    m2 = jnp.mean(gx * xhat, axis=-1, keepdims=True)
    return rstd * (gx - m1 - xhat * m2), jnp.sum(gy * xhat, axis=0, keepdims=True), jnp.sum(gy, axis=0, keepdims=True)


def rcopy(src, dst, ssem, rsem, dev):
    return pltpu.make_async_remote_copy(
        src_ref=src, dst_ref=dst, send_sem=ssem, recv_sem=rsem, device_id=dev, device_id_type=MESH
    )


HEADS = ((0, 1, 2, False), (0, 1, 2, True), (3, 4, 3, False))
SL = 512


def layer_kernel(
    split, tokens, cots, g1, s1, g2, s2, own,
    wf, res, vecs, out, outs, gtok, gtoks,
    tok, cotr, cotp, n1, qkv, prob, mx, mid, br, gn, n2, ust, dst, wbf, ta, tb, gp, gmix,
    po, ps, cr, xr, zr, gv, vcr, vr,
    isem, wsem, csend, crecv, ysend, yrecv, dsend, drecv, zsend, zrecv, xsend, xrecv,
    rcs, rcr, rxs, rxr, rzs, rzr, osend, orecv, vsend, vrecv,
):
    ex, rows, width = tok.shape
    rpad = n1.shape[1]
    t = ex * rpad
    d, tt = lax.axis_index("dp"), lax.axis_index("tensor")
    z, x = d // 2, lax.rem(d, 2)
    y, c = tt // 2, lax.rem(tt, 2)
    sib = (d, y * 2 + 1 - c)
    ynb = (d, (1 - y) * 2 + c)
    xnb = (z * 2 + 1 - x, tt)

    def band(i):
        return pl.ds(pl.multiple_of(i * (width // 8), width // 8), width // 8)

    def zof(k):
        return lax.rem(z + k, 4)

    def znb(k):
        return (zof(k) * 2 + x, tt)

    peers = [sib, ynb] + [(lax.rem(d + k, 8), tt) for k in range(1, 8)]
    barrier = pltpu.get_barrier_semaphore()
    for p in peers:
        pl.semaphore_signal(barrier, 1, device_id=p, device_id_type=MESH)
    pl.semaphore_wait(barrier, len(peers))

    def y_slice(p):
        return rcopy(own.at[p, band(d), :SL], wf.at[1, p, band(d), :SL], ysend.at[p], yrecv.at[p], ynb)

    def y_direct(p):
        return rcopy(own.at[p, :, SL:], wf.at[1, p, :, SL:], dsend.at[p], drecv.at[p], ynb)

    def c_first(p):
        return rcopy(own.at[p], wf.at[0, p], csend.at[p], crecv.at[p], sib)

    def c_second(p):
        return rcopy(wf.at[1, p], wf.at[2, p], csend.at[3 + p], crecv.at[3 + p], sib)

    def z_copy(p, k, slot, sem):
        blk = wf.at[1, p, band(slot), :SL]
        return rcopy(blk, blk, zsend.at[p, k - 1], zrecv.at[p, sem], znb(k))

    def x_copy(p, k, slot):
        blk = wf.at[1, p, band(slot), :SL]
        return rcopy(blk, blk, xsend.at[p, k], xrecv.at[p, k], xnb)

    def g1_step(p):
        y_slice(p).wait_recv()
        for k in (1, 2, 3):
            z_copy(p, k, d, 3 - k).start()
        x_copy(p, 0, d).start()

    def g2_step(p):
        for k in (1, 2, 3):
            s = zof(k) * 2 + x
            z_copy(p, k, s, k - 1).wait_recv()
            x_copy(p, k, s).start()

    def g3_step(p):
        for k in (0, 1, 2, 3):
            x_copy(p, k, zof(k) * 2 + 1 - x).wait_recv()
        y_direct(p).wait_recv()
        c_second(p).start()

    def fetch(j, p, i, b):
        def src(ref):
            if p == 2:
                return ref.at[pl.ds(pl.multiple_of(i * CH, CH), CH), :]
            return ref.at[:, pl.ds(pl.multiple_of(i * CH, CH), CH)]

        dstr = (dst if p == 2 else ust).at[b]
        sem = wsem.at[1 if p == 2 else 0, b]

        @pl.when(j == 0)
        def _():
            pltpu.make_async_copy(src(own.at[p]), dstr, sem).start()

        @pl.when(j > 0)
        def _():
            pltpu.make_async_copy(src(wf.at[jnp.maximum(j - 1, 0), p]), dstr, sem).start()

    def fetched(p, b):
        dstr = (dst if p == 2 else ust).at[b]
        pltpu.make_async_copy(dstr, dstr, wsem.at[1 if p == 2 else 0, b]).wait()

    def load_attn(j):
        fetch(j, 0, 0, 0)
        for i in range(3):
            if i < 2:
                fetch(j, 0, i + 1, (i + 1) % 2)
            fetched(0, i % 2)
            wbf[:, i * CH : (i + 1) * CH] = ust[i % 2].astype(BF16)

    def c_grad(u, slot):
        return rcopy(ps.at[slot], cr.at[u], rcs.at[u], rcr.at[u], sib)

    def x_grad(u, pu, side):
        return rcopy(po.at[pu, :, side], xr.at[u], rxs.at[u], rxr.at[u], xnb)

    def z_grad(u, pu, k, slot):
        return rcopy(po.at[pu, zof(k), x], zr.at[u, slot], rzs.at[u, k - 1], rzr.at[u, slot], znb(k))

    def r1_step(u, pu):
        c_grad(u, 0).wait_recv()
        po[pu, :, 1 - x] += cr[u, :, 1 - x]
        x_grad(u, pu, 1 - x).start()
        po[pu, :, x] += cr[u, :, x]

    def r2_step(u, pu):
        x_grad(u, pu, x).wait_recv()
        po[pu, :, x] += xr[u]
        for k in (1, 2, 3):
            z_grad(u, pu, k, 3 - k).start()

    def r3_step(u, pu):
        for k in (1, 2, 3):
            z_grad(u, pu, k, k - 1).wait_recv()
        res[u] = po[pu, z, x] + zr[u, 0] + zr[u, 1] + zr[u, 2]

    for p in range(3):
        y_slice(p).start()
    c_first(0).start()
    y_direct(0).start()
    tin = pltpu.make_async_copy(tokens.at[pl.ds(c * ex, ex)], tok, isem.at[0])
    tin.start()
    tin.wait()
    n1[...] = jnp.zeros_like(n1)
    mid[...] = jnp.zeros_like(mid)
    cotp[...] = jnp.zeros_like(cotp)
    gv[...] = jnp.zeros_like(gv)

    @pl.loop(0, ex)
    def _(e):
        v = tok[e].astype(F32)
        xhat, _ = ln_stats(v)
        n1[e, :rows, :] = (xhat * g1[...][None] + s1[...][None]).astype(BF16)
        mid[e, :rows, :] = v

    c_first(1).start()
    c_first(2).start()

    low_half = lax.broadcasted_iota(jnp.int32, (rpad, 128), 1) < HD
    qi = lax.broadcasted_iota(jnp.int32, (rpad, rpad), 0)
    kj = lax.broadcasted_iota(jnp.int32, (rpad, rpad), 1)

    @pl.loop(0, 4)
    def _(j):
        @pl.when(j == 1)
        def _():
            g1_step(0)
            c_first(0).wait_recv()

        @pl.when(j == 2)
        def _():
            ccopy = pltpu.make_async_copy(cots.at[pl.ds(c * ex, ex)], cotr, isem.at[1])
            ccopy.start()
            ccopy.wait()

            @pl.loop(0, ex)
            def _(e):
                cotp[e, :rows, :] = cotr[e]

            ta[...] = cotp[...].reshape(t, width).T
            g2_step(0)
            y_direct(1).start()
            y_direct(2).start()
            g3_step(0)
            g1_step(1)

        @pl.when(j == 3)
        def _():
            g1_step(2)
            c_second(0).wait_recv()

        load_attn(j)
        qkv[j] = mm(n1[...].reshape(t, width), wbf[:, :640]).astype(BF16).reshape(ex, rpad, 640)

        @pl.loop(0, ex)
        def _(e):
            allowed = kj <= jnp.maximum(qi, PATCHES - 1 + split[c * ex + e])
            outs_h = []
            for h, (gq, gk, gvv, high) in enumerate(HEADS):
                q = qkv[j, e, :, gq * 128 : gq * 128 + 128]
                q = jnp.where(low_half != high, q, jnp.zeros_like(q))
                k = qkv[j, e, :, gk * 128 : gk * 128 + 128]
                s = mm_nt(q, k) * (HD ** -0.5)
                s = jnp.where(allowed, s, -1e30)
                top = jnp.max(s, axis=-1, keepdims=True)
                p = jnp.exp(s - top)
                p = (p * (1.0 / jnp.sum(p, axis=-1, keepdims=True))).astype(BF16)
                prob[j, e, h] = p
                outs_h.append(mm(p, qkv[j, e, :, gvv * 128 : gvv * 128 + 128]))
            zero = jnp.zeros((rpad, 128), F32)
            mx[j, e, :, :128] = jnp.where(low_half, zero, outs_h[2]).astype(BF16)
            mx[j, e, :, 128:] = jnp.where(low_half, outs_h[0], outs_h[1]).astype(BF16)

        mid[...] += mm_nt(mx[j].reshape(t, 256), wbf[:, 512:]).reshape(ex, rpad, width)

    g2_step(1)

    @pl.loop(0, ex)
    def _(e):
        keep = lax.broadcasted_iota(jnp.int32, (rpad, 1), 0) < rows
        v = jnp.where(keep, mid[e], 0.0)
        mid[e] = v
        xhat, _ = ln_stats(v)
        n2[e] = (xhat * g2[...][None] + s2[...][None]).astype(BF16)
        br[e] = v
        gn[e] = jnp.zeros((rpad, width), F32)

    tb[...] = n2[...].reshape(t, width).T

    def chunk(b):
        u = ust[b].astype(BF16)
        dn = dst[b].astype(BF16)
        pre = mm(n2[...].reshape(t, width), u)
        ga = mm_nt(cotp[...].reshape(t, width), dn)
        phi = 0.5 * (1.0 + lax.erf(pre * (0.5 ** 0.5)))
        act = (pre * phi).astype(BF16)
        gpre = (ga * (phi + pre * jnp.exp(-0.5 * pre * pre) * 0.3989422804014327)).astype(BF16)
        br[...] += mm(act, dn).reshape(ex, rpad, width)
        gn[...] += mm_nt(gpre, u).reshape(ex, rpad, width)
        return act, gpre

    def fetch2(j, i, b):
        fetch(j, 1, i, b)
        fetch(j, 2, i, b)

    def fetched2(b):
        fetched(1, b)
        fetched(2, b)

    c_first(1).wait_recv()
    c_first(2).wait_recv()
    fetch2(1, 0, 0)
    shape5 = po.shape[1:]

    @pl.loop(0, 6)
    def _(n):
        i, b = n // 2, lax.rem(n, 2)

        @pl.when(n < 5)
        def _():
            fetch2(b, (n + 1) // 2, 1 - b)

        fetched2(b)
        act, gpre = chunk(b)
        gd = mm(ta[...], act).reshape(shape5)
        gu = mm(tb[...], gpre).reshape(shape5)
        slot = 2 * lax.rem(i, 2)

        @pl.when(b == 0)
        def _():
            @pl.when(i == 2)
            def _():
                c_grad(0, 0).wait_send()
                c_grad(1, 1).wait_send()

            ps[slot] = gd
            ps[slot + 1] = gu
            c_grad(2 * i, slot).start()
            c_grad(2 * i + 1, slot + 1).start()

        @pl.when(b == 1)
        def _():
            po[2 * i] = gd
            po[2 * i + 1] = gu
            r1_step(2 * i, 2 * i)
            r1_step(2 * i + 1, 2 * i + 1)

        @pl.when(n == 1)
        def _():
            g2_step(2)

        @pl.when(n == 3)
        def _():
            g3_step(1)

    g3_step(2)
    fetch2(2, 0, 0)

    @pl.loop(0, 6)
    def _(n):
        b = lax.rem(n, 2)

        @pl.when(n == 2)
        def _():
            c_second(1).wait_recv()
            c_second(2).wait_recv()

        @pl.when(n < 5)
        def _():
            fetch2(2 + (n + 1) // 3, lax.rem(n + 1, 3), 1 - b)

        fetched2(b)
        chunk(b)

    o_copy = rcopy(br, outs, osend.at[0], orecv.at[0], sib)
    o_copy.start()
    o_keep = pltpu.make_async_copy(br, out, isem.at[2])
    o_keep.start()
    r2_step(0, 0)
    r2_step(1, 1)

    @pl.loop(0, ex)
    def _(e):
        back, dg, ds = ln_back(mid[e], gn[e], g2[...][None])
        gv[2:3, :] += dg
        gv[3:4, :] += ds
        gm = cotp[e].astype(F32) + back
        mid[e] = gm
        n2[e] = gm.astype(BF16)
        gn[e] = jnp.zeros((rpad, width), F32)

    gml = n2
    ta[...] = gml[...].reshape(t, width).T
    tb[...] = n1[...].reshape(t, width).T
    scale = HD ** -0.5

    @pl.loop(0, 4)
    def _(n):
        j = jnp.where(n < 2, 1 - n, n)
        load_attn(j)
        gmix[...] = mm(gml[...].reshape(t, width), wbf[:, 512:]).astype(BF16).reshape(ex, rpad, 256)

        @pl.loop(0, ex)
        def _(e):
            dq, dk, dv = [], [], []
            for h, (gq, gk, gvv, high) in enumerate(HEADS):
                gx = gmix[e, :, :128] if h == 2 else gmix[e, :, 128:]
                gx = jnp.where(low_half != (high or h == 2), gx, jnp.zeros_like(gx))
                p = prob[j, e, h]
                dp = mm_nt(gx, qkv[j, e, :, gvv * 128 : gvv * 128 + 128])
                pf = p.astype(F32)
                pd = pf * dp
                ds = (pd - pf * jnp.sum(pd, axis=-1, keepdims=True)).astype(BF16)
                dq.append(mm(ds, qkv[j, e, :, gk * 128 : gk * 128 + 128]) * scale)
                dk.append(mm_tn(ds, qkv[j, e, :, gq * 128 : gq * 128 + 128]) * scale)
                dv.append(mm_tn(p, gx))
            zero = jnp.zeros((rpad, 128), F32)
            gp[e, :, 0:128] = jnp.where(low_half, dq[0], dq[1]).astype(BF16)
            gp[e, :, 128:256] = jnp.where(low_half, dk[0], dk[1]).astype(BF16)
            gp[e, :, 256:384] = jnp.where(low_half, dv[0], dv[1]).astype(BF16)
            gp[e, :, 384:512] = jnp.where(low_half, dq[2], dv[2]).astype(BF16)
            gp[e, :, 512:640] = jnp.where(low_half, dk[2], zero).astype(BF16)

        gpf = gp[...].reshape(t, 640)
        gn[...] += mm_nt(gpf, wbf[:, :640]).reshape(ex, rpad, width)

        def grads(write):
            write(0, mm(tb[...], gpf[:, :256]).reshape(shape5))
            write(1, mm(tb[...], gpf[:, 256:512]).reshape(shape5))
            og = mm(ta[...], mx[j].reshape(t, 256))
            k2 = mm(tb[...], gpf[:, 512:640])
            write(2, jnp.concatenate([og[:, :128] + k2, og[:, 128:]], axis=1).reshape(shape5))

        @pl.when(n == 0)
        def _():
            for u in range(2, 6):
                c_grad(u, (0, 1, 2, 3, 0, 1)[u]).wait_send()

            def write(i, g):
                ps[i] = g
                c_grad(6 + i, i).start()

            grads(write)

        @pl.when(n == 1)
        def _():
            r3_step(0, 0)
            r3_step(1, 1)
            r2_step(2, 2)
            r2_step(3, 3)
            for u in range(2):
                x_grad(u, u, 1 - x).wait_send()
                for k in (1, 2, 3):
                    z_grad(u, u, k, 3 - k).wait_send()

            def write(i, g):
                pu = (0, 1, 6)[i]
                po[pu] = g
                r1_step(6 + i, pu)

            grads(write)

        @pl.when(n == 2)
        def _():
            r3_step(2, 2)
            r3_step(3, 3)
            r2_step(4, 4)
            r2_step(5, 5)

    r2_step(6, 0)

    o_copy.wait_send()
    o_keep.wait()

    @pl.loop(0, ex)
    def _(e):
        back, dg, ds = ln_back(tok[e].astype(F32), gn[e, :rows, :], g1[...][None])
        gv[0:1, :] += dg
        gv[1:2, :] += ds
        br[e, :rows, :] = mid[e, :rows, :] + back

    t_copy = rcopy(br, gtoks, osend.at[1], orecv.at[1], sib)
    t_copy.start()
    t_keep = pltpu.make_async_copy(br, gtok, isem.at[2])
    t_keep.start()
    v_copy = rcopy(gv, vcr, osend.at[2], orecv.at[2], sib)
    v_copy.start()
    r2_step(7, 1)
    v_copy.wait()
    gv[...] += vcr[...]
    v_sends = []
    for k in range(1, 8):
        cp = rcopy(gv, vr.at[7 - k], vsend.at[k - 1], vrecv.at[7 - k], (lax.rem(d + k, 8), tt))
        cp.start()
        v_sends.append(cp)
    r2_step(8, 6)
    for u in range(4, 9):
        r3_step(u, (0, 1, 2, 3, 4, 5, 0, 1, 6)[u])
    for k in range(1, 8):
        rcopy(gv, vr.at[k - 1], vsend.at[k - 1], vrecv.at[k - 1], sib).wait_recv()
    acc = None
    for i in range(8):
        k = lax.rem(i - d + 8, 8)
        term = jnp.where(k == 0, gv[...], vr[jnp.maximum(k - 1, 0)])
        acc = term if acc is None else acc + term
    vecs[...] = acc

    c_second(1).wait_send()
    o_copy.wait_recv()
    t_copy.wait()
    t_keep.wait()
    for cp in v_sends:
        cp.wait_send()
    for p in range(3):
        y_slice(p).wait_send()
        y_direct(p).wait_send()
        c_first(p).wait_send()
        for k in (1, 2, 3):
            z_copy(p, k, d, 3 - k).wait_send()
        for k in (0, 1, 2, 3):
            x_copy(p, k, d).wait_send()
    c_second(0).wait_send()
    c_second(2).wait_send()
    for u in range(2, 9):
        pu = (0, 1, 2, 3, 4, 5, 0, 1, 6)[u]
        x_grad(u, pu, 1 - x).wait_send()
        for k in (1, 2, 3):
            z_grad(u, pu, k, 3 - k).wait_send()
    for u in range(6, 9):
        c_grad(u, u - 6).wait_send()


def layer(split, tokens, cots, g1, s1, g2, s2, own):
    batch, rows, width = tokens.shape
    ex = batch // 2
    rpad = -(-rows // 16) * 16
    t = ex * rpad
    band = width // 8
    sds = jax.ShapeDtypeStruct
    dma = pltpu.SemaphoreType.DMA
    vm = pltpu.VMEM
    ANY = pl.BlockSpec(memory_space=pl.ANY)
    VM = pl.BlockSpec(memory_space=pltpu.VMEM)
    SM = pl.BlockSpec(memory_space=pltpu.SMEM)
    act = (ex, rpad, width)
    return pl.pallas_call(
        layer_kernel,
        out_shape=(
            sds((3, 3, width, 768), F32), sds((9, band, CH), F32), sds((8, width), F32),
            sds(act, F32), sds(act, F32), sds(act, F32), sds(act, F32),
        ),
        in_specs=[SM, ANY, ANY, VM, VM, VM, VM, ANY],
        out_specs=(ANY, VM, VM, ANY, ANY, ANY, ANY),
        scratch_shapes=[
            vm((ex, rows, width), BF16), vm((ex, rows, width), BF16), vm(act, BF16), vm(act, BF16),
            vm((4, ex, rpad, 640), BF16), vm((4, ex, 3, rpad, rpad), BF16), vm((4, ex, rpad, 256), BF16),
            vm(act, F32), vm(act, F32), vm(act, F32), vm(act, BF16),
            vm((2, width, CH), F32), vm((2, CH, width), F32), vm((width, 768), BF16),
            vm((width, t), BF16), vm((width, t), BF16), vm((ex, rpad, 640), BF16), vm((ex, rpad, 256), BF16),
            vm((7, 4, 2, band, CH), F32), vm((4, 4, 2, band, CH), F32), vm((9, 4, 2, band, CH), F32),
            vm((9, 4, band, CH), F32), vm((9, 3, band, CH), F32),
            vm((8, width), F32), vm((8, width), F32), vm((7, 8, width), F32),
            dma((3,)), dma((2, 2)), dma((6,)), dma((6,)), dma((3,)), dma((3,)), dma((3,)), dma((3,)),
            dma((3, 3)), dma((3, 3)), dma((3, 4)), dma((3, 4)),
            dma((9,)), dma((9,)), dma((9,)), dma((9,)), dma((9, 3)), dma((9, 3)), dma((3,)), dma((3,)),
            dma((7,)), dma((7,)),
        ],
        compiler_params=pltpu.CompilerParams(collective_id=0, has_side_effects=True, vmem_limit_bytes=VLIM),
        name="layer",
    )(split, tokens, cots, g1, s1, g2, s2, own)


VLIM = 64 * 1024 * 1024 - 64 * 1024


def fast_device(tokens, cotangent, split_point, w_qkv, w_out, w_up, w_down, gain_one, shift_one, gain_two, shift_two):
    batch, length, width = tokens.shape
    c = lax.rem(lax.axis_index("tensor"), 2)
    d = lax.axis_index("dp")
    band = width // 8
    q, k, v, o = w_qkv[0], w_qkv[1], w_qkv[2], w_out.T
    attn = jnp.concatenate(
        [q[:, :128], k[:, :128], v[:, :128], q[:, 128:], v[:, 128:], k[:, 128:], o[:, 128:], o[:, :128]], axis=1
    )
    own = jnp.stack([attn, w_up, w_down]).astype(F32)
    _, res, vecs, out, outs, gtok, gtoks = layer(
        split_point, tokens, cotangent, gain_one, shift_one, gain_two, shift_two, own
    )

    def both(mine, other):
        mine, other = mine[:, :length], other[:, :length]
        first = jnp.where(c == 0, mine, other)
        second = jnp.where(c == 0, other, mine)
        return jnp.concatenate([first, second], axis=0).astype(BF16)

    ra = jnp.concatenate([res[6], res[7], res[8]], axis=1)
    gq = jnp.concatenate([ra[:, 0:128], ra[:, 384:448]], axis=1)
    gk = jnp.concatenate([ra[:, 128:256], ra[:, 512:576]], axis=1)
    gv = jnp.concatenate([ra[:, 256:384], ra[:, 448:512]], axis=1)
    go = jnp.concatenate([ra[:, 640:768], ra[:, 576:640]], axis=1).T
    ru = jnp.concatenate([res[1], res[3], res[5]], axis=1)
    rd = jnp.concatenate([res[0], res[2], res[4]], axis=1).T
    mine = lax.dynamic_slice_in_dim(vecs, d * band, band, 1)
    return (
        both(out, outs), both(gtok, gtoks), jnp.stack([gq, gk, gv]), go, ru, rd,
        mine[0], mine[1], mine[2], mine[3],
    )


def layer_norm(values, gain_vec, shift_vec):
    row_mean = jnp.mean(values, axis=-1, keepdims=True)
    centered = values - row_mean
    variance = jnp.mean(centered * centered, axis=-1, keepdims=True)
    return centered * lax.rsqrt(variance + EPSILON) * gain_vec + shift_vec


def attention_forward(inputs, allowed, w_qkv, w_out, gain_one, shift_one):
    batch, length, width = inputs.shape
    local = w_qkv.shape[2]
    head_count = local // HD
    normed = layer_norm(inputs, gain_one, shift_one).astype(jnp.bfloat16)
    packed = jnp.einsum("btd,cde->cbte", normed, w_qkv, preferred_element_type=jnp.float32).astype(
        jnp.bfloat16
    )
    queries = packed[0].reshape(batch, length, head_count, HD)
    keys = packed[1].reshape(batch, length, head_count, HD)
    values = packed[2].reshape(batch, length, head_count, HD)
    scores = jnp.einsum(
        "bqhe,bkhe->bhqk", queries, keys, preferred_element_type=jnp.float32
    ) * HD ** (-0.5)
    scores = jnp.where(allowed[:, None], scores, -1e30)
    log_total = jax.nn.logsumexp(scores, axis=-1, keepdims=True)
    attn_probs = jnp.exp(scores - log_total)
    probs_low = attn_probs.astype(jnp.bfloat16)
    mixed = jnp.einsum("bhqk,bkhe->bqhe", probs_low, values, preferred_element_type=jnp.float32)
    mixed = mixed.reshape(batch, length, local).astype(jnp.bfloat16)
    partial_out = jnp.einsum("btk,kd->btd", mixed, w_out, preferred_element_type=jnp.float32)
    return (normed, queries, keys, values, attn_probs, probs_low, mixed, partial_out)


def mlp_forward(middle, w_up, gain_two, shift_two):
    normed_two = layer_norm(middle, gain_two, shift_two).astype(jnp.bfloat16)
    pre_act = jnp.einsum("btd,df->btf", normed_two, w_up, preferred_element_type=jnp.float32)
    activated = jax.nn.gelu(pre_act, approximate=False).astype(jnp.bfloat16)
    return (normed_two, pre_act, activated)


def per_device(
    tokens,
    cotangent,
    split_point,
    w_qkv,
    w_out,
    w_up,
    w_down,
    gain_one,
    shift_one,
    gain_two,
    shift_two,
):
    inputs = tokens.astype(jnp.float32)
    batch, length, width = tokens.shape
    local = w_qkv.shape[2]
    head_count = local // HD
    score_scale = HD ** (-0.5)
    places = jnp.arange(length, dtype=jnp.int32)
    limit = jnp.maximum(places[None, :, None], PATCHES + split_point[:, None, None] - 1)
    allowed = places[None, None, :] <= limit
    normed, queries, keys, values, attn_probs, probs_low, mixed, partial_out = attention_forward(
        inputs, allowed, w_qkv, w_out, gain_one, shift_one
    )
    middle = inputs + lax.psum(partial_out, "tensor")
    normed_two, pre_act, activated = mlp_forward(middle, w_up, gain_two, shift_two)
    branch = jnp.einsum("btf,fd->btd", activated, w_down, preferred_element_type=jnp.float32)
    output = (middle + lax.psum(branch, "tensor")).astype(jnp.bfloat16)
    normed, queries, keys, values, attn_probs, probs_low, mixed, partial_out = attention_forward(
        inputs, allowed, w_qkv, w_out, gain_one, shift_one
    )
    middle = inputs + lax.psum(partial_out, "tensor")
    normed_two, pre_act, activated = mlp_forward(middle, w_up, gain_two, shift_two)
    grad_output = cotangent.astype(jnp.float32)
    grad_act = jnp.einsum("btd,fd->btf", cotangent, w_down, preferred_element_type=jnp.float32)
    gelu_pull = jax.vjp(partial(jax.nn.gelu, approximate=False), pre_act)[1]
    grad_pre = gelu_pull(grad_act)[0].astype(jnp.bfloat16)
    grad_down_local = jnp.einsum(
        "btf,btd->fd", activated, cotangent, preferred_element_type=jnp.float32
    )
    grad_up_local = jnp.einsum(
        "btd,btf->df", normed_two, grad_pre, preferred_element_type=jnp.float32
    )
    grad_normed_two = lax.psum(
        jnp.einsum("btf,df->btd", grad_pre, w_up, preferred_element_type=jnp.float32), "tensor"
    )
    norm_two_pull = jax.vjp(layer_norm, middle, gain_two, shift_two)[1]
    grad_mid_norm, grad_gain_two, grad_shift_two = norm_two_pull(grad_normed_two)
    grad_middle = grad_output + grad_mid_norm
    grad_mid_low = grad_middle.astype(jnp.bfloat16)
    grad_out_local = jnp.einsum(
        "btk,btd->kd", mixed, grad_mid_low, preferred_element_type=jnp.float32
    )
    grad_mix = jnp.einsum("btd,kd->btk", grad_mid_low, w_out, preferred_element_type=jnp.float32)
    grad_mix = grad_mix.astype(jnp.bfloat16).reshape(batch, length, head_count, HD)
    grad_probs = jnp.einsum("bqhe,bkhe->bhqk", grad_mix, values, preferred_element_type=jnp.float32)
    row_terms = jnp.sum(attn_probs * grad_probs, axis=-1, keepdims=True)
    grad_scores = (attn_probs * (grad_probs - row_terms)).astype(jnp.bfloat16)
    grad_query = (
        jnp.einsum("bhqk,bkhe->bqhe", grad_scores, keys, preferred_element_type=jnp.float32)
        * score_scale
    )
    grad_key = (
        jnp.einsum("bhqk,bqhe->bkhe", grad_scores, queries, preferred_element_type=jnp.float32)
        * score_scale
    )
    grad_value = jnp.einsum(
        "bhqk,bqhe->bkhe", probs_low, grad_mix, preferred_element_type=jnp.float32
    )
    grad_packed = (
        jnp.stack([grad_query, grad_key, grad_value])
        .reshape(3, batch, length, local)
        .astype(jnp.bfloat16)
    )
    grad_qkv_local = jnp.einsum(
        "btd,cbte->cde", normed, grad_packed, preferred_element_type=jnp.float32
    )
    grad_normed = lax.psum(
        jnp.einsum("cbte,cde->btd", grad_packed, w_qkv, preferred_element_type=jnp.float32),
        "tensor",
    )
    norm_one_pull = jax.vjp(layer_norm, inputs, gain_one, shift_one)[1]
    grad_in_norm, grad_gain_one, grad_shift_one = norm_one_pull(grad_normed)
    grad_tokens = (grad_middle + grad_in_norm).astype(jnp.bfloat16)
    (
        qkv_part,
        out_part,
        up_part,
        down_part,
        gain_one_part,
        shift_one_part,
        gain_two_part,
        shift_two_part,
    ) = (
        lax.psum_scatter(grad_qkv_local, "dp", scatter_dimension=1, tiled=True),
        lax.psum_scatter(grad_out_local, "dp", scatter_dimension=1, tiled=True),
        lax.psum_scatter(grad_up_local, "dp", scatter_dimension=0, tiled=True),
        lax.psum_scatter(grad_down_local, "dp", scatter_dimension=1, tiled=True),
        lax.psum_scatter(grad_gain_one, "dp", scatter_dimension=0, tiled=True),
        lax.psum_scatter(grad_shift_one, "dp", scatter_dimension=0, tiled=True),
        lax.psum_scatter(grad_gain_two, "dp", scatter_dimension=0, tiled=True),
        lax.psum_scatter(grad_shift_two, "dp", scatter_dimension=0, tiled=True),
    )
    return (
        output,
        grad_tokens,
        qkv_part,
        out_part,
        up_part,
        down_part,
        gain_one_part,
        shift_one_part,
        gain_two_part,
        shift_two_part,
    )


def solution(mesh):
    in_specs = (
        P("dp", None, None),
        P("dp", None, None),
        P("dp"),
        P(None, None, "tensor"),
        P("tensor", None),
        P(None, "tensor"),
        P("tensor", None),
        P(),
        P(),
        P(),
        P(),
    )
    out_specs = (
        P("dp", None, None),
        P("dp", None, None),
        P(None, "dp", "tensor"),
        P("tensor", "dp"),
        P("dp", "tensor"),
        P("tensor", "dp"),
        P("dp"),
        P("dp"),
        P("dp"),
        P("dp"),
    )
    fast = mesh.shape["dp"] == 8 and mesh.shape["tensor"] == 4
    return jax.shard_map(
        fast_device if fast else per_device, mesh=mesh, in_specs=in_specs, out_specs=out_specs, check_vma=False
    )
```

```python
from functools import partial

import jax
import jax.numpy as jnp
from jax import lax
from jax.experimental import pallas as pl
from jax.experimental.pallas import tpu as pltpu
from jax.sharding import PartitionSpec as P

HD = 64
PATCHES = 196
EPSILON = 1e-05
MESH = pl.DeviceIdType.MESH
F32 = jnp.float32
BF16 = jnp.bfloat16
CH = 256


def mm(a, b):
    return jnp.dot(a, b, preferred_element_type=F32)


def mm_nt(a, b):
    return lax.dot_general(a, b, (((1,), (1,)), ((), ())), preferred_element_type=F32)


def mm_tn(a, b):
    return lax.dot_general(a, b, (((0,), (0,)), ((), ())), preferred_element_type=F32)


def ln_stats(v):
    mean = jnp.mean(v, axis=-1, keepdims=True)
    cen = v - mean
    var = jnp.mean(cen * cen, axis=-1, keepdims=True)
    rstd = lax.rsqrt(var + EPSILON)
    return cen * rstd, rstd


def ln_back(v, gy, gain):
    xhat, rstd = ln_stats(v)
    gx = gy * gain
    m1 = jnp.mean(gx, axis=-1, keepdims=True)
    m2 = jnp.mean(gx * xhat, axis=-1, keepdims=True)
    return rstd * (gx - m1 - xhat * m2), jnp.sum(gy * xhat, axis=0, keepdims=True), jnp.sum(gy, axis=0, keepdims=True)


def rcopy(src, dst, ssem, rsem, dev):
    return pltpu.make_async_remote_copy(
        src_ref=src, dst_ref=dst, send_sem=ssem, recv_sem=rsem, device_id=dev, device_id_type=MESH
    )


HEADS = ((0, 1, 2, False), (0, 1, 2, True), (3, 4, 3, False))


ZFIRST = (False, True, True, False, False, False, False, True, False)
REUSE = (1, 2, 3)

PLAN = {
    ("start", 0): (("s", 0, 0, 0), ("c", 0, 0, 0)),
    ("L", 2): (("g", 0, 0, 1), ("s", 1, 1, 0), ("s", 0, 1, 0), ("d", 0, 0, 0)),
    ("F", 4): (("g", 0, 0, 2),),
    ("F", 5): (("g", 0, 1, 1),),
    ("F", 8): (("g", 0, 0, 3),),
    ("j", 2): (("g", 0, 1, 2), ("g", 0, 1, 3), ("c", 1, 0, 0), ("g", 1, 1, 1), ("s", 2, 0, 0), ("s", 2, 1, 0),
        ("g", 0, 0, 4), ("c", 2, 0, 0), ("g", 1, 1, 2), ("g", 0, 1, 4), ("g", 2, 1, 1), ("d", 2, 0, 0),
        ("g", 1, 1, 3), ("w", 0, 0, 0)),
    ("F", 12): (("g", 2, 1, 2), ("g", 2, 0, 1), ("s", 1, 0, 0)),
    ("F", 15): (("g", 1, 1, 4),),
    ("F", 16): (("g", 1, 0, 1),),
    ("F", 17): (("g", 2, 1, 3),),
    ("F", 18): (("g", 2, 0, 2), ("d", 1, 0, 0)),
    ("fill", 1): (("g", 1, 0, 2),),
    ("O", 0): (("g", 2, 0, 3),),
    ("O", 1): (("g", 1, 0, 3), ("g", 2, 1, 4)),
    ("O", 2): (("r", 0, 0, 1), ("r", 1, 0, 1)),
    ("O", 4): (("r", 2, 0, 1), ("r", 3, 0, 1), ("g", 1, 0, 4), ("g", 2, 0, 4), ("w", 2, 0, 0)),
    ("fill", 2): (("w", 1, 0, 0),),
    ("P", 0): (("r", 4, 0, 1),),
    ("P", 1): (("r", 1, 0, 2),),
    ("P", 2): (("r", 0, 0, 2),),
    ("P", 4): (("r", 2, 0, 2),),
    ("P", 5): (("r", 1, 0, 3), ("r", 5, 0, 1)),
    ("fill", 4): (("r", 3, 0, 2),),
    ("B", 3): (("r", 1, 0, 4), ("r", 2, 0, 3), ("r", 0, 0, 3)),
    ("B", 4): (("r", 4, 0, 2),),
    ("B", 6): (("r", 2, 0, 4), ("r", 3, 0, 3), ("r", 0, 0, 4)),
    ("B", 8): (("r", 5, 0, 2),),
    ("B", 9): (("r", 3, 0, 4),),
    ("b", 1): (("r", 6, 0, 1), ("r", 7, 0, 1), ("r", 5, 0, 3), ("r", 5, 0, 4), ("r", 8, 0, 1), ("r", 4, 0, 3)),
    ("B", 14): (("r", 4, 0, 4), ("r", 6, 0, 2)),
    ("B", 15): (("r", 7, 0, 2),),
    ("B", 18): (("r", 8, 0, 2),),
    ("fill", 6): (("r", 6, 0, 3), ("r", 8, 0, 3), ("r", 6, 0, 4), ("r", 7, 0, 3), ("r", 7, 0, 4), ("r", 8, 0, 4)),
}


def layer_kernel(
    split, tokens, cots, g1, s1, g2, s2, own,
    wf, vecs, gqkv, gout, gup, gdown, output, gtok, outs, gtoks,
    tok, stage, cotp, n1, qkv, prob, mx, mid, br, gn, n2, ust, dst, wbf, ta, tb, gp, gmix,
    po, ps, cr, ra, rb, rc, gv, vcr, vr,
    isem, wsem, csend, crecv, ysend, yrecv, dsend, drecv, rcs, rcr, rsend, rrecv, osend, orecv, vsend, vrecv,
):
    ex, rows, width = tok.shape
    rpad = n1.shape[1]
    t = ex * rpad
    d, tt = lax.axis_index("dp"), lax.axis_index("tensor")
    zh, zl, x = d // 4, lax.rem(d // 2, 2), lax.rem(d, 2)
    y, c = tt // 2, lax.rem(tt, 2)
    sib = (d, y * 2 + 1 - c)
    ynb = (d, (1 - y) * 2 + c)

    def dpi(fh, fl, fx):
        return ((1 - zh) if fh else zh) * 4 + ((1 - zl) if fl else zl) * 2 + ((1 - x) if fx else x)

    znb2, znb1, xnb = (dpi(1, 0, 0), tt), (dpi(0, 1, 0), tt), (dpi(0, 0, 1), tt)

    def band(i):
        return pl.ds(pl.multiple_of(i * (width // 8), width // 8), width // 8)

    peers = [sib, ynb] + [(lax.rem(d + k, 8), tt) for k in range(1, 8)]
    barrier = pltpu.get_barrier_semaphore()
    for p in peers:
        pl.semaphore_signal(barrier, 1, device_id=p, device_id_type=MESH)
    pl.semaphore_wait(barrier, len(peers))

    def third(h):
        return slice(h * CH, (h + 1) * CH)

    def y_slice(p, h):
        return rcopy(own.at[p, band(d), third(h)], wf.at[1, p, band(d), third(h)], ysend.at[p, h], yrecv.at[p, h], ynb)

    def y_direct(p):
        return rcopy(own.at[p, :, third(2)], wf.at[1, p, :, third(2)], ysend.at[p, 2], yrecv.at[p, 2], ynb)

    def c_first(p):
        return rcopy(own.at[p], wf.at[0, p], csend.at[p], crecv.at[p], sib)

    def c_second(p):
        return rcopy(wf.at[1, p], wf.at[2, p], csend.at[3 + p], crecv.at[3 + p], sib)

    hops = (
        (dpi(0, 0, 0), dpi(1, 0, 0), znb2),
        (dpi(0, 0, 0), dpi(0, 1, 0), znb1),
        (dpi(1, 0, 0), dpi(1, 1, 0), znb1),
        (dpi(0, 0, 0), dpi(0, 0, 1), xnb),
        (dpi(1, 0, 0), dpi(1, 0, 1), xnb),
        (dpi(0, 1, 0), dpi(0, 1, 1), xnb),
        (dpi(1, 1, 0), dpi(1, 1, 1), xnb),
    )

    def hop(p, h, k, arriving=False):
        blk = wf.at[1, p, band(hops[k][1] if arriving else hops[k][0]), third(h)]
        return rcopy(blk, blk, dsend.at[2 * p + h, k], drecv.at[2 * p + h, k], hops[k][2])

    def g_step(p, h, stage):
        if stage == 1:
            y_slice(p, h).wait_recv()
            go = (0, 1, 3)
        elif stage == 2:
            hop(p, h, 0, True).wait_recv()
            hop(p, h, 1, True).wait_recv()
            go = (2, 4, 5)
        elif stage == 3:
            hop(p, h, 2, True).wait_recv()
            go = (6,)
        else:
            for k in (3, 4, 5, 6):
                hop(p, h, k, True).wait_recv()
            go = ()
        for k in go:
            hop(p, h, k).start()

    def fetch(j, p, i, b):
        def src(ref):
            if p == 2:
                return ref.at[pl.ds(pl.multiple_of(i * CH, CH), CH), :]
            return ref.at[:, pl.ds(pl.multiple_of(i * CH, CH), CH)]

        dstr = (dst if p == 2 else ust).at[b]
        sem = wsem.at[1 if p == 2 else 0, b]

        @pl.when(j == 0)
        def _():
            pltpu.make_async_copy(src(own.at[p]), dstr, sem).start()

        @pl.when(j > 0)
        def _():
            pltpu.make_async_copy(src(wf.at[jnp.maximum(j - 1, 0), p]), dstr, sem).start()

    def fetched(p, b):
        dstr = (dst if p == 2 else ust).at[b]
        pltpu.make_async_copy(dstr, dstr, wsem.at[1 if p == 2 else 0, b]).wait()

    def load_attn(j):
        fetch(j, 0, 0, 0)
        fetch(j, 0, 1, 1)

    def take_attn(j):
        fetched(0, 0)
        wbf[j, :, :CH] = ust[0].astype(BF16)
        fetch(j, 0, 2, 0)
        fetched(0, 1)
        wbf[j, :, CH : 2 * CH] = ust[1].astype(BF16)
        fetched(0, 0)
        wbf[j, :, 2 * CH :] = ust[0].astype(BF16)

    def c_grad(u, slot):
        return rcopy(ps.at[slot], cr.at[u % 6], rcs.at[u], rcr.at[u], sib)

    def views(pu, zfirst):
        if zfirst:
            return (
                ((pu, slice(None), 1 - zl), (pu, slice(None), zl), znb1),
                ((pu, 1 - zh, zl), (pu, zh, zl), znb2),
                ((pu, zh, zl, 1 - x), (pu, zh, zl, x), xnb),
            )
        return (
            ((pu, slice(None), slice(None), 1 - x), (pu, slice(None), slice(None), x), xnb),
            ((pu, slice(None), 1 - zl, x), (pu, slice(None), zl, x), znb1),
            ((pu, 1 - zh, zl, x), (pu, zh, zl, x), znb2),
        )

    def halving(u, pu, k, zfirst):
        src = po.at[views(pu, zfirst)[k][0]]
        return rcopy(src, (ra, rb, rc)[k].at[u], rsend.at[u, k], rrecv.at[u, k], views(pu, zfirst)[k][2])

    def r_step(u, pu, stage, zfirst):
        view = views(pu, zfirst)
        if stage == 1:
            c_grad(u, 0).wait_recv()
            away = view[0][0][1:]
            po[(pu,) + away] += cr[(u % 6,) + away]
            halving(u, pu, 0, zfirst).start()
            keep = view[0][1][1:]
            po[(pu,) + keep] += cr[(u % 6,) + keep]
        elif stage < 4:
            k = stage - 2
            halving(u, pu, k, zfirst).wait_recv()
            po[view[k][1]] += (ra, rb)[k][u]
            halving(u, pu, k + 1, zfirst).start()
        else:
            halving(u, pu, 2, zfirst).wait_recv()
            hand_out(u, po[view[2][1]] + rc[u])

    def hand_out(u, g):
        if u < 6:
            cols = slice(u // 2 * CH, (u // 2 + 1) * CH)
            if u % 2:
                gup[:, cols] = g
            else:
                gdown[:, cols] = g
        elif u == 6:
            gqkv[0, :, :128] = g[:, :128]
            gqkv[1, :, :128] = g[:, 128:]
        elif u == 7:
            gqkv[2, :, :128] = g[:, :128]
            gqkv[0, :, 128:] = g[:, 128 : 128 + HD]
            gqkv[2, :, 128:] = g[:, 128 + HD :]
        else:
            gqkv[1, :, 128:] = g[:, :HD]
            turned = g.T
            gout[128:, :] = turned[HD:128]
            gout[:128, :] = turned[128:]

    def r_sent(u, pu, zfirst):
        for k in range(3):
            halving(u, pu, k, zfirst).wait_send()

    def place_of(u):
        return u if u < 6 else REUSE[u - 6]

    def run(steps):
        for what, a, b, stage in steps:
            if what == "g":
                g_step(a, b, stage)
            elif what == "s":
                y_slice(a, b).start()
            elif what == "d":
                y_direct(a).start()
            elif what == "c":
                c_first(a).start()
            elif what == "w":
                y_direct(a).wait_recv()
                c_second(a).start()
            else:
                r_step(a, place_of(a), stage, ZFIRST[a])

    def tick(at, where):
        for (name, when), steps in PLAN.items():
            if name == where:
                @pl.when(at == when)
                def _(steps=steps):
                    run(steps)

    def fill(where, at):
        run(PLAN.get((where, at), ()))

    fill("start", 0)
    load_attn(0)
    cin = pltpu.make_async_copy(cots.at[pl.ds(c * ex, ex)], tok, isem.at[1])
    cin.start()
    cotp[...] = jnp.zeros_like(cotp)
    cin.wait()

    @pl.loop(0, ex)
    def _(e):
        cotp[e, :rows, :] = tok[e]

    tin = pltpu.make_async_copy(tokens.at[pl.ds(c * ex, ex)], tok, isem.at[0])
    tin.start()
    ta[...] = cotp[...].reshape(t, width).T
    tin.wait()
    n1[...] = jnp.zeros_like(n1)
    mid[...] = jnp.zeros_like(mid)
    gv[...] = jnp.zeros_like(gv)

    @pl.loop(0, ex)
    def _(e):
        tick(e, "L")
        v = tok[e].astype(F32)
        xhat, _ = ln_stats(v)
        n1[e, :rows, :] = (xhat * g1[...][None] + s1[...][None]).astype(BF16)
        mid[e, :rows, :] = v

    low_half = lax.broadcasted_iota(jnp.int32, (rpad, 128), 1) < HD
    qi = lax.broadcasted_iota(jnp.int32, (rpad, rpad), 0)
    kj = lax.broadcasted_iota(jnp.int32, (rpad, rpad), 1)

    @pl.loop(0, 4)
    def _(j):
        take_attn(j)

        @pl.when(j == 0)
        def _():
            c_first(0).wait_recv()
            load_attn(1)

        tick(j * 5, "F")
        qkv[j] = mm(n1[...].reshape(t, width), wbf[j, :, :640]).astype(BF16).reshape(ex, rpad, 640)

        @pl.loop(0, ex)
        def _(e):
            tick(j * 5 + 1 + e, "F")
            allowed = kj <= jnp.maximum(qi, PATCHES - 1 + split[c * ex + e])
            outs_h = []
            for h, (gq, gk, gvv, high) in enumerate(HEADS):
                q = qkv[j, e, :, gq * 128 : gq * 128 + 128]
                q = jnp.where(low_half != high, q, jnp.zeros_like(q))
                k = qkv[j, e, :, gk * 128 : gk * 128 + 128]
                s = mm_nt(q, k) * (HD ** -0.5)
                s = jnp.where(allowed, s, -1e30)
                top = jnp.max(s, axis=-1, keepdims=True)
                p = jnp.exp(s - top)
                p = (p * (1.0 / jnp.sum(p, axis=-1, keepdims=True))).astype(BF16)
                prob[j, e, h] = p
                outs_h.append(mm(p, qkv[j, e, :, gvv * 128 : gvv * 128 + 128]))
            zero = jnp.zeros((rpad, 128), F32)
            mx[j, e, :, :128] = jnp.where(low_half, zero, outs_h[2]).astype(BF16)
            mx[j, e, :, 128:] = jnp.where(low_half, outs_h[0], outs_h[1]).astype(BF16)

        tick(j * 5 + 4, "F")
        mid[...] += mm_nt(mx[j].reshape(t, 256), wbf[j, :, 512:]).reshape(ex, rpad, width)

        @pl.when(j == 1)
        def _():
            fill("j", 2)
            load_attn(2)

        @pl.when(j == 2)
        def _():
            c_second(0).wait_recv()
            load_attn(3)

    @pl.loop(0, ex)
    def _(e):
        keep = lax.broadcasted_iota(jnp.int32, (rpad, 1), 0) < rows
        v = jnp.where(keep, mid[e], 0.0)
        mid[e] = v
        xhat, _ = ln_stats(v)
        n2[e] = (xhat * g2[...][None] + s2[...][None]).astype(BF16)
        br[e] = v
        gn[e] = jnp.zeros((rpad, width), F32)

    tb[...] = n2[...].reshape(t, width).T

    def chunk(b):
        u = ust[b].astype(BF16)
        dn = dst[b].astype(BF16)
        pre = mm(n2[...].reshape(t, width), u)
        ga = mm_nt(cotp[...].reshape(t, width), dn)
        phi = 0.5 * (1.0 + lax.erf(pre * (0.5 ** 0.5)))
        act = (pre * phi).astype(BF16)
        gpre = (ga * (phi + pre * jnp.exp(-0.5 * pre * pre) * 0.3989422804014327)).astype(BF16)
        br[...] += mm(act, dn).reshape(ex, rpad, width)
        gn[...] += mm_nt(gpre, u).reshape(ex, rpad, width)
        return act, gpre

    def fetch2(j, i, b):
        fetch(j, 1, i, b)
        fetch(j, 2, i, b)

    def fetched2(b):
        fetched(1, b)
        fetched(2, b)

    fill("fill", 1)
    c_first(1).wait_recv()
    c_first(2).wait_recv()
    fetch2(1, 0, 0)
    shape5 = po.shape[1:]

    @pl.loop(0, 6)
    def _(n):
        i, b = n // 2, lax.rem(n, 2)

        @pl.when(n < 5)
        def _():
            fetch2(b, (n + 1) // 2, 1 - b)

        fetched2(b)
        act, gpre = chunk(b)
        gd = mm(ta[...], act).reshape(shape5)
        gu = mm(tb[...], gpre).reshape(shape5)
        slot = 2 * lax.rem(i, 2)

        @pl.when(b == 0)
        def _():
            @pl.when(i == 2)
            def _():
                c_grad(0, 0).wait_send()
                c_grad(1, 1).wait_send()

            ps[slot] = gd
            ps[slot + 1] = gu
            c_grad(2 * i, slot).start()
            c_grad(2 * i + 1, slot + 1).start()

        @pl.when(b == 1)
        def _():
            po[2 * i] = gd
            po[2 * i + 1] = gu

        tick(n, "O")

    fill("fill", 2)
    fetch2(2, 0, 0)

    @pl.loop(0, 6)
    def _(n):
        b = lax.rem(n, 2)

        @pl.when(n == 2)
        def _():
            c_second(1).wait_recv()
            c_second(2).wait_recv()

        @pl.when(n < 5)
        def _():
            fetch2(2 + (n + 1) // 3, lax.rem(n + 1, 3), 1 - b)

        fetched2(b)
        chunk(b)
        tick(n, "P")

    o_copy = rcopy(br, outs, osend.at[0], orecv.at[0], sib)
    o_copy.start()
    fill("fill", 3)

    @pl.loop(0, ex)
    def _(e):
        back, dg, ds = ln_back(mid[e], gn[e], g2[...][None])
        gv[2:3, :] += dg
        gv[3:4, :] += ds
        gm = cotp[e].astype(F32) + back
        mid[e] = gm
        n2[e] = gm.astype(BF16)
        stage[e] = br[e, :rows, :].astype(BF16)
        gn[e] = jnp.zeros((rpad, width), F32)

    fill("fill", 4)
    gml = n2
    ta[...] = gml[...].reshape(t, width).T
    tb[...] = n1[...].reshape(t, width).T
    scale = HD ** -0.5

    mine, theirs = pl.ds(c * ex, ex), pl.ds((1 - c) * ex, ex)
    o_keep = pltpu.make_async_copy(stage, output.at[mine], isem.at[2])
    o_keep.start()
    o_back = pltpu.make_async_copy(outs, br, isem.at[0])
    o_other = pltpu.make_async_copy(stage, output.at[theirs], isem.at[1])

    @pl.loop(0, 4)
    def _(n):
        j = jnp.where(n < 2, 1 - n, n)
        tick(n * 5, "B")
        gmix[...] = mm(gml[...].reshape(t, width), wbf[j, :, 512:]).astype(BF16).reshape(ex, rpad, 256)

        @pl.loop(0, ex)
        def _(e):
            tick(n * 5 + 1 + e, "B")
            dq, dk, dv = [], [], []
            for h, (gq, gk, gvv, high) in enumerate(HEADS):
                gx = gmix[e, :, :128] if h == 2 else gmix[e, :, 128:]
                gx = jnp.where(low_half != (high or h == 2), gx, jnp.zeros_like(gx))
                p = prob[j, e, h]
                dp = mm_nt(gx, qkv[j, e, :, gvv * 128 : gvv * 128 + 128])
                pf = p.astype(F32)
                pd = pf * dp
                ds = (pd - pf * jnp.sum(pd, axis=-1, keepdims=True)).astype(BF16)
                dq.append(mm(ds, qkv[j, e, :, gk * 128 : gk * 128 + 128]) * scale)
                dk.append(mm_tn(ds, qkv[j, e, :, gq * 128 : gq * 128 + 128]) * scale)
                dv.append(mm_tn(p, gx))
            zero = jnp.zeros((rpad, 128), F32)
            gp[e, :, 0:128] = jnp.where(low_half, dq[0], dq[1]).astype(BF16)
            gp[e, :, 128:256] = jnp.where(low_half, dk[0], dk[1]).astype(BF16)
            gp[e, :, 256:384] = jnp.where(low_half, dv[0], dv[1]).astype(BF16)
            gp[e, :, 384:512] = jnp.where(low_half, dq[2], dv[2]).astype(BF16)
            gp[e, :, 512:640] = jnp.where(low_half, dk[2], zero).astype(BF16)

        tick(n * 5 + 4, "B")
        gpf = gp[...].reshape(t, 640)
        gn[...] += mm_nt(gpf, wbf[j, :, :640]).reshape(ex, rpad, width)

        def grads(write):
            write(0, mm(tb[...], gpf[:, :256]).reshape(shape5))
            write(1, mm(tb[...], gpf[:, 256:512]).reshape(shape5))
            og = mm(ta[...], mx[j].reshape(t, 256))
            k2 = mm(tb[...], gpf[:, 512:640])
            write(2, jnp.concatenate([og[:, :128] + k2, og[:, 128:]], axis=1).reshape(shape5))

        @pl.when(n == 0)
        def _():
            for u in range(2, 6):
                c_grad(u, (0, 1, 2, 3, 0, 1)[u]).wait_send()

            def write(i, g):
                ps[i] = g
                c_grad(6 + i, i).start()

            grads(write)

        @pl.when(n == 1)
        def _():
            fill("b", 0)
            for u in REUSE:
                r_sent(u, u, ZFIRST[u])

            def write(i, g):
                po[REUSE[i]] = g

            grads(write)
            fill("b", 1)
            o_copy.wait()
            o_back.start()

        @pl.when(n == 2)
        def _():
            o_back.wait()
            o_keep.wait()

            @pl.loop(0, ex)
            def _(e):
                stage[e] = br[e, :rows, :].astype(BF16)

            o_other.start()

    fill("fill", 5)

    o_other.wait()

    @pl.loop(0, ex)
    def _(e):
        back, dg, ds = ln_back(tok[e].astype(F32), gn[e, :rows, :], g1[...][None])
        gv[0:1, :] += dg
        gv[1:2, :] += ds
        g = mid[e, :rows, :] + back
        br[e, :rows, :] = g
        tok[e] = g.astype(BF16)

    t_copy = rcopy(br, gtoks, osend.at[1], orecv.at[1], sib)
    t_copy.start()
    t_keep = pltpu.make_async_copy(tok, gtok.at[mine], isem.at[2])
    t_keep.start()
    t_back = pltpu.make_async_copy(gtoks, gn, isem.at[0])
    v_copy = rcopy(gv, vcr, osend.at[2], orecv.at[2], sib)
    v_copy.start()
    v_copy.wait()
    gv[...] += vcr[...]
    v_sends = []
    for k in range(1, 8):
        cp = rcopy(gv, vr.at[7 - k], vsend.at[k - 1], vrecv.at[7 - k], (lax.rem(d + k, 8), tt))
        cp.start()
        v_sends.append(cp)
    t_copy.wait()
    t_back.start()
    fill("fill", 6)
    for k in range(1, 8):
        rcopy(gv, vr.at[k - 1], vsend.at[k - 1], vrecv.at[k - 1], sib).wait_recv()
    acc = None
    for i in range(8):
        k = lax.rem(i - d + 8, 8)
        term = jnp.where(k == 0, gv[...], vr[jnp.maximum(k - 1, 0)])
        acc = term if acc is None else acc + term
    vecs[...] = acc

    t_back.wait()
    t_keep.wait()

    @pl.loop(0, ex)
    def _(e):
        tok[e] = gn[e, :rows, :].astype(BF16)

    t_other = pltpu.make_async_copy(tok, gtok.at[theirs], isem.at[1])
    t_other.start()
    for cp in v_sends:
        cp.wait_send()
    for p in range(3):
        y_direct(p).wait_send()
        c_first(p).wait_send()
        c_second(p).wait_send()
        for h in range(2):
            y_slice(p, h).wait_send()
            for k in range(7):
                hop(p, h, k).wait_send()
    for u in range(9):
        if u not in REUSE:
            r_sent(u, place_of(u), ZFIRST[u])
    for u in range(6, 9):
        c_grad(u, u - 6).wait_send()
    t_other.wait()


def layer(split, tokens, cots, g1, s1, g2, s2, own):
    batch, rows, width = tokens.shape
    ex = batch // 2
    rpad = -(-rows // 16) * 16
    t = ex * rpad
    band = width // 8
    sds = jax.ShapeDtypeStruct
    dma = pltpu.SemaphoreType.DMA
    vm = pltpu.VMEM
    ANY = pl.BlockSpec(memory_space=pl.ANY)
    VM = pl.BlockSpec(memory_space=pltpu.VMEM)
    SM = pl.BlockSpec(memory_space=pltpu.SMEM)
    act = (ex, rpad, width)
    return pl.pallas_call(
        layer_kernel,
        out_shape=(
            sds((3, 3, width, 768), F32), sds((8, width), F32),
            sds((3, band, 192), F32), sds((192, band), F32), sds((band, 768), F32), sds((band, 768), F32),
            sds(tokens.shape, BF16), sds(tokens.shape, BF16), sds(act, F32), sds(act, F32),
        ),
        in_specs=[SM, ANY, ANY, VM, VM, VM, VM, ANY],
        out_specs=(ANY, VM, VM, VM, VM, VM, ANY, ANY, ANY, ANY),
        scratch_shapes=[
            vm((ex, rows, width), BF16), vm((ex, rows, width), BF16), vm(act, BF16), vm(act, BF16),
            vm((4, ex, rpad, 640), BF16), vm((4, ex, 3, rpad, rpad), BF16), vm((4, ex, rpad, 256), BF16),
            vm(act, F32), vm(act, F32), vm(act, F32), vm(act, BF16),
            vm((2, width, CH), F32), vm((2, CH, width), F32), vm((4, width, 768), BF16),
            vm((width, t), BF16), vm((width, t), BF16), vm((ex, rpad, 640), BF16), vm((ex, rpad, 256), BF16),
            vm((6, 2, 2, 2, band, CH), F32), vm((4, 2, 2, 2, band, CH), F32), vm((6, 2, 2, 2, band, CH), F32),
            vm((9, 2, 2, band, CH), F32), vm((9, 2, band, CH), F32), vm((9, band, CH), F32),
            vm((8, width), F32), vm((8, width), F32), vm((7, 8, width), F32),
            dma((3,)), dma((2, 2)), dma((6,)), dma((6,)), dma((3, 3)), dma((3, 3)), dma((6, 7)), dma((6, 7)),
            dma((9,)), dma((9,)), dma((9, 3)), dma((9, 3)), dma((3,)), dma((3,)), dma((7,)), dma((7,)),
        ],
        compiler_params=pltpu.CompilerParams(collective_id=0, has_side_effects=True, vmem_limit_bytes=VLIM),
        name="layer",
    )(split, tokens, cots, g1, s1, g2, s2, own)


VLIM = 64 * 1024 * 1024 - 64 * 1024


def prepare_kernel(w_qkv, w_out, w_up, w_down, own):
    part = pl.program_id(0)

    @pl.when(part == 0)
    def _():
        q, k, v = (w_qkv[i].astype(F32).T for i in range(3))
        o = w_out[...].astype(F32).T
        for i, g in enumerate((
            q[:, :128], k[:, :128], v[:, :128], jnp.concatenate([q[:, 128:], v[:, 128:]], axis=1),
            jnp.concatenate([k[:, 128:], o[:, 128:]], axis=1), o[:, :128],
        )):
            own[0, :, i * 128 : (i + 1) * 128] = g

    @pl.when(part == 1)
    def _():
        own[0] = w_up[...].astype(F32)

    @pl.when(part == 2)
    def _():
        own[0] = w_down[...].astype(F32)


def prepare(w_qkv, w_out, w_up, w_down):
    width = w_up.shape[0]
    whole = lambda w: pl.BlockSpec(w.shape, lambda i: (0,) * w.ndim)
    return pl.pallas_call(
        prepare_kernel,
        grid=(3,),
        out_shape=jax.ShapeDtypeStruct((3, width, 768), F32),
        in_specs=[whole(w) for w in (w_qkv, w_out, w_up, w_down)],
        out_specs=pl.BlockSpec((1, width, 768), lambda i: (i, 0, 0)),
        name="prepare",
    )(w_qkv, w_out, w_up, w_down)


def fast_device(tokens, cotangent, split_point, w_qkv, w_out, w_up, w_down, gain_one, shift_one, gain_two, shift_two):
    batch, length, width = tokens.shape
    d = lax.axis_index("dp")
    band = width // 8
    own = prepare(w_qkv.transpose(0, 2, 1), w_out, w_up, w_down)
    _, vecs, gqkv, gout, gup, gdown, output, gtok, _, _ = layer(
        split_point, tokens, cotangent, gain_one, shift_one, gain_two, shift_two, own
    )
    mine = lax.dynamic_slice_in_dim(vecs, d * band, band, 1)
    return output, gtok, gqkv, gout, gup, gdown.T, mine[0], mine[1], mine[2], mine[3]


def layer_norm(values, gain_vec, shift_vec):
    row_mean = jnp.mean(values, axis=-1, keepdims=True)
    centered = values - row_mean
    variance = jnp.mean(centered * centered, axis=-1, keepdims=True)
    return centered * lax.rsqrt(variance + EPSILON) * gain_vec + shift_vec


def attention_forward(inputs, allowed, w_qkv, w_out, gain_one, shift_one):
    batch, length, width = inputs.shape
    local = w_qkv.shape[2]
    head_count = local // HD
    normed = layer_norm(inputs, gain_one, shift_one).astype(jnp.bfloat16)
    packed = jnp.einsum("btd,cde->cbte", normed, w_qkv, preferred_element_type=jnp.float32).astype(
        jnp.bfloat16
    )
    queries = packed[0].reshape(batch, length, head_count, HD)
    keys = packed[1].reshape(batch, length, head_count, HD)
    values = packed[2].reshape(batch, length, head_count, HD)
    scores = jnp.einsum(
        "bqhe,bkhe->bhqk", queries, keys, preferred_element_type=jnp.float32
    ) * HD ** (-0.5)
    scores = jnp.where(allowed[:, None], scores, -1e30)
    log_total = jax.nn.logsumexp(scores, axis=-1, keepdims=True)
    attn_probs = jnp.exp(scores - log_total)
    probs_low = attn_probs.astype(jnp.bfloat16)
    mixed = jnp.einsum("bhqk,bkhe->bqhe", probs_low, values, preferred_element_type=jnp.float32)
    mixed = mixed.reshape(batch, length, local).astype(jnp.bfloat16)
    partial_out = jnp.einsum("btk,kd->btd", mixed, w_out, preferred_element_type=jnp.float32)
    return (normed, queries, keys, values, attn_probs, probs_low, mixed, partial_out)


def mlp_forward(middle, w_up, gain_two, shift_two):
    normed_two = layer_norm(middle, gain_two, shift_two).astype(jnp.bfloat16)
    pre_act = jnp.einsum("btd,df->btf", normed_two, w_up, preferred_element_type=jnp.float32)
    activated = jax.nn.gelu(pre_act, approximate=False).astype(jnp.bfloat16)
    return (normed_two, pre_act, activated)


def per_device(
    tokens,
    cotangent,
    split_point,
    w_qkv,
    w_out,
    w_up,
    w_down,
    gain_one,
    shift_one,
    gain_two,
    shift_two,
):
    inputs = tokens.astype(jnp.float32)
    batch, length, width = tokens.shape
    local = w_qkv.shape[2]
    head_count = local // HD
    score_scale = HD ** (-0.5)
    places = jnp.arange(length, dtype=jnp.int32)
    limit = jnp.maximum(places[None, :, None], PATCHES + split_point[:, None, None] - 1)
    allowed = places[None, None, :] <= limit
    normed, queries, keys, values, attn_probs, probs_low, mixed, partial_out = attention_forward(
        inputs, allowed, w_qkv, w_out, gain_one, shift_one
    )
    middle = inputs + lax.psum(partial_out, "tensor")
    normed_two, pre_act, activated = mlp_forward(middle, w_up, gain_two, shift_two)
    branch = jnp.einsum("btf,fd->btd", activated, w_down, preferred_element_type=jnp.float32)
    output = (middle + lax.psum(branch, "tensor")).astype(jnp.bfloat16)
    normed, queries, keys, values, attn_probs, probs_low, mixed, partial_out = attention_forward(
        inputs, allowed, w_qkv, w_out, gain_one, shift_one
    )
    middle = inputs + lax.psum(partial_out, "tensor")
    normed_two, pre_act, activated = mlp_forward(middle, w_up, gain_two, shift_two)
    grad_output = cotangent.astype(jnp.float32)
    grad_act = jnp.einsum("btd,fd->btf", cotangent, w_down, preferred_element_type=jnp.float32)
    gelu_pull = jax.vjp(partial(jax.nn.gelu, approximate=False), pre_act)[1]
    grad_pre = gelu_pull(grad_act)[0].astype(jnp.bfloat16)
    grad_down_local = jnp.einsum(
        "btf,btd->fd", activated, cotangent, preferred_element_type=jnp.float32
    )
    grad_up_local = jnp.einsum(
        "btd,btf->df", normed_two, grad_pre, preferred_element_type=jnp.float32
    )
    grad_normed_two = lax.psum(
        jnp.einsum("btf,df->btd", grad_pre, w_up, preferred_element_type=jnp.float32), "tensor"
    )
    norm_two_pull = jax.vjp(layer_norm, middle, gain_two, shift_two)[1]
    grad_mid_norm, grad_gain_two, grad_shift_two = norm_two_pull(grad_normed_two)
    grad_middle = grad_output + grad_mid_norm
    grad_mid_low = grad_middle.astype(jnp.bfloat16)
    grad_out_local = jnp.einsum(
        "btk,btd->kd", mixed, grad_mid_low, preferred_element_type=jnp.float32
    )
    grad_mix = jnp.einsum("btd,kd->btk", grad_mid_low, w_out, preferred_element_type=jnp.float32)
    grad_mix = grad_mix.astype(jnp.bfloat16).reshape(batch, length, head_count, HD)
    grad_probs = jnp.einsum("bqhe,bkhe->bhqk", grad_mix, values, preferred_element_type=jnp.float32)
    row_terms = jnp.sum(attn_probs * grad_probs, axis=-1, keepdims=True)
    grad_scores = (attn_probs * (grad_probs - row_terms)).astype(jnp.bfloat16)
    grad_query = (
        jnp.einsum("bhqk,bkhe->bqhe", grad_scores, keys, preferred_element_type=jnp.float32)
        * score_scale
    )
    grad_key = (
        jnp.einsum("bhqk,bqhe->bkhe", grad_scores, queries, preferred_element_type=jnp.float32)
        * score_scale
    )
    grad_value = jnp.einsum(
        "bhqk,bqhe->bkhe", probs_low, grad_mix, preferred_element_type=jnp.float32
    )
    grad_packed = (
        jnp.stack([grad_query, grad_key, grad_value])
        .reshape(3, batch, length, local)
        .astype(jnp.bfloat16)
    )
    grad_qkv_local = jnp.einsum(
        "btd,cbte->cde", normed, grad_packed, preferred_element_type=jnp.float32
    )
    grad_normed = lax.psum(
        jnp.einsum("cbte,cde->btd", grad_packed, w_qkv, preferred_element_type=jnp.float32),
        "tensor",
    )
    norm_one_pull = jax.vjp(layer_norm, inputs, gain_one, shift_one)[1]
    grad_in_norm, grad_gain_one, grad_shift_one = norm_one_pull(grad_normed)
    grad_tokens = (grad_middle + grad_in_norm).astype(jnp.bfloat16)
    (
        qkv_part,
        out_part,
        up_part,
        down_part,
        gain_one_part,
        shift_one_part,
        gain_two_part,
        shift_two_part,
    ) = (
        lax.psum_scatter(grad_qkv_local, "dp", scatter_dimension=1, tiled=True),
        lax.psum_scatter(grad_out_local, "dp", scatter_dimension=1, tiled=True),
        lax.psum_scatter(grad_up_local, "dp", scatter_dimension=0, tiled=True),
        lax.psum_scatter(grad_down_local, "dp", scatter_dimension=1, tiled=True),
        lax.psum_scatter(grad_gain_one, "dp", scatter_dimension=0, tiled=True),
        lax.psum_scatter(grad_shift_one, "dp", scatter_dimension=0, tiled=True),
        lax.psum_scatter(grad_gain_two, "dp", scatter_dimension=0, tiled=True),
        lax.psum_scatter(grad_shift_two, "dp", scatter_dimension=0, tiled=True),
    )
    return (
        output,
        grad_tokens,
        qkv_part,
        out_part,
        up_part,
        down_part,
        gain_one_part,
        shift_one_part,
        gain_two_part,
        shift_two_part,
    )


def solution(mesh):
    in_specs = (
        P("dp", None, None),
        P("dp", None, None),
        P("dp"),
        P(None, None, "tensor"),
        P("tensor", None),
        P(None, "tensor"),
        P("tensor", None),
        P(),
        P(),
        P(),
        P(),
    )
    out_specs = (
        P("dp", None, None),
        P("dp", None, None),
        P(None, "dp", "tensor"),
        P("tensor", "dp"),
        P("dp", "tensor"),
        P("tensor", "dp"),
        P("dp"),
        P("dp"),
        P("dp"),
        P("dp"),
    )
    fast = mesh.shape["dp"] == 8 and mesh.shape["tensor"] == 4
    return jax.shard_map(
        fast_device if fast else per_device, mesh=mesh, in_specs=in_specs, out_specs=out_specs, check_vma=False
    )
```

```python
from functools import partial

import jax
import jax.numpy as jnp
from jax import lax
from jax.experimental import pallas as pl
from jax.experimental.pallas import tpu as pltpu
from jax.sharding import PartitionSpec as P

HD = 64
PATCHES = 196
EPSILON = 1e-05
MESH = pl.DeviceIdType.MESH
F32 = jnp.float32
BF16 = jnp.bfloat16
CH = 256


def mm(a, b):
    return jnp.dot(a, b, preferred_element_type=F32)


def mm_nt(a, b):
    return lax.dot_general(a, b, (((1,), (1,)), ((), ())), preferred_element_type=F32)


def mm_tn(a, b):
    return lax.dot_general(a, b, (((0,), (0,)), ((), ())), preferred_element_type=F32)


def ln_stats(v):
    mean = jnp.mean(v, axis=-1, keepdims=True)
    cen = v - mean
    var = jnp.mean(cen * cen, axis=-1, keepdims=True)
    rstd = lax.rsqrt(var + EPSILON)
    return cen * rstd, rstd


def ln_back(v, gy, gain):
    xhat, rstd = ln_stats(v)
    gx = gy * gain
    m1 = jnp.mean(gx, axis=-1, keepdims=True)
    m2 = jnp.mean(gx * xhat, axis=-1, keepdims=True)
    return rstd * (gx - m1 - xhat * m2), jnp.sum(gy * xhat, axis=0, keepdims=True), jnp.sum(gy, axis=0, keepdims=True)


def rcopy(src, dst, ssem, rsem, dev):
    return pltpu.make_async_remote_copy(
        src_ref=src, dst_ref=dst, send_sem=ssem, recv_sem=rsem, device_id=dev, device_id_type=MESH
    )


ZFIRST = (False, True, False, True, False, False, True, False, False)

PLAN = {
    ("start", 0): (("c", 0, 0, 0), ("s", 0, 1, 0)),
    ("L", 0): (("s", 0, 0, 0),),
    ("L", 2): (("g", 0, 1, 1),),
    ("own", 0): (("c", 1, 0, 0), ("c", 2, 0, 0), ("s", 2, 0, 0)),
    ("F", 1): (("g", 0, 0, 1),),
    ("F", 2): (("d", 0, 0, 0),),
    ("F", 3): (("g", 2, 0, 1),),
    ("j", 1): (("g", 0, 1, 2),),
    ("j", 2): (("g", 0, 0, 2), ("g", 2, 0, 2), ("g", 0, 1, 3), ("s", 1, 1, 0), ("g", 0, 0, 3), ("s", 2, 1, 0),
        ("g", 2, 0, 3), ("s", 1, 0, 0), ("g", 1, 1, 1), ("d", 1, 0, 0), ("g", 0, 1, 4), ("g", 2, 1, 1),
        ("g", 0, 0, 4), ("w", 0, 0, 0)),
    ("F", 7): (("g", 1, 0, 1),),
    ("F", 8): (("g", 2, 0, 4),),
    ("F", 9): (("g", 1, 1, 2),),
    ("F", 11): (("g", 2, 1, 2),),
    ("fill", 1): (("g", 1, 0, 2),),
    ("O", 0): (("d", 2, 0, 0),),
    ("O", 1): (("g", 1, 1, 3),),
    ("O", 2): (("r", 1, 0, 1), ("g", 2, 1, 3), ("g", 1, 0, 3)),
    ("O", 3): (("g", 1, 1, 4), ("r", 0, 0, 1)),
    ("O", 4): (("r", 3, 0, 1),),
    ("O", 5): (("g", 2, 1, 4), ("g", 1, 0, 4), ("w", 1, 0, 0)),
    ("fill", 2): (("r", 4, 0, 1), ("w", 2, 0, 0)),
    ("P", 0): (("r", 1, 0, 2),),
    ("n", 2): (("r", 0, 0, 2), ("r", 2, 0, 1)),
    ("P", 3): (("r", 3, 0, 2),),
    ("fill", 4): (("r", 4, 0, 2), ("r", 5, 0, 1)),
    ("B", 2): (("r", 0, 0, 3),),
    ("B", 3): (("r", 2, 0, 2),),
    ("B", 4): (("r", 1, 0, 3),),
    ("B", 5): (("r", 3, 0, 3), ("r", 0, 0, 4), ("r", 4, 0, 3)),
    ("b", 0): (("r", 1, 0, 4), ("r", 5, 0, 2), ("r", 3, 0, 4)),
    ("b", 1): (("r", 4, 0, 4), ("r", 8, 0, 1), ("r", 2, 0, 3), ("r", 6, 0, 1), ("r", 7, 0, 1)),
    ("B", 8): (("r", 5, 0, 3), ("r", 2, 0, 4)),
    ("B", 11): (("r", 8, 0, 2),),
    ("fill", 5): (("r", 5, 0, 4),),
    ("fill", 6): (("r", 6, 0, 2), ("r", 7, 0, 2), ("r", 8, 0, 3), ("r", 6, 0, 3), ("r", 7, 0, 3), ("r", 6, 0, 4),
        ("r", 8, 0, 4), ("r", 7, 0, 4)),
}


def layer_kernel(
    split, tokens, cots, g1, s1, g2, s2, w_qkv, w_out, w_up, w_down,
    own, wf, vecs, gqkv, gout, gup, gdown, output, gtok, outs, gtoks,
    tok, stage, cotp, n1, qkv, prob, mx, mid, br, gn, n2, ust, wbf, ta, tb, gp, gmix,
    po, ps, cr, ra, rb, rc, gv, vcr, vr,
    isem, ksem, wsem, csend, crecv, ysend, yrecv, dsend, drecv, rcs, rcr, rsend, rrecv, osend, orecv, vsend, vrecv,
):
    ex, rows, width = tok.shape
    rpad = n1.shape[1]
    t = ex * rpad
    d, tt = lax.axis_index("dp"), lax.axis_index("tensor")
    zh, zl, x = d // 4, lax.rem(d // 2, 2), lax.rem(d, 2)
    y, c = tt // 2, lax.rem(tt, 2)
    sib = (d, y * 2 + 1 - c)
    ynb = (d, (1 - y) * 2 + c)

    def dpi(fh, fl, fx):
        return ((1 - zh) if fh else zh) * 4 + ((1 - zl) if fl else zl) * 2 + ((1 - x) if fx else x)

    def at(fh, fl, fx):
        return ((1 - zh) if fh else zh, (1 - zl) if fl else zl, (1 - x) if fx else x)

    znb2, znb1, xnb = (dpi(1, 0, 0), tt), (dpi(0, 1, 0), tt), (dpi(0, 0, 1), tt)

    coming = [
        pltpu.make_async_copy(w_qkv.at[i], wbf.at[1, pl.ds(192 * i, 192)], isem.at[i]) for i in range(3)
    ] + [
        pltpu.make_async_copy(w_out, wbf.at[1, pl.ds(576, 192)], isem.at[3]),
        pltpu.make_async_copy(w_up, wbf.at[2], isem.at[4]),
        pltpu.make_async_copy(w_down, wbf.at[3], isem.at[5]),
        pltpu.make_async_copy(tokens.at[pl.ds(c * ex, ex)], tok, isem.at[6]),
        pltpu.make_async_copy(cots.at[pl.ds(c * ex, ex)], stage, isem.at[7]),
    ]
    for cp in coming:
        cp.start()

    peers = [sib, ynb] + [(lax.rem(d + k, 8), tt) for k in range(1, 8)]
    barrier = pltpu.get_barrier_semaphore()
    for p in peers:
        pl.semaphore_signal(barrier, 1, device_id=p, device_id_type=MESH)
    pl.semaphore_wait(barrier, len(peers))

    def y_slice(p, h):
        blk = (p, h) + at(0, 0, 0)
        return rcopy(own.at[blk], wf.at[(1,) + blk], ysend.at[p, h], yrecv.at[p, h], ynb)

    def y_direct(p):
        return rcopy(own.at[p, 2], wf.at[1, p, 2], ysend.at[p, 2], yrecv.at[p, 2], ynb)

    def c_first(p):
        return rcopy(own.at[p], wf.at[0, p], csend.at[p], crecv.at[p], sib)

    def c_second(p):
        return rcopy(wf.at[1, p], wf.at[2, p], csend.at[3 + p], crecv.at[3 + p], sib)

    hops = (
        (at(0, 0, 0), at(1, 0, 0), znb2),
        (at(0, 0, 0), at(0, 1, 0), znb1),
        (at(1, 0, 0), at(1, 1, 0), znb1),
        (at(0, 0, 0), at(0, 0, 1), xnb),
        (at(1, 0, 0), at(1, 0, 1), xnb),
        (at(0, 1, 0), at(0, 1, 1), xnb),
        (at(1, 1, 0), at(1, 1, 1), xnb),
    )

    def hop(p, h, k, arriving=False):
        blk = wf.at[(1, p, h) + (hops[k][1] if arriving else hops[k][0])]
        return rcopy(blk, blk, dsend.at[2 * p + h, k], drecv.at[2 * p + h, k], hops[k][2])

    def g_step(p, h, stage):
        if stage == 1:
            y_slice(p, h).wait_recv()
            go = (0, 1, 3)
        elif stage == 2:
            hop(p, h, 0, True).wait_recv()
            hop(p, h, 1, True).wait_recv()
            go = (2, 4, 5)
        elif stage == 3:
            hop(p, h, 2, True).wait_recv()
            go = (6,)
        else:
            for k in (3, 4, 5, 6):
                hop(p, h, k, True).wait_recv()
            go = ()
        for k in go:
            hop(p, h, k).start()

    def fetch(j, p, i, b):
        @pl.when(j == 0)
        def _():
            pltpu.make_async_copy(own.at[p, i], ust.at[b], wsem.at[b]).start()

        @pl.when(j > 0)
        def _():
            pltpu.make_async_copy(wf.at[jnp.maximum(j - 1, 0), p, i], ust.at[b], wsem.at[b]).start()

    def fetched(b):
        pltpu.make_async_copy(ust.at[b], ust.at[b], wsem.at[b]).wait()
        return ust[b].reshape(width, CH).astype(BF16)

    def load_attn(j):
        for i in range(3):
            fetch(j, 0, i, i)

    def take_attn(j):
        for i in range(3):
            wbf[j, :, i * CH : (i + 1) * CH] = fetched(i)

    def c_grad(u, slot):
        return rcopy(ps.at[slot], cr.at[u % 6], rcs.at[u], rcr.at[u], sib)

    def place_of(u):
        return (po, u) if u < 6 else (ust, u - 6)

    def views(pu, zfirst):
        if zfirst:
            return (
                ((pu, slice(None), 1 - zl), (pu, slice(None), zl), znb1),
                ((pu, 1 - zh, zl), (pu, zh, zl), znb2),
                ((pu, zh, zl, 1 - x), (pu, zh, zl, x), xnb),
            )
        return (
            ((pu, slice(None), slice(None), 1 - x), (pu, slice(None), slice(None), x), xnb),
            ((pu, slice(None), 1 - zl, x), (pu, slice(None), zl, x), znb1),
            ((pu, 1 - zh, zl, x), (pu, zh, zl, x), znb2),
        )

    def halving(u, k):
        ref, pu = place_of(u)
        away, _, to = views(pu, ZFIRST[u])[k]
        return rcopy(ref.at[away], (ra, rb, rc)[k].at[u], rsend.at[u, k], rrecv.at[u, k], to)

    def r_step(u, stage):
        ref, pu = place_of(u)
        view = views(pu, ZFIRST[u])
        if stage == 1:
            c_grad(u, 0).wait_recv()
            away, keep = view[0][0], view[0][1]
            ref[away] += cr[(u % 6,) + away[1:]]
            halving(u, 0).start()
            ref[keep] += cr[(u % 6,) + keep[1:]]
        elif stage < 4:
            k = stage - 2
            halving(u, k).wait_recv()
            ref[view[k][1]] += (ra, rb)[k][u]
            halving(u, k + 1).start()
        else:
            halving(u, 2).wait_recv()
            hand_out(u, ref[view[2][1]] + rc[u])

    def hand_out(u, g):
        if u < 6:
            cols = slice(u // 2 * CH, (u // 2 + 1) * CH)
            if u % 2:
                gup[:, cols] = g
            else:
                gdown[:, cols] = g
        elif u == 6:
            gqkv[0, :, :128] = g[:, :128]
            gqkv[1, :, :128] = g[:, 128:]
        elif u == 7:
            gqkv[2, :, :128] = g[:, :128]
            gqkv[0, :, 128:] = g[:, 128 : 128 + HD]
            gqkv[2, :, 128:] = g[:, 128 + HD :]
        else:
            gqkv[1, :, 128:] = g[:, :HD]
            turned = g.T
            gout[128:, :] = turned[HD:128]
            gout[:128, :] = turned[128:]

    def run(steps):
        for what, a, b, stage in steps:
            if what == "g":
                g_step(a, b, stage)
            elif what == "s":
                y_slice(a, b).start()
            elif what == "d":
                y_direct(a).start()
            elif what == "c":
                c_first(a).start()
            elif what == "w":
                y_direct(a).wait_recv()
                c_second(a).start()
            else:
                r_step(a, stage)

    def tick(at, where):
        for (name, when), steps in PLAN.items():
            if name == where:
                @pl.when(at == when)
                def _(steps=steps):
                    run(steps)

    def fill(where, at):
        run(PLAN.get((where, at), ()))

    for cp in coming[:4]:
        cp.wait()
    q_, k_, v_, o_ = 0, 192, 384, 576
    row = 0
    for src, n in (
        (q_, 128), (k_, 128), (v_, 128), (q_ + 128, HD), (v_ + 128, HD), (k_ + 128, HD), (o_ + 128, HD), (o_, 128),
    ):
        wbf[0, row : row + n, :] = wbf[1, src : src + n, :]
        row += n
    unit = ust.shape[1:]

    def keep_own(p, h, v, ref, slot):
        ref[slot] = v.astype(F32).reshape(unit)
        cp = pltpu.make_async_copy(ref.at[slot], own.at[p, h], ksem.at[p, h])
        cp.start()
        return cp

    kept = [keep_own(0, h, wbf[0, :, h * CH : (h + 1) * CH], ps, h) for h in range(3)]
    for cp in kept:
        cp.wait()
    fill("start", 0)
    coming[4].wait()
    kept = [keep_own(1, h, wbf[2, :, h * CH : (h + 1) * CH], po, h) for h in range(3)]
    coming[5].wait()
    kept += [keep_own(2, h, wbf[3, h * CH : (h + 1) * CH, :].T, po, 3 + h) for h in range(3)]
    coming[6].wait()
    n1[...] = jnp.zeros_like(n1)
    mid[...] = jnp.zeros_like(mid)
    gv[...] = jnp.zeros_like(gv)

    @pl.loop(0, ex)
    def _(e):
        tick(e, "L")
        v = tok[e].astype(F32)
        xhat, _ = ln_stats(v)
        n1[e, :rows, :] = (xhat * g1[...][None] + s1[...][None]).astype(BF16)
        mid[e, :rows, :] = v

    for cp in kept:
        cp.wait()
    fill("own", 0)

    low_half = lax.broadcasted_iota(jnp.int32, (rpad, 128), 1) < HD
    qi = lax.broadcasted_iota(jnp.int32, (rpad, rpad), 0)
    kj = lax.broadcasted_iota(jnp.int32, (rpad, rpad), 1)

    def group(j, e, i):
        return qkv[j, e, :, i * 128 : (i + 1) * 128]

    def half(v, high):
        return jnp.where(low_half != high, v, jnp.zeros_like(v))

    def pair(v):
        return jnp.concatenate([half(v, False), half(v, True)], axis=0)

    @pl.loop(0, 4)
    def _(j):
        @pl.when(j > 0)
        def _():
            take_attn(j)

        @pl.when(j == 0)
        def _():
            fill("j", 0)
            c_first(0).wait_recv()
            load_attn(1)

        tick(j * 3, "F")
        qkv[j] = mm_nt(n1[...].reshape(t, width), wbf[j, :640, :]).astype(BF16).reshape(ex, rpad, 640)
        tick(j * 3 + 1, "F")

        def scores(e):
            q01, q2 = pair(group(j, e, 0)), half(group(j, e, 3), False)
            return mm_nt(q01, group(j, e, 1)), mm_nt(q2, group(j, e, 4))

        nxt = scores(0)
        for e in range(ex):
            s01, s2 = nxt
            if e + 1 < ex:
                nxt = scores(e + 1)
            allowed = kj <= jnp.maximum(qi, PATCHES - 1 + split[c * ex + e])
            ps_h = []
            for h, s in enumerate((s01[:rpad], s01[rpad:], s2)):
                s = jnp.where(allowed, s * (HD ** -0.5), -1e30)
                p = jnp.exp(s - jnp.max(s, axis=-1, keepdims=True))
                p = (p * (1.0 / jnp.sum(p, axis=-1, keepdims=True))).astype(BF16)
                prob[j, e, h] = p
                ps_h.append(p)
            o01 = mm(jnp.concatenate(ps_h[:2], axis=0), group(j, e, 2))
            o2 = mm(ps_h[2], group(j, e, 3))
            mx[j, e, :, :128] = jnp.where(low_half, 0.0, o2).astype(BF16)
            mx[j, e, :, 128:] = jnp.where(low_half, o01[:rpad], o01[rpad:]).astype(BF16)

        tick(j * 3 + 2, "F")
        mid[...] += mm(mx[j].reshape(t, 256), wbf[j, 512:, :]).reshape(ex, rpad, width)

        @pl.when(j == 1)
        def _():
            fill("j", 1)
            coming[7].wait()
            cotp[...] = jnp.zeros_like(cotp)

            @pl.loop(0, ex)
            def _(e):
                cotp[e, :rows, :] = stage[e]

            ta[...] = cotp[...].reshape(t, width).T
            fill("j", 2)
            load_attn(2)

        @pl.when(j == 2)
        def _():
            fill("j", 3)
            c_second(0).wait_recv()
            load_attn(3)

    @pl.loop(0, ex)
    def _(e):
        keep = lax.broadcasted_iota(jnp.int32, (rpad, 1), 0) < rows
        v = jnp.where(keep, mid[e], 0.0)
        mid[e] = v
        xhat, _ = ln_stats(v)
        n2[e] = (xhat * g2[...][None] + s2[...][None]).astype(BF16)
        br[e] = v
        gn[e] = jnp.zeros((rpad, width), F32)

    tb[...] = n2[...].reshape(t, width).T

    def chunk(b):
        u, dn = fetched(b), fetched(2 + b)
        pre = mm(n2[...].reshape(t, width), u)
        ga = mm(cotp[...].reshape(t, width), dn)
        phi = 0.5 * (1.0 + lax.erf(pre * (0.5 ** 0.5)))
        act = (pre * phi).astype(BF16)
        gpre = (ga * (phi + pre * jnp.exp(-0.5 * pre * pre) * 0.3989422804014327)).astype(BF16)
        br[...] += mm_nt(act, dn).reshape(ex, rpad, width)
        gn[...] += mm_nt(gpre, u).reshape(ex, rpad, width)
        return act, gpre

    def fetch2(j, i, b):
        fetch(j, 1, i, b)
        fetch(j, 2, i, 2 + b)

    fill("fill", 1)
    c_first(1).wait_recv()
    c_first(2).wait_recv()
    fetch2(1, 0, 0)
    shape5 = po.shape[1:]

    @pl.loop(0, 6)
    def _(n):
        i, b = n // 2, lax.rem(n, 2)

        @pl.when(n < 5)
        def _():
            fetch2(b, (n + 1) // 2, 1 - b)

        act, gpre = chunk(b)
        gd = mm(ta[...], act).reshape(shape5)
        gu = mm(tb[...], gpre).reshape(shape5)
        slot = 2 * lax.rem(i, 2)

        @pl.when(b == 0)
        def _():
            @pl.when(i == 2)
            def _():
                c_grad(0, 0).wait_send()
                c_grad(1, 1).wait_send()

            ps[slot] = gd
            ps[slot + 1] = gu
            c_grad(2 * i, slot).start()
            c_grad(2 * i + 1, slot + 1).start()

        @pl.when(b == 1)
        def _():
            po[2 * i] = gd
            po[2 * i + 1] = gu

        tick(n, "O")

    fill("fill", 2)
    fetch2(2, 0, 0)

    @pl.loop(0, 6)
    def _(n):
        b = lax.rem(n, 2)

        @pl.when(n == 2)
        def _():
            fill("n", 2)
            c_second(1).wait_recv()
            c_second(2).wait_recv()

        @pl.when(n < 5)
        def _():
            fetch2(2 + (n + 1) // 3, lax.rem(n + 1, 3), 1 - b)

        chunk(b)
        tick(n, "P")

    o_copy = rcopy(br, outs, osend.at[0], orecv.at[0], sib)
    o_copy.start()
    fill("fill", 3)

    @pl.loop(0, ex)
    def _(e):
        back, dg, ds = ln_back(mid[e], gn[e], g2[...][None])
        gv[2:3, :] += dg
        gv[3:4, :] += ds
        gm = cotp[e].astype(F32) + back
        mid[e] = gm
        n2[e] = gm.astype(BF16)
        stage[e] = br[e, :rows, :].astype(BF16)
        gn[e] = jnp.zeros((rpad, width), F32)

    fill("fill", 4)
    gml = n2
    ta[...] = gml[...].reshape(t, width).T
    tb[...] = n1[...].reshape(t, width).T
    scale = HD ** -0.5

    mine, theirs = pl.ds(c * ex, ex), pl.ds((1 - c) * ex, ex)
    o_keep = pltpu.make_async_copy(stage, output.at[mine], isem.at[2])
    o_keep.start()
    o_back = pltpu.make_async_copy(outs, br, isem.at[0])
    o_other = pltpu.make_async_copy(stage, output.at[theirs], isem.at[1])

    @pl.loop(0, 4)
    def _(n):
        j = jnp.where(n < 2, 1 - n, n)
        tick(n * 3, "B")
        gmix[...] = mm_nt(gml[...].reshape(t, width), wbf[j, 512:, :]).astype(BF16).reshape(ex, rpad, 256)
        tick(n * 3 + 1, "B")

        def first(e):
            g01, g2_ = pair(gmix[e, :, 128:]), half(gmix[e, :, :128], True)
            return g01, g2_, mm_nt(g01, group(j, e, 2)), mm_nt(g2_, group(j, e, 3))

        nxt = first(0)
        for e in range(ex):
            g01, g2_, d01, d2 = nxt
            if e + 1 < ex:
                nxt = first(e + 1)
            q01 = pair(group(j, e, 0))
            ds = []
            for h, dp in enumerate((d01[:rpad], d01[rpad:], d2)):
                pf = prob[j, e, h].astype(F32)
                pd = pf * dp
                ds.append((pd - pf * jnp.sum(pd, axis=-1, keepdims=True)).astype(BF16))
            s01 = jnp.concatenate(ds[:2], axis=0)
            p01 = jnp.concatenate([prob[j, e, 0], prob[j, e, 1]], axis=0)
            dv01, dv2 = mm_tn(p01, g01), mm_tn(prob[j, e, 2], g2_)
            dq01, dq2 = mm(s01, group(j, e, 1)) * scale, mm(ds[2], group(j, e, 4)) * scale
            dk01, dk2 = mm_tn(s01, q01) * scale, mm_tn(ds[2], group(j, e, 3)) * scale
            gp[e, :, 0:128] = jnp.where(low_half, dq01[:rpad], dq01[rpad:]).astype(BF16)
            gp[e, :, 128:256] = dk01.astype(BF16)
            gp[e, :, 256:384] = dv01.astype(BF16)
            gp[e, :, 384:512] = jnp.where(low_half, dq2, dv2).astype(BF16)
            gp[e, :, 512:640] = jnp.where(low_half, dk2, 0.0).astype(BF16)

        tick(n * 3 + 2, "B")
        gpf = gp[...].reshape(t, 640)
        gn[...] += mm(gpf, wbf[j, :640, :]).reshape(ex, rpad, width)

        def grads(write):
            write(0, mm(tb[...], gpf[:, :256]).reshape(shape5))
            write(1, mm(tb[...], gpf[:, 256:512]).reshape(shape5))
            og = mm(ta[...], mx[j].reshape(t, 256))
            k2 = mm(tb[...], gpf[:, 512:640])
            write(2, jnp.concatenate([og[:, :128] + k2, og[:, 128:]], axis=1).reshape(shape5))

        @pl.when(n == 0)
        def _():
            for u in range(2, 6):
                c_grad(u, (0, 1, 2, 3, 0, 1)[u]).wait_send()

            o_copy.wait_recv()

            def write(i, g):
                ps[i] = g
                c_grad(6 + i, i).start()

            grads(write)

        @pl.when(n == 1)
        def _():
            fill("b", 0)

            def write(i, g):
                ust[i] = g

            grads(write)
            fill("b", 1)
            o_copy.wait_send()
            o_back.start()

        @pl.when(n == 2)
        def _():
            o_back.wait()
            o_keep.wait()

            @pl.loop(0, ex)
            def _(e):
                stage[e] = br[e, :rows, :].astype(BF16)

            o_other.start()

    fill("fill", 5)

    o_other.wait()

    @pl.loop(0, ex)
    def _(e):
        back, dg, ds = ln_back(tok[e].astype(F32), gn[e, :rows, :], g1[...][None])
        gv[0:1, :] += dg
        gv[1:2, :] += ds
        g = mid[e, :rows, :] + back
        br[e, :rows, :] = g
        tok[e] = g.astype(BF16)

    t_copy = rcopy(br, gtoks, osend.at[1], orecv.at[1], sib)
    t_copy.start()
    t_keep = pltpu.make_async_copy(tok, gtok.at[mine], isem.at[2])
    t_keep.start()
    t_back = pltpu.make_async_copy(gtoks, gn, isem.at[0])
    v_copy = rcopy(gv, vcr, osend.at[2], orecv.at[2], sib)
    v_copy.start()
    v_copy.wait()
    gv[...] += vcr[...]
    v_sends = []
    for k in range(1, 8):
        cp = rcopy(gv, vr.at[7 - k], vsend.at[k - 1], vrecv.at[7 - k], (lax.rem(d + k, 8), tt))
        cp.start()
        v_sends.append(cp)
    t_copy.wait()
    t_back.start()
    fill("fill", 6)
    for k in range(1, 8):
        rcopy(gv, vr.at[k - 1], vsend.at[k - 1], vrecv.at[k - 1], sib).wait_recv()
    acc = None
    for i in range(8):
        k = lax.rem(i - d + 8, 8)
        term = jnp.where(k == 0, gv[...], vr[jnp.maximum(k - 1, 0)])
        acc = term if acc is None else acc + term
    mine_v = jnp.zeros(vecs.shape, F32)
    for i in range(8):
        mine_v = jnp.where(d == i, acc[:, i * (width // 8) : (i + 1) * (width // 8)], mine_v)
    vecs[...] = mine_v

    t_back.wait()
    t_keep.wait()

    @pl.loop(0, ex)
    def _(e):
        tok[e] = gn[e, :rows, :].astype(BF16)

    t_other = pltpu.make_async_copy(tok, gtok.at[theirs], isem.at[1])
    t_other.start()
    for cp in v_sends:
        cp.wait_send()
    for p in range(3):
        y_direct(p).wait_send()
        c_first(p).wait_send()
        c_second(p).wait_send()
        for h in range(2):
            y_slice(p, h).wait_send()
            for k in range(7):
                hop(p, h, k).wait_send()
    for u in range(9):
        for k in range(3):
            halving(u, k).wait_send()
    for u in range(6, 9):
        c_grad(u, u - 6).wait_send()
    t_other.wait()


def layer(split, tokens, cots, g1, s1, g2, s2, w_qkv, w_out, w_up, w_down):
    batch, rows, width = tokens.shape
    ex = batch // 2
    rpad = -(-rows // 16) * 16
    t = ex * rpad
    band = width // 8
    sds = jax.ShapeDtypeStruct
    dma = pltpu.SemaphoreType.DMA
    vm = pltpu.VMEM
    ANY = pl.BlockSpec(memory_space=pl.ANY)
    VM = pl.BlockSpec(memory_space=pltpu.VMEM)
    SM = pl.BlockSpec(memory_space=pltpu.SMEM)
    act = (ex, rpad, width)
    unit = (2, 2, 2, band, CH)
    return pl.pallas_call(
        layer_kernel,
        out_shape=(
            sds((3, 3) + unit, F32), sds((3, 3, 3) + unit, F32), sds((8, band), F32),
            sds((3, band, 192), F32), sds((192, band), F32), sds((band, 768), F32), sds((band, 768), F32),
            sds(tokens.shape, BF16), sds(tokens.shape, BF16), sds(act, F32), sds(act, F32),
        ),
        in_specs=[SM, ANY, ANY, VM, VM, VM, VM, ANY, ANY, ANY, ANY],
        out_specs=(ANY, ANY, VM, VM, VM, VM, VM, ANY, ANY, ANY, ANY),
        scratch_shapes=[
            vm((ex, rows, width), BF16), vm((ex, rows, width), BF16), vm(act, BF16), vm(act, BF16),
            vm((4, ex, rpad, 640), BF16), vm((4, ex, 3, rpad, rpad), BF16), vm((4, ex, rpad, 256), BF16),
            vm(act, F32), vm(act, F32), vm(act, F32), vm(act, BF16),
            vm((4,) + unit, F32), vm((4, width, 768), BF16),
            vm((width, t), BF16), vm((width, t), BF16), vm((ex, rpad, 640), BF16), vm((ex, rpad, 256), BF16),
            vm((6,) + unit, F32), vm((4,) + unit, F32), vm((6,) + unit, F32),
            vm((9, 2, 2, band, CH), F32), vm((9, 2, band, CH), F32), vm((9, band, CH), F32),
            vm((8, width), F32), vm((8, width), F32), vm((7, 8, width), F32),
            dma((8,)), dma((3, 3)), dma((4,)), dma((6,)), dma((6,)), dma((3, 3)), dma((3, 3)), dma((6, 7)), dma((6, 7)),
            dma((9,)), dma((9,)), dma((9, 3)), dma((9, 3)), dma((3,)), dma((3,)), dma((7,)), dma((7,)),
        ],
        compiler_params=pltpu.CompilerParams(collective_id=0, has_side_effects=True, vmem_limit_bytes=VLIM),
        name="layer",
    )(split, tokens, cots, g1, s1, g2, s2, w_qkv, w_out, w_up, w_down)


VLIM = 64 * 1024 * 1024 - 64 * 1024


def fast_device(tokens, cotangent, split_point, w_qkv, w_out, w_up, w_down, gain_one, shift_one, gain_two, shift_two):
    batch, length, width = tokens.shape
    _, _, vecs, gqkv, gout, gup, gdown, output, gtok, _, _ = layer(
        split_point, tokens, cotangent, gain_one, shift_one, gain_two, shift_two,
        w_qkv.transpose(0, 2, 1), w_out, w_up, w_down,
    )
    return output, gtok, gqkv, gout, gup, gdown.T, vecs[0], vecs[1], vecs[2], vecs[3]


def layer_norm(values, gain_vec, shift_vec):
    row_mean = jnp.mean(values, axis=-1, keepdims=True)
    centered = values - row_mean
    variance = jnp.mean(centered * centered, axis=-1, keepdims=True)
    return centered * lax.rsqrt(variance + EPSILON) * gain_vec + shift_vec


def attention_forward(inputs, allowed, w_qkv, w_out, gain_one, shift_one):
    batch, length, width = inputs.shape
    local = w_qkv.shape[2]
    head_count = local // HD
    normed = layer_norm(inputs, gain_one, shift_one).astype(jnp.bfloat16)
    packed = jnp.einsum("btd,cde->cbte", normed, w_qkv, preferred_element_type=jnp.float32).astype(
        jnp.bfloat16
    )
    queries = packed[0].reshape(batch, length, head_count, HD)
    keys = packed[1].reshape(batch, length, head_count, HD)
    values = packed[2].reshape(batch, length, head_count, HD)
    scores = jnp.einsum(
        "bqhe,bkhe->bhqk", queries, keys, preferred_element_type=jnp.float32
    ) * HD ** (-0.5)
    scores = jnp.where(allowed[:, None], scores, -1e30)
    log_total = jax.nn.logsumexp(scores, axis=-1, keepdims=True)
    attn_probs = jnp.exp(scores - log_total)
    probs_low = attn_probs.astype(jnp.bfloat16)
    mixed = jnp.einsum("bhqk,bkhe->bqhe", probs_low, values, preferred_element_type=jnp.float32)
    mixed = mixed.reshape(batch, length, local).astype(jnp.bfloat16)
    partial_out = jnp.einsum("btk,kd->btd", mixed, w_out, preferred_element_type=jnp.float32)
    return (normed, queries, keys, values, attn_probs, probs_low, mixed, partial_out)


def mlp_forward(middle, w_up, gain_two, shift_two):
    normed_two = layer_norm(middle, gain_two, shift_two).astype(jnp.bfloat16)
    pre_act = jnp.einsum("btd,df->btf", normed_two, w_up, preferred_element_type=jnp.float32)
    activated = jax.nn.gelu(pre_act, approximate=False).astype(jnp.bfloat16)
    return (normed_two, pre_act, activated)


def per_device(
    tokens,
    cotangent,
    split_point,
    w_qkv,
    w_out,
    w_up,
    w_down,
    gain_one,
    shift_one,
    gain_two,
    shift_two,
):
    inputs = tokens.astype(jnp.float32)
    batch, length, width = tokens.shape
    local = w_qkv.shape[2]
    head_count = local // HD
    score_scale = HD ** (-0.5)
    places = jnp.arange(length, dtype=jnp.int32)
    limit = jnp.maximum(places[None, :, None], PATCHES + split_point[:, None, None] - 1)
    allowed = places[None, None, :] <= limit
    normed, queries, keys, values, attn_probs, probs_low, mixed, partial_out = attention_forward(
        inputs, allowed, w_qkv, w_out, gain_one, shift_one
    )
    middle = inputs + lax.psum(partial_out, "tensor")
    normed_two, pre_act, activated = mlp_forward(middle, w_up, gain_two, shift_two)
    branch = jnp.einsum("btf,fd->btd", activated, w_down, preferred_element_type=jnp.float32)
    output = (middle + lax.psum(branch, "tensor")).astype(jnp.bfloat16)
    normed, queries, keys, values, attn_probs, probs_low, mixed, partial_out = attention_forward(
        inputs, allowed, w_qkv, w_out, gain_one, shift_one
    )
    middle = inputs + lax.psum(partial_out, "tensor")
    normed_two, pre_act, activated = mlp_forward(middle, w_up, gain_two, shift_two)
    grad_output = cotangent.astype(jnp.float32)
    grad_act = jnp.einsum("btd,fd->btf", cotangent, w_down, preferred_element_type=jnp.float32)
    gelu_pull = jax.vjp(partial(jax.nn.gelu, approximate=False), pre_act)[1]
    grad_pre = gelu_pull(grad_act)[0].astype(jnp.bfloat16)
    grad_down_local = jnp.einsum(
        "btf,btd->fd", activated, cotangent, preferred_element_type=jnp.float32
    )
    grad_up_local = jnp.einsum(
        "btd,btf->df", normed_two, grad_pre, preferred_element_type=jnp.float32
    )
    grad_normed_two = lax.psum(
        jnp.einsum("btf,df->btd", grad_pre, w_up, preferred_element_type=jnp.float32), "tensor"
    )
    norm_two_pull = jax.vjp(layer_norm, middle, gain_two, shift_two)[1]
    grad_mid_norm, grad_gain_two, grad_shift_two = norm_two_pull(grad_normed_two)
    grad_middle = grad_output + grad_mid_norm
    grad_mid_low = grad_middle.astype(jnp.bfloat16)
    grad_out_local = jnp.einsum(
        "btk,btd->kd", mixed, grad_mid_low, preferred_element_type=jnp.float32
    )
    grad_mix = jnp.einsum("btd,kd->btk", grad_mid_low, w_out, preferred_element_type=jnp.float32)
    grad_mix = grad_mix.astype(jnp.bfloat16).reshape(batch, length, head_count, HD)
    grad_probs = jnp.einsum("bqhe,bkhe->bhqk", grad_mix, values, preferred_element_type=jnp.float32)
    row_terms = jnp.sum(attn_probs * grad_probs, axis=-1, keepdims=True)
    grad_scores = (attn_probs * (grad_probs - row_terms)).astype(jnp.bfloat16)
    grad_query = (
        jnp.einsum("bhqk,bkhe->bqhe", grad_scores, keys, preferred_element_type=jnp.float32)
        * score_scale
    )
    grad_key = (
        jnp.einsum("bhqk,bqhe->bkhe", grad_scores, queries, preferred_element_type=jnp.float32)
        * score_scale
    )
    grad_value = jnp.einsum(
        "bhqk,bqhe->bkhe", probs_low, grad_mix, preferred_element_type=jnp.float32
    )
    grad_packed = (
        jnp.stack([grad_query, grad_key, grad_value])
        .reshape(3, batch, length, local)
        .astype(jnp.bfloat16)
    )
    grad_qkv_local = jnp.einsum(
        "btd,cbte->cde", normed, grad_packed, preferred_element_type=jnp.float32
    )
    grad_normed = lax.psum(
        jnp.einsum("cbte,cde->btd", grad_packed, w_qkv, preferred_element_type=jnp.float32),
        "tensor",
    )
    norm_one_pull = jax.vjp(layer_norm, inputs, gain_one, shift_one)[1]
    grad_in_norm, grad_gain_one, grad_shift_one = norm_one_pull(grad_normed)
    grad_tokens = (grad_middle + grad_in_norm).astype(jnp.bfloat16)
    (
        qkv_part,
        out_part,
        up_part,
        down_part,
        gain_one_part,
        shift_one_part,
        gain_two_part,
        shift_two_part,
    ) = (
        lax.psum_scatter(grad_qkv_local, "dp", scatter_dimension=1, tiled=True),
        lax.psum_scatter(grad_out_local, "dp", scatter_dimension=1, tiled=True),
        lax.psum_scatter(grad_up_local, "dp", scatter_dimension=0, tiled=True),
        lax.psum_scatter(grad_down_local, "dp", scatter_dimension=1, tiled=True),
        lax.psum_scatter(grad_gain_one, "dp", scatter_dimension=0, tiled=True),
        lax.psum_scatter(grad_shift_one, "dp", scatter_dimension=0, tiled=True),
        lax.psum_scatter(grad_gain_two, "dp", scatter_dimension=0, tiled=True),
        lax.psum_scatter(grad_shift_two, "dp", scatter_dimension=0, tiled=True),
    )
    return (
        output,
        grad_tokens,
        qkv_part,
        out_part,
        up_part,
        down_part,
        gain_one_part,
        shift_one_part,
        gain_two_part,
        shift_two_part,
    )


def solution(mesh):
    in_specs = (
        P("dp", None, None),
        P("dp", None, None),
        P("dp"),
        P(None, None, "tensor"),
        P("tensor", None),
        P(None, "tensor"),
        P("tensor", None),
        P(),
        P(),
        P(),
        P(),
    )
    out_specs = (
        P("dp", None, None),
        P("dp", None, None),
        P(None, "dp", "tensor"),
        P("tensor", "dp"),
        P("dp", "tensor"),
        P("tensor", "dp"),
        P("dp"),
        P("dp"),
        P("dp"),
        P("dp"),
    )
    fast = mesh.shape["dp"] == 8 and mesh.shape["tensor"] == 4
    return jax.shard_map(
        fast_device if fast else per_device, mesh=mesh, in_specs=in_specs, out_specs=out_specs, check_vma=False
    )
```

```python
from functools import partial

import jax
import jax.numpy as jnp
from jax import lax
from jax.experimental import pallas as pl
from jax.experimental.pallas import tpu as pltpu
from jax.sharding import PartitionSpec as P

HD = 64
PATCHES = 196
EPSILON = 1e-05
MESH = pl.DeviceIdType.MESH
F32 = jnp.float32
BF16 = jnp.bfloat16
CH = 256


def mm(a, b):
    return jnp.dot(a, b, preferred_element_type=F32)


def mm_nt(a, b):
    return lax.dot_general(a, b, (((1,), (1,)), ((), ())), preferred_element_type=F32)


def mm_tn(a, b):
    return lax.dot_general(a, b, (((0,), (0,)), ((), ())), preferred_element_type=F32)


def ln_stats(v):
    mean = jnp.mean(v, axis=-1, keepdims=True)
    cen = v - mean
    var = jnp.mean(cen * cen, axis=-1, keepdims=True)
    rstd = lax.rsqrt(var + EPSILON)
    return cen * rstd, rstd


def ln_back(v, gy, gain):
    xhat, rstd = ln_stats(v)
    gx = gy * gain
    m1 = jnp.mean(gx, axis=-1, keepdims=True)
    m2 = jnp.mean(gx * xhat, axis=-1, keepdims=True)
    return rstd * (gx - m1 - xhat * m2), jnp.sum(gy * xhat, axis=0, keepdims=True), jnp.sum(gy, axis=0, keepdims=True)


def rcopy(src, dst, ssem, rsem, dev):
    return pltpu.make_async_remote_copy(
        src_ref=src, dst_ref=dst, send_sem=ssem, recv_sem=rsem, device_id=dev, device_id_type=MESH
    )


ZFIRST = (True, True, False, True, False, False, False, False, False)

PLAN = {
    ("start", 0): (("c", 0, 0, 0), ("s", 0, 0, 0), ("s", 0, 1, 0)),
    ("L", 0): (("d", 0, 0, 0),),
    ("own", 0): (("c", 1, 0, 0), ("c", 2, 0, 0)),
    ("j", 0): (("g", 0, 0, 1),),
    ("F", 3): (("g", 0, 1, 1),),
    ("F", 4): (("g", 0, 0, 2),),
    ("j", 2): (("s", 1, 0, 0), ("g", 0, 1, 2), ("g", 0, 0, 3), ("s", 1, 1, 0), ("g", 0, 1, 3), ("s", 2, 1, 0),
        ("g", 1, 0, 1), ("s", 2, 0, 0), ("g", 0, 0, 4), ("g", 1, 1, 1), ("d", 1, 0, 0), ("g", 0, 1, 4),
        ("w", 0, 0, 0)),
    ("F", 6): (("g", 1, 0, 2),),
    ("F", 7): (("g", 2, 1, 1), ("g", 2, 0, 1)),
    ("F", 10): (("g", 1, 1, 2),),
    ("O", 1): (("g", 1, 0, 3),),
    ("O", 2): (("d", 2, 0, 0), ("g", 2, 1, 2), ("g", 2, 0, 2)),
    ("O", 3): (("g", 1, 1, 3),),
    ("O", 4): (("r", 0, 0, 1),),
    ("O", 6): (("g", 1, 0, 4),),
    ("O", 7): (("g", 2, 1, 3), ("g", 2, 0, 3)),
    ("O", 9): (("r", 1, 0, 1),),
    ("O", 11): (("r", 2, 0, 1),),
    ("fill", 2): (("g", 1, 1, 4), ("w", 1, 0, 0), ("r", 0, 0, 2), ("g", 2, 1, 4), ("g", 2, 0, 4), ("w", 2, 0, 0)),
    ("P", 1): (("r", 5, 0, 1), ("r", 3, 0, 1)),
    ("P", 3): (("r", 0, 0, 3), ("r", 2, 0, 2)),
    ("P", 4): (("r", 1, 0, 2),),
    ("P", 5): (("r", 4, 0, 1),),
    ("N", 2): (("r", 0, 0, 4),),
    ("B", 3): (("r", 5, 0, 2), ("r", 2, 0, 3)),
    ("B", 5): (("r", 4, 0, 2), ("r", 1, 0, 3)),
    ("b", 1): (("r", 7, 0, 1), ("r", 3, 0, 2)),
    ("B", 7): (("r", 1, 0, 4),),
    ("B", 8): (("r", 2, 0, 4),),
    ("B", 9): (("r", 8, 0, 1),),
    ("B", 11): (("r", 5, 0, 3),),
    ("fill", 6): (("r", 4, 0, 3), ("r", 7, 0, 2), ("r", 6, 0, 1), ("r", 3, 0, 3), ("r", 5, 0, 4), ("r", 4, 0, 4),
        ("r", 7, 0, 3), ("r", 3, 0, 4), ("r", 8, 0, 2), ("r", 7, 0, 4), ("r", 6, 0, 2), ("r", 8, 0, 3),
        ("r", 8, 0, 4), ("r", 6, 0, 3), ("r", 6, 0, 4)),
}


def layer_kernel(
    split, tokens, cots, g1, s1, g2, s2, w_qkv, w_out, w_up, w_down,
    own, wf, vecs, gqkv, gout, gup, gdown, output, gtok, outs, gtoks,
    tok, stage, cotp, n1, qkv, prob, mx, mid, br, gn, n2, ust, wbf, ta, tb, gp, gmix,
    po, ps, cr, ra, rb, rc, gv, vcr, vr,
    isem, ksem, wsem, csend, crecv, ysend, yrecv, dsend, drecv, rcs, rcr, rsend, rrecv, osend, orecv, vsend, vrecv,
):
    ex, rows, width = tok.shape
    rpad = n1.shape[1]
    t = ex * rpad
    d, tt = lax.axis_index("dp"), lax.axis_index("tensor")
    zh, zl, x = d // 4, lax.rem(d // 2, 2), lax.rem(d, 2)
    y, c = tt // 2, lax.rem(tt, 2)
    sib = (d, y * 2 + 1 - c)
    ynb = (d, (1 - y) * 2 + c)

    def dpi(fh, fl, fx):
        return ((1 - zh) if fh else zh) * 4 + ((1 - zl) if fl else zl) * 2 + ((1 - x) if fx else x)

    def at(fh, fl, fx):
        return ((1 - zh) if fh else zh, (1 - zl) if fl else zl, (1 - x) if fx else x)

    znb2, znb1, xnb = (dpi(1, 0, 0), tt), (dpi(0, 1, 0), tt), (dpi(0, 0, 1), tt)

    coming = [
        pltpu.make_async_copy(w_qkv.at[i], wbf.at[1, pl.ds(192 * i, 192)], isem.at[i]) for i in range(3)
    ] + [
        pltpu.make_async_copy(w_out, wbf.at[1, pl.ds(576, 192)], isem.at[3]),
        pltpu.make_async_copy(w_up, wbf.at[2], isem.at[4]),
        pltpu.make_async_copy(w_down, wbf.at[3], isem.at[5]),
        pltpu.make_async_copy(tokens.at[pl.ds(c * ex, ex)], tok, isem.at[6]),
        pltpu.make_async_copy(cots.at[pl.ds(c * ex, ex)], stage, isem.at[7]),
    ]
    for cp in coming[:4]:
        cp.start()

    peers = [sib, ynb] + [(lax.rem(d + k, 8), tt) for k in range(1, 8)]
    barrier = pltpu.get_barrier_semaphore()
    for p in peers:
        pl.semaphore_signal(barrier, 1, device_id=p, device_id_type=MESH)

    def y_slice(p, h):
        blk = (p, h) + at(0, 0, 0)
        src = own.at[blk] if p else ps.at[(h,) + at(0, 0, 0)]
        return rcopy(src, wf.at[(1,) + blk], ysend.at[p, h], yrecv.at[p, h], ynb)

    def y_direct(p):
        return rcopy(own.at[p, 2] if p else ps.at[2], wf.at[1, p, 2], ysend.at[p, 2], yrecv.at[p, 2], ynb)

    def c_first(p):
        return rcopy(own.at[p] if p else ps.at[pl.ds(0, 3)], wf.at[0, p], csend.at[p], crecv.at[p], sib)

    def c_second(p):
        return rcopy(wf.at[1, p], wf.at[2, p], csend.at[3 + p], crecv.at[3 + p], sib)

    hops = (
        (at(0, 0, 0), at(1, 0, 0), znb2),
        (at(0, 0, 0), at(0, 1, 0), znb1),
        (at(1, 0, 0), at(1, 1, 0), znb1),
        (at(0, 0, 0), at(0, 0, 1), xnb),
        (at(1, 0, 0), at(1, 0, 1), xnb),
        (at(0, 1, 0), at(0, 1, 1), xnb),
        (at(1, 1, 0), at(1, 1, 1), xnb),
    )

    def hop(p, h, k, arriving=False):
        blk = wf.at[(1, p, h) + (hops[k][1] if arriving else hops[k][0])]
        return rcopy(blk, blk, dsend.at[2 * p + h, k], drecv.at[2 * p + h, k], hops[k][2])

    def g_step(p, h, stage):
        if stage == 1:
            y_slice(p, h).wait_recv()
            go = (0, 1, 3)
        elif stage == 2:
            hop(p, h, 0, True).wait_recv()
            hop(p, h, 1, True).wait_recv()
            go = (2, 4, 5)
        elif stage == 3:
            hop(p, h, 2, True).wait_recv()
            go = (6,)
        else:
            for k in (3, 4, 5, 6):
                hop(p, h, k, True).wait_recv()
            go = ()
        for k in go:
            hop(p, h, k).start()

    def fetch(j, p, i, b):
        @pl.when(j == 0)
        def _():
            pltpu.make_async_copy(own.at[p, i], ust.at[b], wsem.at[b]).start()

        @pl.when(j > 0)
        def _():
            pltpu.make_async_copy(wf.at[jnp.maximum(j - 1, 0), p, i], ust.at[b], wsem.at[b]).start()

    def fetched(b):
        pltpu.make_async_copy(ust.at[b], ust.at[b], wsem.at[b]).wait()
        return ust[b].reshape(width, CH).astype(BF16)

    def load_attn(j):
        for i in range(3):
            fetch(j, 0, i, i)

    def take_attn(j):
        for i in range(3):
            wbf[j, :, i * CH : (i + 1) * CH] = fetched(i)

    def c_grad(u, slot):
        return rcopy(ps.at[slot], cr.at[u % 6], rcs.at[u], rcr.at[u], sib)

    def place_of(u):
        return (po, u) if u < 6 else (ust, u - 6)

    def views(pu, zfirst):
        if zfirst:
            return (
                ((pu, slice(None), 1 - zl), (pu, slice(None), zl), znb1),
                ((pu, 1 - zh, zl), (pu, zh, zl), znb2),
                ((pu, zh, zl, 1 - x), (pu, zh, zl, x), xnb),
            )
        return (
            ((pu, slice(None), slice(None), 1 - x), (pu, slice(None), slice(None), x), xnb),
            ((pu, slice(None), 1 - zl, x), (pu, slice(None), zl, x), znb1),
            ((pu, 1 - zh, zl, x), (pu, zh, zl, x), znb2),
        )

    def halving(u, k):
        ref, pu = place_of(u)
        away, _, to = views(pu, ZFIRST[u])[k]
        return rcopy(ref.at[away], (ra, rb, rc)[k].at[u], rsend.at[u, k], rrecv.at[u, k], to)

    def r_step(u, stage):
        ref, pu = place_of(u)
        view = views(pu, ZFIRST[u])
        if stage == 1:
            c_grad(u, 0).wait_recv()
            away, keep = view[0][0], view[0][1]
            ref[away] += cr[(u % 6,) + away[1:]]
            halving(u, 0).start()
            ref[keep] += cr[(u % 6,) + keep[1:]]
        elif stage < 4:
            k = stage - 2
            halving(u, k).wait_recv()
            ref[view[k][1]] += (ra, rb)[k][u]
            halving(u, k + 1).start()
        else:
            halving(u, 2).wait_recv()
            hand_out(u, ref[view[2][1]] + rc[u])

    def hand_out(u, g):
        if u < 6:
            cols = slice(u // 2 * CH, (u // 2 + 1) * CH)
            if u % 2:
                gup[:, cols] = g
            else:
                gdown[:, cols] = g
        elif u == 6:
            gqkv[0, :, :128] = g[:, :128]
            gqkv[1, :, :128] = g[:, 128:]
        elif u == 7:
            gqkv[2, :, :128] = g[:, :128]
            gqkv[0, :, 128:] = g[:, 128 : 128 + HD]
            gqkv[2, :, 128:] = g[:, 128 + HD :]
        else:
            gqkv[1, :, 128:] = g[:, :HD]
            turned = g.T
            gout[128:, :] = turned[HD:128]
            gout[:128, :] = turned[128:]

    def run(steps):
        for what, a, b, stage in steps:
            if what == "g":
                g_step(a, b, stage)
            elif what == "s":
                y_slice(a, b).start()
            elif what == "d":
                y_direct(a).start()
            elif what == "c":
                c_first(a).start()
            elif what == "w":
                y_direct(a).wait_recv()
                c_second(a).start()
            else:
                r_step(a, stage)

    def tick(at, where):
        for (name, when), steps in PLAN.items():
            if name == where:
                @pl.when(at == when)
                def _(steps=steps):
                    run(steps)

    def fill(where, at):
        run(PLAN.get((where, at), ()))

    for cp in coming[:4]:
        cp.wait()
    q_, k_, v_, o_ = 0, 192, 384, 576
    row = 0
    for src, n in (
        (q_, 128), (k_, 128), (v_, 128), (q_ + 128, HD), (v_ + 128, HD), (k_ + 128, HD), (o_ + 128, HD), (o_, 128),
    ):
        wbf[0, row : row + n, :] = wbf[1, src : src + n, :]
        row += n
    unit = ust.shape[1:]

    def keep_own(p, h, v, ref, slot):
        ref[slot] = v.astype(F32).reshape(unit)
        cp = pltpu.make_async_copy(ref.at[slot], own.at[p, h], ksem.at[p, h])
        cp.start()
        return cp

    for h in range(3):
        ps[h] = wbf[0, :, h * CH : (h + 1) * CH].astype(F32).reshape(unit)
    pl.semaphore_wait(barrier, len(peers))
    fill("start", 0)
    for cp in coming[4:]:
        cp.start()
    coming[4].wait()
    kept = [keep_own(1, h, wbf[2, :, h * CH : (h + 1) * CH], po, h) for h in range(3)]
    coming[5].wait()
    kept += [keep_own(2, h, wbf[3, h * CH : (h + 1) * CH, :].T, po, 3 + h) for h in range(3)]
    coming[6].wait()
    n1[...] = jnp.zeros_like(n1)
    mid[...] = jnp.zeros_like(mid)
    gv[...] = jnp.zeros_like(gv)

    @pl.loop(0, ex)
    def _(e):
        tick(e, "L")
        v = tok[e].astype(F32)
        xhat, _ = ln_stats(v)
        n1[e, :rows, :] = (xhat * g1[...][None] + s1[...][None]).astype(BF16)
        mid[e, :rows, :] = v

    for cp in kept:
        cp.wait()
    fill("own", 0)

    low_half = lax.broadcasted_iota(jnp.int32, (rpad, 128), 1) < HD
    qi = lax.broadcasted_iota(jnp.int32, (rpad, rpad), 0)
    kj = lax.broadcasted_iota(jnp.int32, (rpad, rpad), 1)

    def group(j, e, i):
        return qkv[j, e, :, i * 128 : (i + 1) * 128]

    def half(v, high):
        return jnp.where(low_half != high, v, jnp.zeros_like(v))

    def pair(v):
        return jnp.concatenate([half(v, False), half(v, True)], axis=0)

    @pl.loop(0, 4)
    def _(j):
        @pl.when(j > 0)
        def _():
            take_attn(j)

        @pl.when(j == 0)
        def _():
            fill("j", 0)
            c_first(0).wait_recv()
            load_attn(1)

        tick(j * 3, "F")
        qkv[j] = mm_nt(n1[...].reshape(t, width), wbf[j, :640, :]).astype(BF16).reshape(ex, rpad, 640)
        tick(j * 3 + 1, "F")

        def scores(e):
            q01, q2 = pair(group(j, e, 0)), half(group(j, e, 3), False)
            return mm_nt(q01, group(j, e, 1)), mm_nt(q2, group(j, e, 4))

        nxt = scores(0)
        for e in range(ex):
            s01, s2 = nxt
            if e + 1 < ex:
                nxt = scores(e + 1)
            allowed = kj <= jnp.maximum(qi, PATCHES - 1 + split[c * ex + e])
            ps_h = []
            for h, s in enumerate((s01[:rpad], s01[rpad:], s2)):
                s = jnp.where(allowed, s * (HD ** -0.5), -1e30)
                p = jnp.exp(s - jnp.max(s, axis=-1, keepdims=True))
                p = (p * (1.0 / jnp.sum(p, axis=-1, keepdims=True))).astype(BF16)
                prob[j, e, h] = p
                ps_h.append(p)
            o01 = mm(jnp.concatenate(ps_h[:2], axis=0), group(j, e, 2))
            o2 = mm(ps_h[2], group(j, e, 3))
            mx[j, e, :, :128] = jnp.where(low_half, 0.0, o2).astype(BF16)
            mx[j, e, :, 128:] = jnp.where(low_half, o01[:rpad], o01[rpad:]).astype(BF16)

        tick(j * 3 + 2, "F")
        mid[...] += mm(mx[j].reshape(t, 256), wbf[j, 512:, :]).reshape(ex, rpad, width)

        @pl.when(j == 1)
        def _():
            fill("j", 1)
            coming[7].wait()
            cotp[...] = jnp.zeros_like(cotp)

            @pl.loop(0, ex)
            def _(e):
                cotp[e, :rows, :] = stage[e]

            ta[...] = cotp[...].reshape(t, width).T
            fill("j", 2)
            load_attn(2)

        @pl.when(j == 2)
        def _():
            fill("j", 3)
            c_second(0).wait_recv()
            load_attn(3)

    @pl.loop(0, ex)
    def _(e):
        tick(e, "M")
        keep = lax.broadcasted_iota(jnp.int32, (rpad, 1), 0) < rows
        v = jnp.where(keep, mid[e], 0.0)
        mid[e] = v
        xhat, _ = ln_stats(v)
        n2[e] = (xhat * g2[...][None] + s2[...][None]).astype(BF16)
        br[e] = v
        gn[e] = jnp.zeros((rpad, width), F32)

    tb[...] = n2[...].reshape(t, width).T

    def chunk(b, between=None):
        u, dn = fetched(b), fetched(2 + b)
        pre = mm(n2[...].reshape(t, width), u)
        ga = mm(cotp[...].reshape(t, width), dn)
        phi = 0.5 * (1.0 + lax.erf(pre * (0.5 ** 0.5)))
        act = (pre * phi).astype(BF16)
        gpre = (ga * (phi + pre * jnp.exp(-0.5 * pre * pre) * 0.3989422804014327)).astype(BF16)
        if between is not None:
            between()
        br[...] += mm_nt(act, dn).reshape(ex, rpad, width)
        gn[...] += mm_nt(gpre, u).reshape(ex, rpad, width)
        return act, gpre

    def fetch2(j, i, b):
        fetch(j, 1, i, b)
        fetch(j, 2, i, 2 + b)

    fill("fill", 1)
    c_first(1).wait_recv()
    c_first(2).wait_recv()
    fetch2(1, 0, 0)
    shape5 = po.shape[1:]

    @pl.loop(0, 6)
    def _(n):
        i, b = n // 2, lax.rem(n, 2)

        @pl.when(n < 5)
        def _():
            fetch2(b, (n + 1) // 2, 1 - b)

        act, gpre = chunk(b, lambda: tick(2 * n, "O"))
        gd = mm(ta[...], act).reshape(shape5)
        gu = mm(tb[...], gpre).reshape(shape5)
        slot = 2 * lax.rem(i, 2)

        @pl.when(b == 0)
        def _():
            @pl.when(i == 0)
            def _():
                y_slice(0, 0).wait_send()
                y_slice(0, 1).wait_send()
                y_direct(0).wait_send()
                c_first(0).wait_send()

            @pl.when(i == 2)
            def _():
                c_grad(0, 0).wait_send()
                c_grad(1, 1).wait_send()

            ps[slot] = gd
            ps[slot + 1] = gu
            c_grad(2 * i, slot).start()
            c_grad(2 * i + 1, slot + 1).start()

        @pl.when(b == 1)
        def _():
            po[2 * i] = gd
            po[2 * i + 1] = gu

        tick(2 * n + 1, "O")

    fill("fill", 2)
    fetch2(2, 0, 0)

    @pl.loop(0, 6)
    def _(n):
        b = lax.rem(n, 2)

        @pl.when(n == 2)
        def _():
            fill("n", 2)
            c_second(1).wait_recv()
            c_second(2).wait_recv()

        @pl.when(n < 5)
        def _():
            fetch2(2 + (n + 1) // 3, lax.rem(n + 1, 3), 1 - b)

        chunk(b)
        tick(n, "P")

    o_copy = rcopy(br, outs, osend.at[0], orecv.at[0], sib)
    o_copy.start()
    fill("fill", 3)

    @pl.loop(0, ex)
    def _(e):
        tick(e, "N")
        back, dg, ds = ln_back(mid[e], gn[e], g2[...][None])
        gv[2:3, :] += dg
        gv[3:4, :] += ds
        gm = cotp[e].astype(F32) + back
        mid[e] = gm
        n2[e] = gm.astype(BF16)
        stage[e] = br[e, :rows, :].astype(BF16)
        gn[e] = jnp.zeros((rpad, width), F32)

    fill("fill", 4)
    gml = n2
    ta[...] = gml[...].reshape(t, width).T
    tb[...] = n1[...].reshape(t, width).T
    scale = HD ** -0.5

    mine, theirs = pl.ds(c * ex, ex), pl.ds((1 - c) * ex, ex)
    o_keep = pltpu.make_async_copy(stage, output.at[mine], isem.at[2])
    o_keep.start()
    o_back = pltpu.make_async_copy(outs, br, isem.at[0])
    o_other = pltpu.make_async_copy(stage, output.at[theirs], isem.at[1])

    @pl.loop(0, 4)
    def _(n):
        j = jnp.where(n < 2, 1 - n, n)
        tick(n * 3, "B")
        gmix[...] = mm_nt(gml[...].reshape(t, width), wbf[j, 512:, :]).astype(BF16).reshape(ex, rpad, 256)
        tick(n * 3 + 1, "B")

        def first(e):
            g01, g2_ = pair(gmix[e, :, 128:]), half(gmix[e, :, :128], True)
            return g01, g2_, mm_nt(g01, group(j, e, 2)), mm_nt(g2_, group(j, e, 3))

        nxt = first(0)
        for e in range(ex):
            g01, g2_, d01, d2 = nxt
            if e + 1 < ex:
                nxt = first(e + 1)
            q01 = pair(group(j, e, 0))
            ds = []
            for h, dp in enumerate((d01[:rpad], d01[rpad:], d2)):
                pf = prob[j, e, h].astype(F32)
                pd = pf * dp
                ds.append((pd - pf * jnp.sum(pd, axis=-1, keepdims=True)).astype(BF16))
            s01 = jnp.concatenate(ds[:2], axis=0)
            p01 = jnp.concatenate([prob[j, e, 0], prob[j, e, 1]], axis=0)
            dv01, dv2 = mm_tn(p01, g01), mm_tn(prob[j, e, 2], g2_)
            dq01, dq2 = mm(s01, group(j, e, 1)) * scale, mm(ds[2], group(j, e, 4)) * scale
            dk01, dk2 = mm_tn(s01, q01) * scale, mm_tn(ds[2], group(j, e, 3)) * scale
            gp[e, :, 0:128] = jnp.where(low_half, dq01[:rpad], dq01[rpad:]).astype(BF16)
            gp[e, :, 128:256] = dk01.astype(BF16)
            gp[e, :, 256:384] = dv01.astype(BF16)
            gp[e, :, 384:512] = jnp.where(low_half, dq2, dv2).astype(BF16)
            gp[e, :, 512:640] = jnp.where(low_half, dk2, 0.0).astype(BF16)

        tick(n * 3 + 2, "B")
        gpf = gp[...].reshape(t, 640)

        def grads(write):
            write(0, mm(tb[...], gpf[:, :256]).reshape(shape5))
            write(1, mm(tb[...], gpf[:, 256:512]).reshape(shape5))
            og = mm(ta[...], mx[j].reshape(t, 256))
            k2 = mm(tb[...], gpf[:, 512:640])
            write(2, jnp.concatenate([og[:, :128] + k2, og[:, 128:]], axis=1).reshape(shape5))

        @pl.when(n == 0)
        def _():
            for u in range(2, 6):
                c_grad(u, (0, 1, 2, 3, 0, 1)[u]).wait_send()

            o_copy.wait_recv()

            def write(i, g):
                ps[i] = g
                c_grad(6 + i, i).start()

            grads(write)

        @pl.when(n == 1)
        def _():
            fill("b", 0)

            def write(i, g):
                ust[i] = g

            grads(write)
            fill("b", 1)
            o_copy.wait_send()
            o_back.start()

        gn[...] += mm(gpf, wbf[j, :640, :]).reshape(ex, rpad, width)

        @pl.when(n == 2)
        def _():
            o_back.wait()
            o_keep.wait()

            @pl.loop(0, ex)
            def _(e):
                stage[e] = br[e, :rows, :].astype(BF16)

            o_other.start()

    fill("fill", 5)

    o_other.wait()

    @pl.loop(0, ex)
    def _(e):
        back, dg, ds = ln_back(tok[e].astype(F32), gn[e, :rows, :], g1[...][None])
        gv[0:1, :] += dg
        gv[1:2, :] += ds
        g = mid[e, :rows, :] + back
        br[e, :rows, :] = g
        tok[e] = g.astype(BF16)

    t_copy = rcopy(br, gtoks, osend.at[1], orecv.at[1], sib)
    t_copy.start()
    t_keep = pltpu.make_async_copy(tok, gtok.at[mine], isem.at[2])
    t_keep.start()
    t_back = pltpu.make_async_copy(gtoks, gn, isem.at[0])
    v_copy = rcopy(gv, vcr, osend.at[2], orecv.at[2], sib)
    v_copy.start()
    last = PLAN[("fill", 6)]
    run(last[: len(last) // 2])
    v_copy.wait()
    gv[...] += vcr[...]
    v_sends = []
    for k in range(1, 8):
        cp = rcopy(gv, vr.at[7 - k], vsend.at[k - 1], vrecv.at[7 - k], (lax.rem(d + k, 8), tt))
        cp.start()
        v_sends.append(cp)
    t_copy.wait()
    t_back.start()
    run(last[len(last) // 2 : -1])
    for k in range(1, 8):
        rcopy(gv, vr.at[k - 1], vsend.at[k - 1], vrecv.at[k - 1], sib).wait_recv()
    acc = None
    for i in range(8):
        k = lax.rem(i - d + 8, 8)
        term = jnp.where(k == 0, gv[...], vr[jnp.maximum(k - 1, 0)])
        acc = term if acc is None else acc + term
    mine_v = jnp.zeros(vecs.shape, F32)
    for i in range(8):
        mine_v = jnp.where(d == i, acc[:, i * (width // 8) : (i + 1) * (width // 8)], mine_v)
    vecs[...] = mine_v
    t_back.wait()
    t_keep.wait()

    @pl.loop(0, ex)
    def _(e):
        tok[e] = gn[e, :rows, :].astype(BF16)

    t_other = pltpu.make_async_copy(tok, gtok.at[theirs], isem.at[1])
    t_other.start()
    run(last[-1:])

    for cp in v_sends:
        cp.wait_send()
    for p in range(3):
        c_second(p).wait_send()
        if p:
            y_direct(p).wait_send()
            c_first(p).wait_send()
        for h in range(2):
            if p:
                y_slice(p, h).wait_send()
            for k in range(7):
                hop(p, h, k).wait_send()
    for u in range(9):
        for k in range(3):
            halving(u, k).wait_send()
    for u in range(6, 9):
        c_grad(u, u - 6).wait_send()
    t_other.wait()


def layer(split, tokens, cots, g1, s1, g2, s2, w_qkv, w_out, w_up, w_down):
    batch, rows, width = tokens.shape
    ex = batch // 2
    rpad = -(-rows // 16) * 16
    t = ex * rpad
    band = width // 8
    sds = jax.ShapeDtypeStruct
    dma = pltpu.SemaphoreType.DMA
    vm = pltpu.VMEM
    ANY = pl.BlockSpec(memory_space=pl.ANY)
    VM = pl.BlockSpec(memory_space=pltpu.VMEM)
    SM = pl.BlockSpec(memory_space=pltpu.SMEM)
    act = (ex, rpad, width)
    unit = (2, 2, 2, band, CH)
    return pl.pallas_call(
        layer_kernel,
        out_shape=(
            sds((3, 3) + unit, F32), sds((3, 3, 3) + unit, F32), sds((8, band), F32),
            sds((3, band, 192), F32), sds((192, band), F32), sds((band, 768), F32), sds((band, 768), F32),
            sds(tokens.shape, BF16), sds(tokens.shape, BF16), sds(act, F32), sds(act, F32),
        ),
        in_specs=[SM, ANY, ANY, VM, VM, VM, VM, ANY, ANY, ANY, ANY],
        out_specs=(ANY, ANY, VM, VM, VM, VM, VM, ANY, ANY, ANY, ANY),
        scratch_shapes=[
            vm((ex, rows, width), BF16), vm((ex, rows, width), BF16), vm(act, BF16), vm(act, BF16),
            vm((4, ex, rpad, 640), BF16), vm((4, ex, 3, rpad, rpad), BF16), vm((4, ex, rpad, 256), BF16),
            vm(act, F32), vm(act, F32), vm(act, F32), vm(act, BF16),
            vm((4,) + unit, F32), vm((4, width, 768), BF16),
            vm((width, t), BF16), vm((width, t), BF16), vm((ex, rpad, 640), BF16), vm((ex, rpad, 256), BF16),
            vm((6,) + unit, F32), vm((4,) + unit, F32), vm((6,) + unit, F32),
            vm((9, 2, 2, band, CH), F32), vm((9, 2, band, CH), F32), vm((9, band, CH), F32),
            vm((8, width), F32), vm((8, width), F32), vm((7, 8, width), F32),
            dma((8,)), dma((3, 3)), dma((4,)), dma((6,)), dma((6,)), dma((3, 3)), dma((3, 3)), dma((6, 7)), dma((6, 7)),
            dma((9,)), dma((9,)), dma((9, 3)), dma((9, 3)), dma((3,)), dma((3,)), dma((7,)), dma((7,)),
        ],
        compiler_params=pltpu.CompilerParams(collective_id=0, has_side_effects=True, vmem_limit_bytes=VLIM),
        name="layer",
    )(split, tokens, cots, g1, s1, g2, s2, w_qkv, w_out, w_up, w_down)


VLIM = 64 * 1024 * 1024 - 64 * 1024


def fast_device(tokens, cotangent, split_point, w_qkv, w_out, w_up, w_down, gain_one, shift_one, gain_two, shift_two):
    batch, length, width = tokens.shape
    _, _, vecs, gqkv, gout, gup, gdown, output, gtok, _, _ = layer(
        split_point, tokens, cotangent, gain_one, shift_one, gain_two, shift_two,
        w_qkv.transpose(0, 2, 1), w_out, w_up, w_down,
    )
    return output, gtok, gqkv, gout, gup, gdown.T, vecs[0], vecs[1], vecs[2], vecs[3]


def layer_norm(values, gain_vec, shift_vec):
    row_mean = jnp.mean(values, axis=-1, keepdims=True)
    centered = values - row_mean
    variance = jnp.mean(centered * centered, axis=-1, keepdims=True)
    return centered * lax.rsqrt(variance + EPSILON) * gain_vec + shift_vec


def attention_forward(inputs, allowed, w_qkv, w_out, gain_one, shift_one):
    batch, length, width = inputs.shape
    local = w_qkv.shape[2]
    head_count = local // HD
    normed = layer_norm(inputs, gain_one, shift_one).astype(jnp.bfloat16)
    packed = jnp.einsum("btd,cde->cbte", normed, w_qkv, preferred_element_type=jnp.float32).astype(
        jnp.bfloat16
    )
    queries = packed[0].reshape(batch, length, head_count, HD)
    keys = packed[1].reshape(batch, length, head_count, HD)
    values = packed[2].reshape(batch, length, head_count, HD)
    scores = jnp.einsum(
        "bqhe,bkhe->bhqk", queries, keys, preferred_element_type=jnp.float32
    ) * HD ** (-0.5)
    scores = jnp.where(allowed[:, None], scores, -1e30)
    log_total = jax.nn.logsumexp(scores, axis=-1, keepdims=True)
    attn_probs = jnp.exp(scores - log_total)
    probs_low = attn_probs.astype(jnp.bfloat16)
    mixed = jnp.einsum("bhqk,bkhe->bqhe", probs_low, values, preferred_element_type=jnp.float32)
    mixed = mixed.reshape(batch, length, local).astype(jnp.bfloat16)
    partial_out = jnp.einsum("btk,kd->btd", mixed, w_out, preferred_element_type=jnp.float32)
    return (normed, queries, keys, values, attn_probs, probs_low, mixed, partial_out)


def mlp_forward(middle, w_up, gain_two, shift_two):
    normed_two = layer_norm(middle, gain_two, shift_two).astype(jnp.bfloat16)
    pre_act = jnp.einsum("btd,df->btf", normed_two, w_up, preferred_element_type=jnp.float32)
    activated = jax.nn.gelu(pre_act, approximate=False).astype(jnp.bfloat16)
    return (normed_two, pre_act, activated)


def per_device(
    tokens,
    cotangent,
    split_point,
    w_qkv,
    w_out,
    w_up,
    w_down,
    gain_one,
    shift_one,
    gain_two,
    shift_two,
):
    inputs = tokens.astype(jnp.float32)
    batch, length, width = tokens.shape
    local = w_qkv.shape[2]
    head_count = local // HD
    score_scale = HD ** (-0.5)
    places = jnp.arange(length, dtype=jnp.int32)
    limit = jnp.maximum(places[None, :, None], PATCHES + split_point[:, None, None] - 1)
    allowed = places[None, None, :] <= limit
    normed, queries, keys, values, attn_probs, probs_low, mixed, partial_out = attention_forward(
        inputs, allowed, w_qkv, w_out, gain_one, shift_one
    )
    middle = inputs + lax.psum(partial_out, "tensor")
    normed_two, pre_act, activated = mlp_forward(middle, w_up, gain_two, shift_two)
    branch = jnp.einsum("btf,fd->btd", activated, w_down, preferred_element_type=jnp.float32)
    output = (middle + lax.psum(branch, "tensor")).astype(jnp.bfloat16)
    normed, queries, keys, values, attn_probs, probs_low, mixed, partial_out = attention_forward(
        inputs, allowed, w_qkv, w_out, gain_one, shift_one
    )
    middle = inputs + lax.psum(partial_out, "tensor")
    normed_two, pre_act, activated = mlp_forward(middle, w_up, gain_two, shift_two)
    grad_output = cotangent.astype(jnp.float32)
    grad_act = jnp.einsum("btd,fd->btf", cotangent, w_down, preferred_element_type=jnp.float32)
    gelu_pull = jax.vjp(partial(jax.nn.gelu, approximate=False), pre_act)[1]
    grad_pre = gelu_pull(grad_act)[0].astype(jnp.bfloat16)
    grad_down_local = jnp.einsum(
        "btf,btd->fd", activated, cotangent, preferred_element_type=jnp.float32
    )
    grad_up_local = jnp.einsum(
        "btd,btf->df", normed_two, grad_pre, preferred_element_type=jnp.float32
    )
    grad_normed_two = lax.psum(
        jnp.einsum("btf,df->btd", grad_pre, w_up, preferred_element_type=jnp.float32), "tensor"
    )
    norm_two_pull = jax.vjp(layer_norm, middle, gain_two, shift_two)[1]
    grad_mid_norm, grad_gain_two, grad_shift_two = norm_two_pull(grad_normed_two)
    grad_middle = grad_output + grad_mid_norm
    grad_mid_low = grad_middle.astype(jnp.bfloat16)
    grad_out_local = jnp.einsum(
        "btk,btd->kd", mixed, grad_mid_low, preferred_element_type=jnp.float32
    )
    grad_mix = jnp.einsum("btd,kd->btk", grad_mid_low, w_out, preferred_element_type=jnp.float32)
    grad_mix = grad_mix.astype(jnp.bfloat16).reshape(batch, length, head_count, HD)
    grad_probs = jnp.einsum("bqhe,bkhe->bhqk", grad_mix, values, preferred_element_type=jnp.float32)
    row_terms = jnp.sum(attn_probs * grad_probs, axis=-1, keepdims=True)
    grad_scores = (attn_probs * (grad_probs - row_terms)).astype(jnp.bfloat16)
    grad_query = (
        jnp.einsum("bhqk,bkhe->bqhe", grad_scores, keys, preferred_element_type=jnp.float32)
        * score_scale
    )
    grad_key = (
        jnp.einsum("bhqk,bqhe->bkhe", grad_scores, queries, preferred_element_type=jnp.float32)
        * score_scale
    )
    grad_value = jnp.einsum(
        "bhqk,bqhe->bkhe", probs_low, grad_mix, preferred_element_type=jnp.float32
    )
    grad_packed = (
        jnp.stack([grad_query, grad_key, grad_value])
        .reshape(3, batch, length, local)
        .astype(jnp.bfloat16)
    )
    grad_qkv_local = jnp.einsum(
        "btd,cbte->cde", normed, grad_packed, preferred_element_type=jnp.float32
    )
    grad_normed = lax.psum(
        jnp.einsum("cbte,cde->btd", grad_packed, w_qkv, preferred_element_type=jnp.float32),
        "tensor",
    )
    norm_one_pull = jax.vjp(layer_norm, inputs, gain_one, shift_one)[1]
    grad_in_norm, grad_gain_one, grad_shift_one = norm_one_pull(grad_normed)
    grad_tokens = (grad_middle + grad_in_norm).astype(jnp.bfloat16)
    (
        qkv_part,
        out_part,
        up_part,
        down_part,
        gain_one_part,
        shift_one_part,
        gain_two_part,
        shift_two_part,
    ) = (
        lax.psum_scatter(grad_qkv_local, "dp", scatter_dimension=1, tiled=True),
        lax.psum_scatter(grad_out_local, "dp", scatter_dimension=1, tiled=True),
        lax.psum_scatter(grad_up_local, "dp", scatter_dimension=0, tiled=True),
        lax.psum_scatter(grad_down_local, "dp", scatter_dimension=1, tiled=True),
        lax.psum_scatter(grad_gain_one, "dp", scatter_dimension=0, tiled=True),
        lax.psum_scatter(grad_shift_one, "dp", scatter_dimension=0, tiled=True),
        lax.psum_scatter(grad_gain_two, "dp", scatter_dimension=0, tiled=True),
        lax.psum_scatter(grad_shift_two, "dp", scatter_dimension=0, tiled=True),
    )
    return (
        output,
        grad_tokens,
        qkv_part,
        out_part,
        up_part,
        down_part,
        gain_one_part,
        shift_one_part,
        gain_two_part,
        shift_two_part,
    )


def solution(mesh):
    in_specs = (
        P("dp", None, None),
        P("dp", None, None),
        P("dp"),
        P(None, None, "tensor"),
        P("tensor", None),
        P(None, "tensor"),
        P("tensor", None),
        P(),
        P(),
        P(),
        P(),
    )
    out_specs = (
        P("dp", None, None),
        P("dp", None, None),
        P(None, "dp", "tensor"),
        P("tensor", "dp"),
        P("dp", "tensor"),
        P("tensor", "dp"),
        P("dp"),
        P("dp"),
        P("dp"),
        P("dp"),
    )
    fast = mesh.shape["dp"] == 8 and mesh.shape["tensor"] == 4
    return jax.shard_map(
        fast_device if fast else per_device, mesh=mesh, in_specs=in_specs, out_specs=out_specs, check_vma=False
    )
```

```python
from functools import partial

import jax
import jax.numpy as jnp
from jax import lax
from jax.experimental import pallas as pl
from jax.experimental.pallas import tpu as pltpu
from jax.sharding import PartitionSpec as P

HD = 64
PATCHES = 196
EPSILON = 1e-05
MESH = pl.DeviceIdType.MESH
F32 = jnp.float32
BF16 = jnp.bfloat16
CH = 256


def mm(a, b):
    return jnp.dot(a, b, preferred_element_type=F32)


def mm_nt(a, b):
    return lax.dot_general(a, b, (((1,), (1,)), ((), ())), preferred_element_type=F32)


def mm_tn(a, b):
    return lax.dot_general(a, b, (((0,), (0,)), ((), ())), preferred_element_type=F32)


def ln_stats(v):
    mean = jnp.mean(v, axis=-1, keepdims=True)
    cen = v - mean
    var = jnp.mean(cen * cen, axis=-1, keepdims=True)
    rstd = lax.rsqrt(var + EPSILON)
    return cen * rstd, rstd


def ln_back(v, gy, gain):
    xhat, rstd = ln_stats(v)
    gx = gy * gain
    m1 = jnp.mean(gx, axis=-1, keepdims=True)
    m2 = jnp.mean(gx * xhat, axis=-1, keepdims=True)
    return rstd * (gx - m1 - xhat * m2), jnp.sum(gy * xhat, axis=0, keepdims=True), jnp.sum(gy, axis=0, keepdims=True)


def rcopy(src, dst, ssem, rsem, dev):
    return pltpu.make_async_remote_copy(
        src_ref=src, dst_ref=dst, send_sem=ssem, recv_sem=rsem, device_id=dev, device_id_type=MESH
    )


ZFIRST = (True, True, False, True, False, False, False, False, False)

PLAN = {
    ("start", 0): (("c", 0, 0, 0), ("s", 0, 0, 0), ("s", 0, 1, 0)),
    ("L", 0): (("d", 0, 0, 0),),
    ("own", 0): (("c", 1, 0, 0), ("c", 2, 0, 0)),
    ("j", 0): (("g", 0, 0, 1),),
    ("F", 3): (("g", 0, 1, 1),),
    ("F", 4): (("g", 0, 0, 2),),
    ("j", 2): (("s", 1, 0, 0), ("g", 0, 1, 2), ("g", 0, 0, 3), ("s", 1, 1, 0), ("g", 0, 1, 3), ("s", 2, 1, 0),
        ("g", 1, 0, 1), ("s", 2, 0, 0), ("g", 0, 0, 4), ("g", 1, 1, 1), ("d", 1, 0, 0), ("g", 0, 1, 4),
        ("w", 0, 0, 0)),
    ("F", 6): (("g", 1, 0, 2),),
    ("F", 7): (("g", 2, 1, 1), ("g", 2, 0, 1)),
    ("F", 10): (("g", 1, 1, 2),),
    ("O", 1): (("g", 1, 0, 3),),
    ("O", 2): (("d", 2, 0, 0), ("g", 2, 1, 2), ("g", 2, 0, 2)),
    ("O", 3): (("g", 1, 1, 3),),
    ("O", 4): (("r", 0, 0, 1),),
    ("O", 6): (("g", 1, 0, 4),),
    ("O", 7): (("g", 2, 1, 3), ("g", 2, 0, 3)),
    ("O", 9): (("r", 1, 0, 1),),
    ("O", 11): (("r", 2, 0, 1),),
    ("fill", 2): (("g", 1, 1, 4), ("w", 1, 0, 0), ("r", 0, 0, 2), ("g", 2, 1, 4), ("g", 2, 0, 4), ("w", 2, 0, 0)),
    ("P", 1): (("r", 5, 0, 1), ("r", 3, 0, 1)),
    ("P", 3): (("r", 0, 0, 3), ("r", 2, 0, 2)),
    ("P", 4): (("r", 1, 0, 2),),
    ("P", 5): (("r", 4, 0, 1),),
    ("N", 2): (("r", 0, 0, 4),),
    ("B", 3): (("r", 5, 0, 2), ("r", 2, 0, 3)),
    ("B", 5): (("r", 4, 0, 2), ("r", 1, 0, 3)),
    ("b", 1): (("r", 7, 0, 1), ("r", 3, 0, 2)),
    ("B", 7): (("r", 1, 0, 4),),
    ("B", 8): (("r", 2, 0, 4),),
    ("B", 9): (("r", 8, 0, 1),),
    ("B", 11): (("r", 5, 0, 3),),
    ("fill", 6): (("r", 4, 0, 3), ("r", 7, 0, 2), ("r", 6, 0, 1), ("r", 3, 0, 3), ("r", 5, 0, 4), ("r", 4, 0, 4),
        ("r", 7, 0, 3), ("r", 3, 0, 4), ("r", 8, 0, 2), ("r", 7, 0, 4), ("r", 6, 0, 2), ("r", 8, 0, 3),
        ("r", 8, 0, 4), ("r", 6, 0, 3), ("r", 6, 0, 4)),
}


def layer_kernel(
    split, tokens, cots, g1, s1, g2, s2, w_qkv, w_out, w_up, w_down,
    own, wf, vecs, gqkv, gout, gffn, results, outs, gtoks,
    tok, stage, cotp, n1, qkv, prob, mx, mid, br, gn, n2, ust, wbf, ta, tb, gp, gmix,
    po, ps, cr, ra, rb, rc, gv, vcr, vr,
    isem, ksem, wsem, csend, crecv, ysend, yrecv, dsend, drecv, rcs, rcr, rsend, rrecv, osend, orecv, vsend, vrecv,
):
    ex, rows, width = tok.shape
    output, gtok = results.at[0], results.at[1]
    gup, gdown = gffn.at[0], gffn.at[1]
    rpad = n1.shape[1]
    t = ex * rpad
    d, tt = lax.axis_index("dp"), lax.axis_index("tensor")
    zh, zl, x = d // 4, lax.rem(d // 2, 2), lax.rem(d, 2)
    y, c = tt // 2, lax.rem(tt, 2)
    sib = (d, y * 2 + 1 - c)
    ynb = (d, (1 - y) * 2 + c)

    def dpi(fh, fl, fx):
        return ((1 - zh) if fh else zh) * 4 + ((1 - zl) if fl else zl) * 2 + ((1 - x) if fx else x)

    def at(fh, fl, fx):
        return ((1 - zh) if fh else zh, (1 - zl) if fl else zl, (1 - x) if fx else x)

    znb2, znb1, xnb = (dpi(1, 0, 0), tt), (dpi(0, 1, 0), tt), (dpi(0, 0, 1), tt)

    coming = [
        pltpu.make_async_copy(w_qkv.at[i], wbf.at[1, pl.ds(192 * i, 192)], isem.at[i]) for i in range(3)
    ] + [
        pltpu.make_async_copy(w_out, wbf.at[1, pl.ds(576, 192)], isem.at[3]),
        pltpu.make_async_copy(w_up, wbf.at[2], isem.at[4]),
        pltpu.make_async_copy(w_down, wbf.at[3], isem.at[5]),
        pltpu.make_async_copy(tokens.at[pl.ds(c * ex, ex)], tok, isem.at[6]),
        pltpu.make_async_copy(cots.at[pl.ds(c * ex, ex)], stage, isem.at[7]),
    ]
    for cp in coming[:4]:
        cp.start()

    peers = [sib, ynb] + [(lax.rem(d + k, 8), tt) for k in range(1, 8)]
    barrier = pltpu.get_barrier_semaphore()
    for p in peers:
        pl.semaphore_signal(barrier, 1, device_id=p, device_id_type=MESH)

    def y_slice(p, h):
        blk = (p, h) + at(0, 0, 0)
        src = own.at[blk] if p else ps.at[(h,) + at(0, 0, 0)]
        return rcopy(src, wf.at[(1,) + blk], ysend.at[p, h], yrecv.at[p, h], ynb)

    def y_direct(p):
        return rcopy(own.at[p, 2] if p else ps.at[2], wf.at[1, p, 2], ysend.at[p, 2], yrecv.at[p, 2], ynb)

    def c_first(p):
        return rcopy(own.at[p] if p else ps.at[pl.ds(0, 3)], wf.at[0, p], csend.at[p], crecv.at[p], sib)

    def c_second(p):
        return rcopy(wf.at[1, p], wf.at[2, p], csend.at[3 + p], crecv.at[3 + p], sib)

    hops = (
        (at(0, 0, 0), at(1, 0, 0), znb2),
        (at(0, 0, 0), at(0, 1, 0), znb1),
        (at(1, 0, 0), at(1, 1, 0), znb1),
        (at(0, 0, 0), at(0, 0, 1), xnb),
        (at(1, 0, 0), at(1, 0, 1), xnb),
        (at(0, 1, 0), at(0, 1, 1), xnb),
        (at(1, 1, 0), at(1, 1, 1), xnb),
    )

    def hop(p, h, k, arriving=False):
        blk = wf.at[(1, p, h) + (hops[k][1] if arriving else hops[k][0])]
        return rcopy(blk, blk, dsend.at[2 * p + h, k], drecv.at[2 * p + h, k], hops[k][2])

    def g_step(p, h, stage):
        if stage == 1:
            y_slice(p, h).wait_recv()
            go = (0, 1, 3)
        elif stage == 2:
            hop(p, h, 0, True).wait_recv()
            hop(p, h, 1, True).wait_recv()
            go = (2, 4, 5)
        elif stage == 3:
            hop(p, h, 2, True).wait_recv()
            go = (6,)
        else:
            for k in (3, 4, 5, 6):
                hop(p, h, k, True).wait_recv()
            go = ()
        for k in go:
            hop(p, h, k).start()

    def fetch(j, p, i, b):
        @pl.when(j == 0)
        def _():
            pltpu.make_async_copy(own.at[p, i], ust.at[b], wsem.at[b]).start()

        @pl.when(j > 0)
        def _():
            pltpu.make_async_copy(wf.at[jnp.maximum(j - 1, 0), p, i], ust.at[b], wsem.at[b]).start()

    def fetched(b):
        pltpu.make_async_copy(ust.at[b], ust.at[b], wsem.at[b]).wait()
        return ust[b].reshape(width, CH).astype(BF16)

    def load_attn(j):
        for i in range(3):
            fetch(j, 0, i, i)

    def take_attn(j):
        for i in range(3):
            wbf[j, :, i * CH : (i + 1) * CH] = fetched(i)

    def c_grad(u, slot):
        return rcopy(ps.at[slot], cr.at[u % 6], rcs.at[u], rcr.at[u], sib)

    def place_of(u):
        return (po, u) if u < 6 else (ust, u - 6)

    def views(pu, zfirst):
        if zfirst:
            return (
                ((pu, slice(None), 1 - zl), (pu, slice(None), zl), znb1),
                ((pu, 1 - zh, zl), (pu, zh, zl), znb2),
                ((pu, zh, zl, 1 - x), (pu, zh, zl, x), xnb),
            )
        return (
            ((pu, slice(None), slice(None), 1 - x), (pu, slice(None), slice(None), x), xnb),
            ((pu, slice(None), 1 - zl, x), (pu, slice(None), zl, x), znb1),
            ((pu, 1 - zh, zl, x), (pu, zh, zl, x), znb2),
        )

    def halving(u, k):
        ref, pu = place_of(u)
        away, _, to = views(pu, ZFIRST[u])[k]
        return rcopy(ref.at[away], (ra, rb, rc)[k].at[u], rsend.at[u, k], rrecv.at[u, k], to)

    def r_step(u, stage):
        ref, pu = place_of(u)
        view = views(pu, ZFIRST[u])
        if stage == 1:
            c_grad(u, 0).wait_recv()
            away, keep = view[0][0], view[0][1]
            ref[away] += cr[(u % 6,) + away[1:]]
            halving(u, 0).start()
            ref[keep] += cr[(u % 6,) + keep[1:]]
        elif stage < 4:
            k = stage - 2
            halving(u, k).wait_recv()
            ref[view[k][1]] += (ra, rb)[k][u]
            halving(u, k + 1).start()
        else:
            halving(u, 2).wait_recv()
            hand_out(u, ref[view[2][1]] + rc[u])

    def hand_out(u, g):
        if u < 6:
            cols = slice(u // 2 * CH, (u // 2 + 1) * CH)
            if u % 2:
                gup[:, cols] = g
            else:
                gdown[:, cols] = g
        elif u == 6:
            gqkv[0, :, :128] = g[:, :128]
            gqkv[1, :, :128] = g[:, 128:]
        elif u == 7:
            gqkv[2, :, :128] = g[:, :128]
            gqkv[0, :, 128:] = g[:, 128 : 128 + HD]
            gqkv[2, :, 128:] = g[:, 128 + HD :]
        else:
            gqkv[1, :, 128:] = g[:, :HD]
            turned = g.T
            gout[128:, :] = turned[HD:128]
            gout[:128, :] = turned[128:]

    def run(steps):
        for what, a, b, stage in steps:
            if what == "g":
                g_step(a, b, stage)
            elif what == "s":
                y_slice(a, b).start()
            elif what == "d":
                y_direct(a).start()
            elif what == "c":
                c_first(a).start()
            elif what == "w":
                y_direct(a).wait_recv()
                c_second(a).start()
            else:
                r_step(a, stage)

    def tick(at, where):
        for (name, when), steps in PLAN.items():
            if name == where:
                @pl.when(at == when)
                def _(steps=steps):
                    run(steps)

    def fill(where, at):
        run(PLAN.get((where, at), ()))

    for cp in coming[:4]:
        cp.wait()
    q_, k_, v_, o_ = 0, 192, 384, 576
    row = 0
    for src, n in (
        (q_, 128), (k_, 128), (v_, 128), (q_ + 128, HD), (v_ + 128, HD), (k_ + 128, HD), (o_ + 128, HD), (o_, 128),
    ):
        wbf[0, row : row + n, :] = wbf[1, src : src + n, :]
        row += n
    unit = ust.shape[1:]

    def keep_own(p, h, v, ref, slot):
        ref[slot] = v.astype(F32).reshape(unit)
        cp = pltpu.make_async_copy(ref.at[slot], own.at[p, h], ksem.at[p, h])
        cp.start()
        return cp

    for h in range(3):
        ps[h] = wbf[0, :, h * CH : (h + 1) * CH].astype(F32).reshape(unit)
    pl.semaphore_wait(barrier, len(peers))
    fill("start", 0)
    for cp in coming[4:]:
        cp.start()
    coming[4].wait()
    kept = [keep_own(1, h, wbf[2, :, h * CH : (h + 1) * CH], po, h) for h in range(3)]
    coming[5].wait()
    kept += [keep_own(2, h, wbf[3, h * CH : (h + 1) * CH, :].T, po, 3 + h) for h in range(3)]
    coming[6].wait()
    n1[...] = jnp.zeros_like(n1)
    mid[...] = jnp.zeros_like(mid)
    gv[...] = jnp.zeros_like(gv)

    @pl.loop(0, ex)
    def _(e):
        tick(e, "L")
        v = tok[e].astype(F32)
        xhat, _ = ln_stats(v)
        n1[e, :rows, :] = (xhat * g1[...][None] + s1[...][None]).astype(BF16)
        mid[e, :rows, :] = v

    for cp in kept:
        cp.wait()
    fill("own", 0)

    low_half = lax.broadcasted_iota(jnp.int32, (rpad, 128), 1) < HD
    qi = lax.broadcasted_iota(jnp.int32, (rpad, rpad), 0)
    kj = lax.broadcasted_iota(jnp.int32, (rpad, rpad), 1)

    def group(j, e, i):
        return qkv[j, e, :, i * 128 : (i + 1) * 128]

    def half(v, high):
        return jnp.where(low_half != high, v, jnp.zeros_like(v))

    def pair(v):
        return jnp.concatenate([half(v, False), half(v, True)], axis=0)

    @pl.loop(0, 4)
    def _(j):
        @pl.when(j > 0)
        def _():
            take_attn(j)

        @pl.when(j == 0)
        def _():
            fill("j", 0)
            c_first(0).wait_recv()
            load_attn(1)

        tick(j * 3, "F")
        qkv[j] = mm_nt(n1[...].reshape(t, width), wbf[j, :640, :]).astype(BF16).reshape(ex, rpad, 640)
        tick(j * 3 + 1, "F")

        def scores(e):
            q01, q2 = pair(group(j, e, 0)), half(group(j, e, 3), False)
            return mm_nt(q01, group(j, e, 1)), mm_nt(q2, group(j, e, 4))

        nxt = scores(0)
        for e in range(ex):
            s01, s2 = nxt
            if e + 1 < ex:
                nxt = scores(e + 1)
            allowed = kj <= jnp.maximum(qi, PATCHES - 1 + split[c * ex + e])
            ps_h = []
            for h, s in enumerate((s01[:rpad], s01[rpad:], s2)):
                s = jnp.where(allowed, s * (HD ** -0.5), -1e30)
                p = jnp.exp(s - jnp.max(s, axis=-1, keepdims=True))
                p = (p * (1.0 / jnp.sum(p, axis=-1, keepdims=True))).astype(BF16)
                prob[j, e, h] = p
                ps_h.append(p)
            o01 = mm(jnp.concatenate(ps_h[:2], axis=0), group(j, e, 2))
            o2 = mm(ps_h[2], group(j, e, 3))
            mx[j, e, :, :128] = jnp.where(low_half, 0.0, o2).astype(BF16)
            mx[j, e, :, 128:] = jnp.where(low_half, o01[:rpad], o01[rpad:]).astype(BF16)

        tick(j * 3 + 2, "F")
        mid[...] += mm(mx[j].reshape(t, 256), wbf[j, 512:, :]).reshape(ex, rpad, width)

        @pl.when(j == 1)
        def _():
            fill("j", 1)
            coming[7].wait()
            cotp[...] = jnp.zeros_like(cotp)

            @pl.loop(0, ex)
            def _(e):
                cotp[e, :rows, :] = stage[e]

            ta[...] = cotp[...].reshape(t, width).T
            fill("j", 2)
            load_attn(2)

        @pl.when(j == 2)
        def _():
            fill("j", 3)
            c_second(0).wait_recv()
            load_attn(3)

    @pl.loop(0, ex)
    def _(e):
        tick(e, "M")
        keep = lax.broadcasted_iota(jnp.int32, (rpad, 1), 0) < rows
        v = jnp.where(keep, mid[e], 0.0)
        mid[e] = v
        xhat, _ = ln_stats(v)
        n2[e] = (xhat * g2[...][None] + s2[...][None]).astype(BF16)
        br[e] = v
        gn[e] = jnp.zeros((rpad, width), F32)

    tb[...] = n2[...].reshape(t, width).T

    def chunk(b, between=None):
        u, dn = fetched(b), fetched(2 + b)
        pre = mm(n2[...].reshape(t, width), u)
        ga = mm(cotp[...].reshape(t, width), dn)
        phi = 0.5 * (1.0 + lax.erf(pre * (0.5 ** 0.5)))
        act = (pre * phi).astype(BF16)
        gpre = (ga * (phi + pre * jnp.exp(-0.5 * pre * pre) * 0.3989422804014327)).astype(BF16)
        if between is not None:
            between()
        br[...] += mm_nt(act, dn).reshape(ex, rpad, width)
        gn[...] += mm_nt(gpre, u).reshape(ex, rpad, width)
        return act, gpre

    def fetch2(j, i, b):
        fetch(j, 1, i, b)
        fetch(j, 2, i, 2 + b)

    fill("fill", 1)
    c_first(1).wait_recv()
    c_first(2).wait_recv()
    fetch2(1, 0, 0)
    shape5 = po.shape[1:]

    @pl.loop(0, 6)
    def _(n):
        i, b = n // 2, lax.rem(n, 2)

        @pl.when(n < 5)
        def _():
            fetch2(b, (n + 1) // 2, 1 - b)

        act, gpre = chunk(b, lambda: tick(2 * n, "O"))
        gd = mm(ta[...], act).reshape(shape5)
        gu = mm(tb[...], gpre).reshape(shape5)
        slot = 2 * lax.rem(i, 2)

        @pl.when(b == 0)
        def _():
            @pl.when(i == 0)
            def _():
                y_slice(0, 0).wait_send()
                y_slice(0, 1).wait_send()
                y_direct(0).wait_send()
                c_first(0).wait_send()

            @pl.when(i == 2)
            def _():
                c_grad(0, 0).wait_send()
                c_grad(1, 1).wait_send()

            ps[slot] = gd
            ps[slot + 1] = gu
            c_grad(2 * i, slot).start()
            c_grad(2 * i + 1, slot + 1).start()

        @pl.when(b == 1)
        def _():
            po[2 * i] = gd
            po[2 * i + 1] = gu

        tick(2 * n + 1, "O")

    fill("fill", 2)
    fetch2(2, 0, 0)

    @pl.loop(0, 6)
    def _(n):
        b = lax.rem(n, 2)

        @pl.when(n == 2)
        def _():
            fill("n", 2)
            c_second(1).wait_recv()
            c_second(2).wait_recv()

        @pl.when(n < 5)
        def _():
            fetch2(2 + (n + 1) // 3, lax.rem(n + 1, 3), 1 - b)

        chunk(b)
        tick(n, "P")

    o_copy = rcopy(br, outs, osend.at[0], orecv.at[0], sib)
    o_copy.start()
    fill("fill", 3)

    @pl.loop(0, ex)
    def _(e):
        tick(e, "N")
        back, dg, ds = ln_back(mid[e], gn[e], g2[...][None])
        gv[2:3, :] += dg
        gv[3:4, :] += ds
        gm = cotp[e].astype(F32) + back
        mid[e] = gm
        n2[e] = gm.astype(BF16)
        stage[e] = br[e, :rows, :].astype(BF16)
        gn[e] = jnp.zeros((rpad, width), F32)

    fill("fill", 4)
    gml = n2
    ta[...] = gml[...].reshape(t, width).T
    tb[...] = n1[...].reshape(t, width).T
    scale = HD ** -0.5

    mine, theirs = pl.ds(c * ex, ex), pl.ds((1 - c) * ex, ex)
    o_keep = pltpu.make_async_copy(stage, output.at[mine], isem.at[2])
    o_keep.start()
    o_back = pltpu.make_async_copy(outs, br, isem.at[0])
    o_other = pltpu.make_async_copy(stage, output.at[theirs], isem.at[1])

    @pl.loop(0, 4)
    def _(n):
        j = jnp.where(n < 2, 1 - n, n)
        tick(n * 3, "B")
        gmix[...] = mm_nt(gml[...].reshape(t, width), wbf[j, 512:, :]).astype(BF16).reshape(ex, rpad, 256)
        tick(n * 3 + 1, "B")

        def first(e):
            g01, g2_ = pair(gmix[e, :, 128:]), half(gmix[e, :, :128], True)
            return g01, g2_, mm_nt(g01, group(j, e, 2)), mm_nt(g2_, group(j, e, 3))

        nxt = first(0)
        for e in range(ex):
            g01, g2_, d01, d2 = nxt
            if e + 1 < ex:
                nxt = first(e + 1)
            q01 = pair(group(j, e, 0))
            ds = []
            for h, dp in enumerate((d01[:rpad], d01[rpad:], d2)):
                pf = prob[j, e, h].astype(F32)
                pd = pf * dp
                ds.append((pd - pf * jnp.sum(pd, axis=-1, keepdims=True)).astype(BF16))
            s01 = jnp.concatenate(ds[:2], axis=0)
            p01 = jnp.concatenate([prob[j, e, 0], prob[j, e, 1]], axis=0)
            dv01, dv2 = mm_tn(p01, g01), mm_tn(prob[j, e, 2], g2_)
            dq01, dq2 = mm(s01, group(j, e, 1)) * scale, mm(ds[2], group(j, e, 4)) * scale
            dk01, dk2 = mm_tn(s01, q01) * scale, mm_tn(ds[2], group(j, e, 3)) * scale
            gp[e, :, 0:128] = jnp.where(low_half, dq01[:rpad], dq01[rpad:]).astype(BF16)
            gp[e, :, 128:256] = dk01.astype(BF16)
            gp[e, :, 256:384] = dv01.astype(BF16)
            gp[e, :, 384:512] = jnp.where(low_half, dq2, dv2).astype(BF16)
            gp[e, :, 512:640] = jnp.where(low_half, dk2, 0.0).astype(BF16)

        tick(n * 3 + 2, "B")
        gpf = gp[...].reshape(t, 640)

        def grads(write):
            write(0, mm(tb[...], gpf[:, :256]).reshape(shape5))
            write(1, mm(tb[...], gpf[:, 256:512]).reshape(shape5))
            og = mm(ta[...], mx[j].reshape(t, 256))
            k2 = mm(tb[...], gpf[:, 512:640])
            write(2, jnp.concatenate([og[:, :128] + k2, og[:, 128:]], axis=1).reshape(shape5))

        @pl.when(n == 0)
        def _():
            for u in range(2, 6):
                c_grad(u, (0, 1, 2, 3, 0, 1)[u]).wait_send()

            o_copy.wait_recv()

            def write(i, g):
                ps[i] = g
                c_grad(6 + i, i).start()

            grads(write)

        @pl.when(n == 1)
        def _():
            fill("b", 0)

            def write(i, g):
                ust[i] = g

            grads(write)
            fill("b", 1)
            o_copy.wait_send()
            o_back.start()

        gn[...] += mm(gpf, wbf[j, :640, :]).reshape(ex, rpad, width)

        @pl.when(n == 2)
        def _():
            o_back.wait()
            o_keep.wait()

            @pl.loop(0, ex)
            def _(e):
                stage[e] = br[e, :rows, :].astype(BF16)

            o_other.start()

    fill("fill", 5)

    o_other.wait()

    @pl.loop(0, ex)
    def _(e):
        back, dg, ds = ln_back(tok[e].astype(F32), gn[e, :rows, :], g1[...][None])
        gv[0:1, :] += dg
        gv[1:2, :] += ds
        g = mid[e, :rows, :] + back
        br[e, :rows, :] = g
        tok[e] = g.astype(BF16)

    t_copy = rcopy(br, gtoks, osend.at[1], orecv.at[1], sib)
    t_copy.start()
    t_keep = pltpu.make_async_copy(tok, gtok.at[mine], isem.at[2])
    t_keep.start()
    t_back = pltpu.make_async_copy(gtoks, gn, isem.at[0])
    v_copy = rcopy(gv, vcr, osend.at[2], orecv.at[2], sib)
    v_copy.start()
    last = PLAN[("fill", 6)]
    run(last[: len(last) // 2])
    v_copy.wait()
    gv[...] += vcr[...]
    v_sends = []
    for k in range(1, 8):
        cp = rcopy(gv, vr.at[7 - k], vsend.at[k - 1], vrecv.at[7 - k], (lax.rem(d + k, 8), tt))
        cp.start()
        v_sends.append(cp)
    t_copy.wait()
    t_back.start()
    run(last[len(last) // 2 : -1])
    for k in range(1, 8):
        rcopy(gv, vr.at[k - 1], vsend.at[k - 1], vrecv.at[k - 1], sib).wait_recv()
    acc = None
    for i in range(8):
        k = lax.rem(i - d + 8, 8)
        term = jnp.where(k == 0, gv[...], vr[jnp.maximum(k - 1, 0)])
        acc = term if acc is None else acc + term
    mine_v = jnp.zeros(vecs.shape, F32)
    for i in range(8):
        mine_v = jnp.where(d == i, acc[:, i * (width // 8) : (i + 1) * (width // 8)], mine_v)
    vecs[...] = mine_v
    t_back.wait()
    t_keep.wait()

    @pl.loop(0, ex)
    def _(e):
        tok[e] = gn[e, :rows, :].astype(BF16)

    t_other = pltpu.make_async_copy(tok, gtok.at[theirs], isem.at[1])
    t_other.start()
    run(last[-1:])

    for cp in v_sends:
        cp.wait_send()
    for p in range(3):
        c_second(p).wait_send()
        if p:
            y_direct(p).wait_send()
            c_first(p).wait_send()
        for h in range(2):
            if p:
                y_slice(p, h).wait_send()
            for k in range(7):
                hop(p, h, k).wait_send()
    for u in range(9):
        for k in range(3):
            halving(u, k).wait_send()
    for u in range(6, 9):
        c_grad(u, u - 6).wait_send()
    t_other.wait()


def layer(split, tokens, cots, g1, s1, g2, s2, w_qkv, w_out, w_up, w_down):
    batch, rows, width = tokens.shape
    ex = batch // 2
    rpad = -(-rows // 16) * 16
    t = ex * rpad
    band = width // 8
    sds = jax.ShapeDtypeStruct
    dma = pltpu.SemaphoreType.DMA
    vm = pltpu.VMEM
    ANY = pl.BlockSpec(memory_space=pl.ANY)
    VM = pl.BlockSpec(memory_space=pltpu.VMEM)
    SM = pl.BlockSpec(memory_space=pltpu.SMEM)
    act = (ex, rpad, width)
    unit = (2, 2, 2, band, CH)
    return pl.pallas_call(
        layer_kernel,
        out_shape=(
            sds((3, 3) + unit, F32), sds((3, 3, 3) + unit, F32), sds((8, band), F32),
            sds((3, band, 192), F32), sds((192, band), F32), sds((2, band, 768), F32),
            sds((2,) + tokens.shape, BF16), sds(act, F32), sds(act, F32),
        ),
        in_specs=[SM, ANY, ANY, VM, VM, VM, VM, ANY, ANY, ANY, ANY],
        out_specs=(ANY, ANY, VM, VM, VM, VM, ANY, ANY, ANY),
        scratch_shapes=[
            vm((ex, rows, width), BF16), vm((ex, rows, width), BF16), vm(act, BF16), vm(act, BF16),
            vm((4, ex, rpad, 640), BF16), vm((4, ex, 3, rpad, rpad), BF16), vm((4, ex, rpad, 256), BF16),
            vm(act, F32), vm(act, F32), vm(act, F32), vm(act, BF16),
            vm((4,) + unit, F32), vm((4, width, 768), BF16),
            vm((width, t), BF16), vm((width, t), BF16), vm((ex, rpad, 640), BF16), vm((ex, rpad, 256), BF16),
            vm((6,) + unit, F32), vm((4,) + unit, F32), vm((6,) + unit, F32),
            vm((9, 2, 2, band, CH), F32), vm((9, 2, band, CH), F32), vm((9, band, CH), F32),
            vm((8, width), F32), vm((8, width), F32), vm((7, 8, width), F32),
            dma((8,)), dma((3, 3)), dma((4,)), dma((6,)), dma((6,)), dma((3, 3)), dma((3, 3)), dma((6, 7)), dma((6, 7)),
            dma((9,)), dma((9,)), dma((9, 3)), dma((9, 3)), dma((3,)), dma((3,)), dma((7,)), dma((7,)),
        ],
        compiler_params=pltpu.CompilerParams(collective_id=0, has_side_effects=True, vmem_limit_bytes=VLIM),
        name="layer",
    )(split, tokens, cots, g1, s1, g2, s2, w_qkv, w_out, w_up, w_down)


VLIM = 64 * 1024 * 1024 - 64 * 1024


def fast_device(tokens, cotangent, split_point, w_qkv, w_out, w_up, w_down, gain_one, shift_one, gain_two, shift_two):
    batch, length, width = tokens.shape
    _, _, vecs, gqkv, gout, gffn, results, _, _ = layer(
        split_point, tokens, cotangent, gain_one, shift_one, gain_two, shift_two,
        w_qkv.transpose(0, 2, 1), w_out, w_up, w_down,
    )
    return results[0], results[1], gqkv, gout, gffn[0], gffn[1].T, vecs[0], vecs[1], vecs[2], vecs[3]


def layer_norm(values, gain_vec, shift_vec):
    row_mean = jnp.mean(values, axis=-1, keepdims=True)
    centered = values - row_mean
    variance = jnp.mean(centered * centered, axis=-1, keepdims=True)
    return centered * lax.rsqrt(variance + EPSILON) * gain_vec + shift_vec


def attention_forward(inputs, allowed, w_qkv, w_out, gain_one, shift_one):
    batch, length, width = inputs.shape
    local = w_qkv.shape[2]
    head_count = local // HD
    normed = layer_norm(inputs, gain_one, shift_one).astype(jnp.bfloat16)
    packed = jnp.einsum("btd,cde->cbte", normed, w_qkv, preferred_element_type=jnp.float32).astype(
        jnp.bfloat16
    )
    queries = packed[0].reshape(batch, length, head_count, HD)
    keys = packed[1].reshape(batch, length, head_count, HD)
    values = packed[2].reshape(batch, length, head_count, HD)
    scores = jnp.einsum(
        "bqhe,bkhe->bhqk", queries, keys, preferred_element_type=jnp.float32
    ) * HD ** (-0.5)
    scores = jnp.where(allowed[:, None], scores, -1e30)
    log_total = jax.nn.logsumexp(scores, axis=-1, keepdims=True)
    attn_probs = jnp.exp(scores - log_total)
    probs_low = attn_probs.astype(jnp.bfloat16)
    mixed = jnp.einsum("bhqk,bkhe->bqhe", probs_low, values, preferred_element_type=jnp.float32)
    mixed = mixed.reshape(batch, length, local).astype(jnp.bfloat16)
    partial_out = jnp.einsum("btk,kd->btd", mixed, w_out, preferred_element_type=jnp.float32)
    return (normed, queries, keys, values, attn_probs, probs_low, mixed, partial_out)


def mlp_forward(middle, w_up, gain_two, shift_two):
    normed_two = layer_norm(middle, gain_two, shift_two).astype(jnp.bfloat16)
    pre_act = jnp.einsum("btd,df->btf", normed_two, w_up, preferred_element_type=jnp.float32)
    activated = jax.nn.gelu(pre_act, approximate=False).astype(jnp.bfloat16)
    return (normed_two, pre_act, activated)


def per_device(
    tokens,
    cotangent,
    split_point,
    w_qkv,
    w_out,
    w_up,
    w_down,
    gain_one,
    shift_one,
    gain_two,
    shift_two,
):
    inputs = tokens.astype(jnp.float32)
    batch, length, width = tokens.shape
    local = w_qkv.shape[2]
    head_count = local // HD
    score_scale = HD ** (-0.5)
    places = jnp.arange(length, dtype=jnp.int32)
    limit = jnp.maximum(places[None, :, None], PATCHES + split_point[:, None, None] - 1)
    allowed = places[None, None, :] <= limit
    normed, queries, keys, values, attn_probs, probs_low, mixed, partial_out = attention_forward(
        inputs, allowed, w_qkv, w_out, gain_one, shift_one
    )
    middle = inputs + lax.psum(partial_out, "tensor")
    normed_two, pre_act, activated = mlp_forward(middle, w_up, gain_two, shift_two)
    branch = jnp.einsum("btf,fd->btd", activated, w_down, preferred_element_type=jnp.float32)
    output = (middle + lax.psum(branch, "tensor")).astype(jnp.bfloat16)
    normed, queries, keys, values, attn_probs, probs_low, mixed, partial_out = attention_forward(
        inputs, allowed, w_qkv, w_out, gain_one, shift_one
    )
    middle = inputs + lax.psum(partial_out, "tensor")
    normed_two, pre_act, activated = mlp_forward(middle, w_up, gain_two, shift_two)
    grad_output = cotangent.astype(jnp.float32)
    grad_act = jnp.einsum("btd,fd->btf", cotangent, w_down, preferred_element_type=jnp.float32)
    gelu_pull = jax.vjp(partial(jax.nn.gelu, approximate=False), pre_act)[1]
    grad_pre = gelu_pull(grad_act)[0].astype(jnp.bfloat16)
    grad_down_local = jnp.einsum(
        "btf,btd->fd", activated, cotangent, preferred_element_type=jnp.float32
    )
    grad_up_local = jnp.einsum(
        "btd,btf->df", normed_two, grad_pre, preferred_element_type=jnp.float32
    )
    grad_normed_two = lax.psum(
        jnp.einsum("btf,df->btd", grad_pre, w_up, preferred_element_type=jnp.float32), "tensor"
    )
    norm_two_pull = jax.vjp(layer_norm, middle, gain_two, shift_two)[1]
    grad_mid_norm, grad_gain_two, grad_shift_two = norm_two_pull(grad_normed_two)
    grad_middle = grad_output + grad_mid_norm
    grad_mid_low = grad_middle.astype(jnp.bfloat16)
    grad_out_local = jnp.einsum(
        "btk,btd->kd", mixed, grad_mid_low, preferred_element_type=jnp.float32
    )
    grad_mix = jnp.einsum("btd,kd->btk", grad_mid_low, w_out, preferred_element_type=jnp.float32)
    grad_mix = grad_mix.astype(jnp.bfloat16).reshape(batch, length, head_count, HD)
    grad_probs = jnp.einsum("bqhe,bkhe->bhqk", grad_mix, values, preferred_element_type=jnp.float32)
    row_terms = jnp.sum(attn_probs * grad_probs, axis=-1, keepdims=True)
    grad_scores = (attn_probs * (grad_probs - row_terms)).astype(jnp.bfloat16)
    grad_query = (
        jnp.einsum("bhqk,bkhe->bqhe", grad_scores, keys, preferred_element_type=jnp.float32)
        * score_scale
    )
    grad_key = (
        jnp.einsum("bhqk,bqhe->bkhe", grad_scores, queries, preferred_element_type=jnp.float32)
        * score_scale
    )
    grad_value = jnp.einsum(
        "bhqk,bqhe->bkhe", probs_low, grad_mix, preferred_element_type=jnp.float32
    )
    grad_packed = (
        jnp.stack([grad_query, grad_key, grad_value])
        .reshape(3, batch, length, local)
        .astype(jnp.bfloat16)
    )
    grad_qkv_local = jnp.einsum(
        "btd,cbte->cde", normed, grad_packed, preferred_element_type=jnp.float32
    )
    grad_normed = lax.psum(
        jnp.einsum("cbte,cde->btd", grad_packed, w_qkv, preferred_element_type=jnp.float32),
        "tensor",
    )
    norm_one_pull = jax.vjp(layer_norm, inputs, gain_one, shift_one)[1]
    grad_in_norm, grad_gain_one, grad_shift_one = norm_one_pull(grad_normed)
    grad_tokens = (grad_middle + grad_in_norm).astype(jnp.bfloat16)
    (
        qkv_part,
        out_part,
        up_part,
        down_part,
        gain_one_part,
        shift_one_part,
        gain_two_part,
        shift_two_part,
    ) = (
        lax.psum_scatter(grad_qkv_local, "dp", scatter_dimension=1, tiled=True),
        lax.psum_scatter(grad_out_local, "dp", scatter_dimension=1, tiled=True),
        lax.psum_scatter(grad_up_local, "dp", scatter_dimension=0, tiled=True),
        lax.psum_scatter(grad_down_local, "dp", scatter_dimension=1, tiled=True),
        lax.psum_scatter(grad_gain_one, "dp", scatter_dimension=0, tiled=True),
        lax.psum_scatter(grad_shift_one, "dp", scatter_dimension=0, tiled=True),
        lax.psum_scatter(grad_gain_two, "dp", scatter_dimension=0, tiled=True),
        lax.psum_scatter(grad_shift_two, "dp", scatter_dimension=0, tiled=True),
    )
    return (
        output,
        grad_tokens,
        qkv_part,
        out_part,
        up_part,
        down_part,
        gain_one_part,
        shift_one_part,
        gain_two_part,
        shift_two_part,
    )


def solution(mesh):
    in_specs = (
        P("dp", None, None),
        P("dp", None, None),
        P("dp"),
        P(None, None, "tensor"),
        P("tensor", None),
        P(None, "tensor"),
        P("tensor", None),
        P(),
        P(),
        P(),
        P(),
    )
    out_specs = (
        P("dp", None, None),
        P("dp", None, None),
        P(None, "dp", "tensor"),
        P("tensor", "dp"),
        P("dp", "tensor"),
        P("tensor", "dp"),
        P("dp"),
        P("dp"),
        P("dp"),
        P("dp"),
    )
    fast = mesh.shape["dp"] == 8 and mesh.shape["tensor"] == 4
    return jax.shard_map(
        fast_device if fast else per_device, mesh=mesh, in_specs=in_specs, out_specs=out_specs, check_vma=False
    )
```

```python
from functools import partial

import jax
import jax.numpy as jnp
from jax import lax
from jax.experimental import pallas as pl
from jax.experimental.pallas import tpu as pltpu
from jax.sharding import PartitionSpec as P

HD = 64
PATCHES = 196
EPSILON = 1e-05
MESH = pl.DeviceIdType.MESH
F32 = jnp.float32
BF16 = jnp.bfloat16
CH = 256


def mm(a, b):
    return jnp.dot(a, b, preferred_element_type=F32)


def mm_nt(a, b):
    return lax.dot_general(a, b, (((1,), (1,)), ((), ())), preferred_element_type=F32)


def mm_tn(a, b):
    return lax.dot_general(a, b, (((0,), (0,)), ((), ())), preferred_element_type=F32)


def ln_stats(v):
    mean = jnp.mean(v, axis=-1, keepdims=True)
    cen = v - mean
    var = jnp.mean(cen * cen, axis=-1, keepdims=True)
    rstd = lax.rsqrt(var + EPSILON)
    return cen * rstd, rstd


def ln_back(v, gy, gain):
    xhat, rstd = ln_stats(v)
    gx = gy * gain
    m1 = jnp.mean(gx, axis=-1, keepdims=True)
    m2 = jnp.mean(gx * xhat, axis=-1, keepdims=True)
    return rstd * (gx - m1 - xhat * m2), jnp.sum(gy * xhat, axis=0, keepdims=True), jnp.sum(gy, axis=0, keepdims=True)


def rcopy(src, dst, ssem, rsem, dev):
    return pltpu.make_async_remote_copy(
        src_ref=src, dst_ref=dst, send_sem=ssem, recv_sem=rsem, device_id=dev, device_id_type=MESH
    )


ZFIRST = (True, False, False, True, False, False, True, False, False)

PLAN = {
    ("start", 0): (("c", 0, 0, 0), ("s", 0, 1, 0), ("s", 0, 0, 0)),
    ("L", 2): (("d", 0, 0, 0),),
    ("own", 0): (("c", 1, 0, 0), ("c", 2, 0, 0)),
    ("j", 0): (("g", 0, 1, 1), ("g", 0, 0, 1)),
    ("F", 3): (("s", 1, 1, 0),),
    ("F", 5): (("s", 1, 0, 0),),
    ("j", 2): (("g", 0, 1, 2), ("s", 2, 0, 0), ("s", 2, 1, 0), ("g", 0, 0, 2), ("g", 0, 1, 3), ("g", 0, 0, 3),
        ("g", 1, 1, 1), ("g", 1, 0, 1), ("d", 1, 0, 0), ("g", 2, 0, 1), ("g", 0, 1, 4), ("g", 1, 1, 2),
        ("g", 0, 0, 4), ("w", 0, 0, 0)),
    ("j", 3): (("g", 2, 1, 1),),
    ("F", 10): (("g", 1, 0, 2),),
    ("M", 1): (("g", 2, 0, 2),),
    ("M", 2): (("g", 1, 1, 3),),
    ("O", 0): (("d", 2, 0, 0),),
    ("O", 2): (("g", 2, 1, 2),),
    ("O", 3): (("g", 1, 0, 3), ("g", 2, 0, 3)),
    ("O", 5): (("r", 0, 0, 1), ("g", 2, 1, 3)),
    ("O", 7): (("g", 1, 1, 4),),
    ("O", 11): (("r", 2, 0, 1), ("r", 3, 0, 1)),
    ("fill", 2): (("g", 1, 0, 4), ("g", 2, 0, 4), ("w", 1, 0, 0), ("g", 2, 1, 4), ("w", 2, 0, 0)),
    ("P", 1): (("r", 0, 0, 2),),
    ("n", 2): (("r", 1, 0, 1), ("r", 2, 0, 2)),
    ("P", 3): (("r", 3, 0, 2),),
    ("P", 4): (("r", 4, 0, 1),),
    ("N", 2): (("r", 1, 0, 2),),
    ("B", 2): (("r", 2, 0, 3), ("r", 0, 0, 3)),
    ("B", 3): (("r", 3, 0, 3),),
    ("B", 4): (("r", 4, 0, 2),),
    ("B", 5): (("r", 2, 0, 4), ("r", 1, 0, 3), ("r", 0, 0, 4), ("r", 5, 0, 1)),
    ("b", 1): (("r", 3, 0, 4),),
    ("B", 6): (("r", 6, 0, 1),),
    ("B", 8): (("r", 1, 0, 4),),
    ("B", 10): (("r", 8, 0, 1),),
    ("B", 11): (("r", 4, 0, 3),),
    ("fill", 5): (("r", 5, 0, 2),),
    ("fill", 6): (("r", 6, 0, 2), ("r", 7, 0, 1), ("r", 4, 0, 4), ("r", 8, 0, 2), ("r", 5, 0, 3), ("r", 6, 0, 3),
        ("r", 7, 0, 2), ("r", 6, 0, 4), ("r", 5, 0, 4), ("r", 8, 0, 3), ("r", 7, 0, 3), ("r", 8, 0, 4),
        ("r", 7, 0, 4)),
}


def layer_kernel(
    split, tokens, cots, g1, s1, g2, s2, w_qkv, w_out, w_up, w_down,
    own, wf, vecs, gqkv, gout, gffn, results, outs, gtoks,
    tok, stage, cotp, n1, qkv, prob, mx, mid, br, gn, n2, ust, wbf, ta, tb, gp, gmix,
    po, ps, cr, ra, rb, rc, gv, vcr, vr,
    isem, ksem, wsem, csend, crecv, ysend, yrecv, dsend, drecv, rcs, rcr, rsend, rrecv, osend, orecv, vsend, vrecv,
):
    ex, rows, width = tok.shape
    output, gtok = results.at[0], results.at[1]
    gup, gdown = gffn.at[0], gffn.at[1]
    rpad = n1.shape[1]
    t = ex * rpad
    d, tt = lax.axis_index("dp"), lax.axis_index("tensor")
    zh, zl, x = d // 4, lax.rem(d // 2, 2), lax.rem(d, 2)
    y, c = tt // 2, lax.rem(tt, 2)
    sib = (d, y * 2 + 1 - c)
    ynb = (d, (1 - y) * 2 + c)

    def dpi(fh, fl, fx):
        return ((1 - zh) if fh else zh) * 4 + ((1 - zl) if fl else zl) * 2 + ((1 - x) if fx else x)

    def at(fh, fl, fx):
        return ((1 - zh) if fh else zh, (1 - zl) if fl else zl, (1 - x) if fx else x)

    znb2, znb1, xnb = (dpi(1, 0, 0), tt), (dpi(0, 1, 0), tt), (dpi(0, 0, 1), tt)

    coming = [
        pltpu.make_async_copy(w_qkv.at[i], wbf.at[1, pl.ds(192 * i, 192)], isem.at[i]) for i in range(3)
    ] + [
        pltpu.make_async_copy(w_out, wbf.at[1, pl.ds(576, 192)], isem.at[3]),
        pltpu.make_async_copy(w_up, wbf.at[2], isem.at[4]),
        pltpu.make_async_copy(w_down, wbf.at[3], isem.at[5]),
        pltpu.make_async_copy(tokens.at[pl.ds(c * ex, ex)], tok, isem.at[6]),
        pltpu.make_async_copy(cots.at[pl.ds(c * ex, ex)], stage, isem.at[7]),
    ]
    for cp in coming[:4]:
        cp.start()

    peers = [sib, ynb] + [(lax.rem(d + k, 8), tt) for k in range(1, 8)]
    barrier = pltpu.get_barrier_semaphore()
    for p in peers:
        pl.semaphore_signal(barrier, 1, device_id=p, device_id_type=MESH)

    def y_slice(p, h):
        blk = (p, h) + at(0, 0, 0)
        src = own.at[blk] if p else ps.at[(h,) + at(0, 0, 0)]
        return rcopy(src, wf.at[(1,) + blk], ysend.at[p, h], yrecv.at[p, h], ynb)

    def y_direct(p):
        return rcopy(own.at[p, 2] if p else ps.at[2], wf.at[1, p, 2], ysend.at[p, 2], yrecv.at[p, 2], ynb)

    def c_first(p):
        return rcopy(own.at[p] if p else ps.at[pl.ds(0, 3)], wf.at[0, p], csend.at[p], crecv.at[p], sib)

    def c_second(p):
        return rcopy(wf.at[1, p], wf.at[2, p], csend.at[3 + p], crecv.at[3 + p], sib)

    hops = (
        (at(0, 0, 0), at(1, 0, 0), znb2),
        (at(0, 0, 0), at(0, 1, 0), znb1),
        (at(1, 0, 0), at(1, 1, 0), znb1),
        (at(0, 0, 0), at(0, 0, 1), xnb),
        (at(1, 0, 0), at(1, 0, 1), xnb),
        (at(0, 1, 0), at(0, 1, 1), xnb),
        (at(1, 1, 0), at(1, 1, 1), xnb),
    )

    def hop(p, h, k, arriving=False):
        blk = wf.at[(1, p, h) + (hops[k][1] if arriving else hops[k][0])]
        return rcopy(blk, blk, dsend.at[2 * p + h, k], drecv.at[2 * p + h, k], hops[k][2])

    def g_step(p, h, stage):
        if stage == 1:
            y_slice(p, h).wait_recv()
            go = (0, 1, 3)
        elif stage == 2:
            hop(p, h, 0, True).wait_recv()
            hop(p, h, 1, True).wait_recv()
            go = (2, 4, 5)
        elif stage == 3:
            hop(p, h, 2, True).wait_recv()
            go = (6,)
        else:
            for k in (3, 4, 5, 6):
                hop(p, h, k, True).wait_recv()
            go = ()
        for k in go:
            hop(p, h, k).start()

    def fetch(j, p, i, b):
        @pl.when(j == 0)
        def _():
            pltpu.make_async_copy(own.at[p, i], ust.at[b], wsem.at[b]).start()

        @pl.when(j > 0)
        def _():
            pltpu.make_async_copy(wf.at[jnp.maximum(j - 1, 0), p, i], ust.at[b], wsem.at[b]).start()

    def fetched(b):
        pltpu.make_async_copy(ust.at[b], ust.at[b], wsem.at[b]).wait()
        return ust[b].reshape(width, CH).astype(BF16)

    def load_attn(j):
        for i in range(3):
            fetch(j, 0, i, i)

    def take_attn(j):
        for i in range(3):
            wbf[j, :, i * CH : (i + 1) * CH] = fetched(i)

    def c_grad(u, slot):
        return rcopy(ps.at[slot], cr.at[u % 6], rcs.at[u], rcr.at[u], sib)

    def place_of(u):
        return (po, u) if u < 6 else (ust, u - 6)

    def views(pu, zfirst):
        if zfirst:
            return (
                ((pu, slice(None), 1 - zl), (pu, slice(None), zl), znb1),
                ((pu, 1 - zh, zl), (pu, zh, zl), znb2),
                ((pu, zh, zl, 1 - x), (pu, zh, zl, x), xnb),
            )
        return (
            ((pu, slice(None), slice(None), 1 - x), (pu, slice(None), slice(None), x), xnb),
            ((pu, slice(None), 1 - zl, x), (pu, slice(None), zl, x), znb1),
            ((pu, 1 - zh, zl, x), (pu, zh, zl, x), znb2),
        )

    def halving(u, k):
        ref, pu = place_of(u)
        away, _, to = views(pu, ZFIRST[u])[k]
        return rcopy(ref.at[away], (ra, rb, rc)[k].at[u], rsend.at[u, k], rrecv.at[u, k], to)

    def r_step(u, stage):
        ref, pu = place_of(u)
        view = views(pu, ZFIRST[u])
        if stage == 1:
            c_grad(u, 0).wait_recv()
            away, keep = view[0][0], view[0][1]
            ref[away] += cr[(u % 6,) + away[1:]]
            halving(u, 0).start()
            ref[keep] += cr[(u % 6,) + keep[1:]]
        elif stage < 4:
            k = stage - 2
            halving(u, k).wait_recv()
            ref[view[k][1]] += (ra, rb)[k][u]
            halving(u, k + 1).start()
        else:
            halving(u, 2).wait_recv()
            hand_out(u, ref[view[2][1]] + rc[u])

    def hand_out(u, g):
        if u < 6:
            cols = slice(u // 2 * CH, (u // 2 + 1) * CH)
            if u % 2:
                gup[:, cols] = g
            else:
                gdown[:, cols] = g
        elif u == 6:
            gqkv[0, :, :128] = g[:, :128]
            gqkv[1, :, :128] = g[:, 128:]
        elif u == 7:
            gqkv[2, :, :128] = g[:, :128]
            gqkv[0, :, 128:] = g[:, 128 : 128 + HD]
            gqkv[2, :, 128:] = g[:, 128 + HD :]
        else:
            gqkv[1, :, 128:] = g[:, :HD]
            turned = g.T
            gout[128:, :] = turned[HD:128]
            gout[:128, :] = turned[128:]

    def run(steps):
        for what, a, b, stage in steps:
            if what == "g":
                g_step(a, b, stage)
            elif what == "s":
                y_slice(a, b).start()
            elif what == "d":
                y_direct(a).start()
            elif what == "c":
                c_first(a).start()
            elif what == "w":
                y_direct(a).wait_recv()
                c_second(a).start()
            else:
                r_step(a, stage)

    def tick(at, where):
        for (name, when), steps in PLAN.items():
            if name == where:
                @pl.when(at == when)
                def _(steps=steps):
                    run(steps)

    def fill(where, at):
        run(PLAN.get((where, at), ()))

    for cp in coming[:4]:
        cp.wait()
    q_, k_, v_, o_ = 0, 192, 384, 576
    row = 0
    for src, n in (
        (q_, 128), (k_, 128), (v_, 128), (q_ + 128, HD), (v_ + 128, HD), (k_ + 128, HD), (o_ + 128, HD), (o_, 128),
    ):
        wbf[0, row : row + n, :] = wbf[1, src : src + n, :]
        row += n
    unit = ust.shape[1:]

    def keep_own(p, h, v, ref, slot):
        ref[slot] = v.astype(F32).reshape(unit)
        cp = pltpu.make_async_copy(ref.at[slot], own.at[p, h], ksem.at[p, h])
        cp.start()
        return cp

    for h in range(3):
        ps[h] = wbf[0, :, h * CH : (h + 1) * CH].astype(F32).reshape(unit)
    pl.semaphore_wait(barrier, len(peers))
    fill("start", 0)
    for cp in coming[4:]:
        cp.start()
    coming[4].wait()
    kept = [keep_own(1, h, wbf[2, :, h * CH : (h + 1) * CH], po, h) for h in range(3)]
    coming[5].wait()
    kept += [keep_own(2, h, wbf[3, h * CH : (h + 1) * CH, :].T, po, 3 + h) for h in range(3)]
    coming[6].wait()
    n1[...] = jnp.zeros_like(n1)
    mid[...] = jnp.zeros_like(mid)
    gv[...] = jnp.zeros_like(gv)

    @pl.loop(0, ex)
    def _(e):
        tick(e, "L")
        v = tok[e].astype(F32)
        xhat, _ = ln_stats(v)
        n1[e, :rows, :] = (xhat * g1[...][None] + s1[...][None]).astype(BF16)
        mid[e, :rows, :] = v

    for cp in kept:
        cp.wait()
    fill("own", 0)

    low_half = lax.broadcasted_iota(jnp.int32, (rpad, 128), 1) < HD
    qi = lax.broadcasted_iota(jnp.int32, (rpad, rpad), 0)
    kj = lax.broadcasted_iota(jnp.int32, (rpad, rpad), 1)

    def group(j, e, i):
        return qkv[j, e, :, i * 128 : (i + 1) * 128]

    def half(v, high):
        return jnp.where(low_half != high, v, jnp.zeros_like(v))

    def pair(v):
        return jnp.concatenate([half(v, False), half(v, True)], axis=0)

    @pl.loop(0, 4)
    def _(j):
        @pl.when(j > 0)
        def _():
            take_attn(j)

        @pl.when(j == 0)
        def _():
            fill("j", 0)
            c_first(0).wait_recv()
            load_attn(1)

        tick(j * 3, "F")
        qkv[j] = mm_nt(n1[...].reshape(t, width), wbf[j, :640, :]).astype(BF16).reshape(ex, rpad, 640)
        tick(j * 3 + 1, "F")

        def scores(e):
            q01, q2 = pair(group(j, e, 0)), half(group(j, e, 3), False)
            return mm_nt(q01, group(j, e, 1)), mm_nt(q2, group(j, e, 4))

        nxt = scores(0)
        for e in range(ex):
            s01, s2 = nxt
            if e + 1 < ex:
                nxt = scores(e + 1)
            allowed = kj <= jnp.maximum(qi, PATCHES - 1 + split[c * ex + e])
            ps_h = []
            for h, s in enumerate((s01[:rpad], s01[rpad:], s2)):
                s = jnp.where(allowed, s * (HD ** -0.5), -1e30)
                p = jnp.exp(s - jnp.max(s, axis=-1, keepdims=True))
                p = (p * (1.0 / jnp.sum(p, axis=-1, keepdims=True))).astype(BF16)
                prob[j, e, h] = p
                ps_h.append(p)
            o01 = mm(jnp.concatenate(ps_h[:2], axis=0), group(j, e, 2))
            o2 = mm(ps_h[2], group(j, e, 3))
            mx[j, e, :, :128] = jnp.where(low_half, 0.0, o2).astype(BF16)
            mx[j, e, :, 128:] = jnp.where(low_half, o01[:rpad], o01[rpad:]).astype(BF16)

        tick(j * 3 + 2, "F")
        mid[...] += mm(mx[j].reshape(t, 256), wbf[j, 512:, :]).reshape(ex, rpad, width)

        @pl.when(j == 1)
        def _():
            fill("j", 1)
            coming[7].wait()
            cotp[...] = jnp.zeros_like(cotp)

            @pl.loop(0, ex)
            def _(e):
                cotp[e, :rows, :] = stage[e]

            ta[...] = cotp[...].reshape(t, width).T
            fill("j", 2)
            load_attn(2)

        @pl.when(j == 2)
        def _():
            fill("j", 3)
            c_second(0).wait_recv()
            load_attn(3)

    @pl.loop(0, ex)
    def _(e):
        tick(e, "M")
        keep = lax.broadcasted_iota(jnp.int32, (rpad, 1), 0) < rows
        v = jnp.where(keep, mid[e], 0.0)
        mid[e] = v
        xhat, _ = ln_stats(v)
        n2[e] = (xhat * g2[...][None] + s2[...][None]).astype(BF16)
        br[e] = v
        gn[e] = jnp.zeros((rpad, width), F32)

    tb[...] = n2[...].reshape(t, width).T

    def chunk(b, between=None):
        u, dn = fetched(b), fetched(2 + b)
        pre = mm(n2[...].reshape(t, width), u)
        ga = mm(cotp[...].reshape(t, width), dn)
        phi = 0.5 * (1.0 + lax.erf(pre * (0.5 ** 0.5)))
        act = (pre * phi).astype(BF16)
        gpre = (ga * (phi + pre * jnp.exp(-0.5 * pre * pre) * 0.3989422804014327)).astype(BF16)
        if between is not None:
            between()
        br[...] += mm_nt(act, dn).reshape(ex, rpad, width)
        gn[...] += mm_nt(gpre, u).reshape(ex, rpad, width)
        return act, gpre

    def fetch2(j, i, b):
        fetch(j, 1, i, b)
        fetch(j, 2, i, 2 + b)

    fill("fill", 1)
    c_first(1).wait_recv()
    c_first(2).wait_recv()
    fetch2(1, 0, 0)
    shape5 = po.shape[1:]

    @pl.loop(0, 6)
    def _(n):
        i, b = n // 2, lax.rem(n, 2)

        @pl.when(n < 5)
        def _():
            fetch2(b, (n + 1) // 2, 1 - b)

        act, gpre = chunk(b, lambda: tick(2 * n, "O"))
        gd = mm(ta[...], act).reshape(shape5)
        gu = mm(tb[...], gpre).reshape(shape5)
        slot = 2 * lax.rem(i, 2)

        @pl.when(b == 0)
        def _():
            @pl.when(i == 0)
            def _():
                y_slice(0, 0).wait_send()
                y_slice(0, 1).wait_send()
                y_direct(0).wait_send()
                c_first(0).wait_send()

            @pl.when(i == 2)
            def _():
                c_grad(0, 0).wait_send()
                c_grad(1, 1).wait_send()

            ps[slot] = gd
            ps[slot + 1] = gu
            c_grad(2 * i, slot).start()
            c_grad(2 * i + 1, slot + 1).start()

        @pl.when(b == 1)
        def _():
            po[2 * i] = gd
            po[2 * i + 1] = gu

        tick(2 * n + 1, "O")

    fill("fill", 2)
    fetch2(2, 0, 0)

    @pl.loop(0, 6)
    def _(n):
        b = lax.rem(n, 2)

        @pl.when(n == 2)
        def _():
            fill("n", 2)
            c_second(1).wait_recv()
            c_second(2).wait_recv()

        @pl.when(n < 5)
        def _():
            fetch2(2 + (n + 1) // 3, lax.rem(n + 1, 3), 1 - b)

        chunk(b)
        tick(n, "P")

    o_copy = rcopy(br, outs, osend.at[0], orecv.at[0], sib)
    o_copy.start()
    fill("fill", 3)

    @pl.loop(0, ex)
    def _(e):
        tick(e, "N")
        back, dg, ds = ln_back(mid[e], gn[e], g2[...][None])
        gv[2:3, :] += dg
        gv[3:4, :] += ds
        gm = cotp[e].astype(F32) + back
        mid[e] = gm
        n2[e] = gm.astype(BF16)
        stage[e] = br[e, :rows, :].astype(BF16)
        gn[e] = jnp.zeros((rpad, width), F32)

    fill("fill", 4)
    gml = n2
    ta[...] = gml[...].reshape(t, width).T
    tb[...] = n1[...].reshape(t, width).T
    scale = HD ** -0.5

    mine, theirs = pl.ds(c * ex, ex), pl.ds((1 - c) * ex, ex)
    o_keep = pltpu.make_async_copy(stage, output.at[mine], isem.at[2])
    o_keep.start()
    o_back = pltpu.make_async_copy(outs, br, isem.at[0])
    o_other = pltpu.make_async_copy(stage, output.at[theirs], isem.at[1])

    @pl.loop(0, 4)
    def _(n):
        j = jnp.where(n < 2, 1 - n, n)
        tick(n * 3, "B")
        gmix[...] = mm_nt(gml[...].reshape(t, width), wbf[j, 512:, :]).astype(BF16).reshape(ex, rpad, 256)
        tick(n * 3 + 1, "B")

        def first(e):
            g01, g2_ = pair(gmix[e, :, 128:]), half(gmix[e, :, :128], True)
            return g01, g2_, mm_nt(g01, group(j, e, 2)), mm_nt(g2_, group(j, e, 3))

        nxt = first(0)
        for e in range(ex):
            g01, g2_, d01, d2 = nxt
            if e + 1 < ex:
                nxt = first(e + 1)
            q01 = pair(group(j, e, 0))
            ds = []
            for h, dp in enumerate((d01[:rpad], d01[rpad:], d2)):
                pf = prob[j, e, h].astype(F32)
                pd = pf * dp
                ds.append((pd - pf * jnp.sum(pd, axis=-1, keepdims=True)).astype(BF16))
            s01 = jnp.concatenate(ds[:2], axis=0)
            p01 = jnp.concatenate([prob[j, e, 0], prob[j, e, 1]], axis=0)
            dv01, dv2 = mm_tn(p01, g01), mm_tn(prob[j, e, 2], g2_)
            dq01, dq2 = mm(s01, group(j, e, 1)) * scale, mm(ds[2], group(j, e, 4)) * scale
            dk01, dk2 = mm_tn(s01, q01) * scale, mm_tn(ds[2], group(j, e, 3)) * scale
            gp[e, :, 0:128] = jnp.where(low_half, dq01[:rpad], dq01[rpad:]).astype(BF16)
            gp[e, :, 128:256] = dk01.astype(BF16)
            gp[e, :, 256:384] = dv01.astype(BF16)
            gp[e, :, 384:512] = jnp.where(low_half, dq2, dv2).astype(BF16)
            gp[e, :, 512:640] = jnp.where(low_half, dk2, 0.0).astype(BF16)

        tick(n * 3 + 2, "B")
        gpf = gp[...].reshape(t, 640)

        def grads(write):
            write(0, mm(tb[...], gpf[:, :256]).reshape(shape5))
            write(1, mm(tb[...], gpf[:, 256:512]).reshape(shape5))
            og = mm(ta[...], mx[j].reshape(t, 256))
            k2 = mm(tb[...], gpf[:, 512:640])
            write(2, jnp.concatenate([og[:, :128] + k2, og[:, 128:]], axis=1).reshape(shape5))

        @pl.when(n == 0)
        def _():
            for u in range(2, 6):
                c_grad(u, (0, 1, 2, 3, 0, 1)[u]).wait_send()

            o_copy.wait_recv()

            def write(i, g):
                ps[i] = g
                c_grad(6 + i, i).start()

            grads(write)

        @pl.when(n == 1)
        def _():
            fill("b", 0)

            def write(i, g):
                ust[i] = g

            grads(write)
            fill("b", 1)
            o_copy.wait_send()
            o_back.start()

        gn[...] += mm(gpf, wbf[j, :640, :]).reshape(ex, rpad, width)

        @pl.when(n == 2)
        def _():
            o_back.wait()
            o_keep.wait()

            @pl.loop(0, ex)
            def _(e):
                stage[e] = br[e, :rows, :].astype(BF16)

            o_other.start()

    fill("fill", 5)

    o_other.wait()

    @pl.loop(0, ex)
    def _(e):
        back, dg, ds = ln_back(tok[e].astype(F32), gn[e, :rows, :], g1[...][None])
        gv[0:1, :] += dg
        gv[1:2, :] += ds
        g = mid[e, :rows, :] + back
        br[e, :rows, :] = g
        tok[e] = g.astype(BF16)

    t_copy = rcopy(br, gtoks, osend.at[1], orecv.at[1], sib)
    t_copy.start()
    t_keep = pltpu.make_async_copy(tok, gtok.at[mine], isem.at[2])
    t_keep.start()
    t_back = pltpu.make_async_copy(gtoks, gn, isem.at[0])
    v_copy = rcopy(gv, vcr, osend.at[2], orecv.at[2], sib)
    v_copy.start()
    last = PLAN[("fill", 6)]
    run(last[: len(last) // 2])
    v_copy.wait()
    gv[...] += vcr[...]
    v_sends = []
    for k in range(1, 8):
        cp = rcopy(gv, vr.at[7 - k], vsend.at[k - 1], vrecv.at[7 - k], (lax.rem(d + k, 8), tt))
        cp.start()
        v_sends.append(cp)
    t_copy.wait()
    t_back.start()
    run(last[len(last) // 2 : -1])
    for k in range(1, 8):
        rcopy(gv, vr.at[k - 1], vsend.at[k - 1], vrecv.at[k - 1], sib).wait_recv()
    acc = None
    for i in range(8):
        k = lax.rem(i - d + 8, 8)
        term = jnp.where(k == 0, gv[...], vr[jnp.maximum(k - 1, 0)])
        acc = term if acc is None else acc + term
    mine_v = jnp.zeros(vecs.shape, F32)
    for i in range(8):
        mine_v = jnp.where(d == i, acc[:, i * (width // 8) : (i + 1) * (width // 8)], mine_v)
    vecs[...] = mine_v
    t_back.wait()
    t_keep.wait()

    @pl.loop(0, ex)
    def _(e):
        tok[e] = gn[e, :rows, :].astype(BF16)

    t_other = pltpu.make_async_copy(tok, gtok.at[theirs], isem.at[1])
    t_other.start()
    run(last[-1:])

    for cp in v_sends:
        cp.wait_send()
    for p in range(3):
        c_second(p).wait_send()
        if p:
            y_direct(p).wait_send()
            c_first(p).wait_send()
        for h in range(2):
            if p:
                y_slice(p, h).wait_send()
            for k in range(7):
                hop(p, h, k).wait_send()
    for u in range(9):
        for k in range(3):
            halving(u, k).wait_send()
    for u in range(6, 9):
        c_grad(u, u - 6).wait_send()
    t_other.wait()


def layer(split, tokens, cots, g1, s1, g2, s2, w_qkv, w_out, w_up, w_down):
    batch, rows, width = tokens.shape
    ex = batch // 2
    rpad = -(-rows // 16) * 16
    t = ex * rpad
    band = width // 8
    sds = jax.ShapeDtypeStruct
    dma = pltpu.SemaphoreType.DMA
    vm = pltpu.VMEM
    ANY = pl.BlockSpec(memory_space=pl.ANY)
    VM = pl.BlockSpec(memory_space=pltpu.VMEM)
    SM = pl.BlockSpec(memory_space=pltpu.SMEM)
    act = (ex, rpad, width)
    unit = (2, 2, 2, band, CH)
    return pl.pallas_call(
        layer_kernel,
        out_shape=(
            sds((3, 3) + unit, F32), sds((3, 3, 3) + unit, F32), sds((8, band), F32),
            sds((3, band, 192), F32), sds((192, band), F32), sds((2, band, 768), F32),
            sds((2,) + tokens.shape, BF16), sds(act, F32), sds(act, F32),
        ),
        in_specs=[SM, ANY, ANY, VM, VM, VM, VM, ANY, ANY, ANY, ANY],
        out_specs=(ANY, ANY, VM, VM, VM, VM, ANY, ANY, ANY),
        scratch_shapes=[
            vm((ex, rows, width), BF16), vm((ex, rows, width), BF16), vm(act, BF16), vm(act, BF16),
            vm((4, ex, rpad, 640), BF16), vm((4, ex, 3, rpad, rpad), BF16), vm((4, ex, rpad, 256), BF16),
            vm(act, F32), vm(act, F32), vm(act, F32), vm(act, BF16),
            vm((4,) + unit, F32), vm((4, width, 768), BF16),
            vm((width, t), BF16), vm((width, t), BF16), vm((ex, rpad, 640), BF16), vm((ex, rpad, 256), BF16),
            vm((6,) + unit, F32), vm((4,) + unit, F32), vm((6,) + unit, F32),
            vm((9, 2, 2, band, CH), F32), vm((9, 2, band, CH), F32), vm((9, band, CH), F32),
            vm((8, width), F32), vm((8, width), F32), vm((7, 8, width), F32),
            dma((8,)), dma((3, 3)), dma((4,)), dma((6,)), dma((6,)), dma((3, 3)), dma((3, 3)), dma((6, 7)), dma((6, 7)),
            dma((9,)), dma((9,)), dma((9, 3)), dma((9, 3)), dma((3,)), dma((3,)), dma((7,)), dma((7,)),
        ],
        compiler_params=pltpu.CompilerParams(collective_id=0, has_side_effects=True, vmem_limit_bytes=VLIM),
        name="layer",
    )(split, tokens, cots, g1, s1, g2, s2, w_qkv, w_out, w_up, w_down)


VLIM = 64 * 1024 * 1024 - 64 * 1024


def fast_device(tokens, cotangent, split_point, w_qkv, w_out, w_up, w_down, gain_one, shift_one, gain_two, shift_two):
    batch, length, width = tokens.shape
    _, _, vecs, gqkv, gout, gffn, results, _, _ = layer(
        split_point, tokens, cotangent, gain_one, shift_one, gain_two, shift_two,
        w_qkv.transpose(0, 2, 1), w_out, w_up, w_down,
    )
    return results[0], results[1], gqkv, gout, gffn[0], gffn[1].T, vecs[0], vecs[1], vecs[2], vecs[3]


def layer_norm(values, gain_vec, shift_vec):
    row_mean = jnp.mean(values, axis=-1, keepdims=True)
    centered = values - row_mean
    variance = jnp.mean(centered * centered, axis=-1, keepdims=True)
    return centered * lax.rsqrt(variance + EPSILON) * gain_vec + shift_vec


def attention_forward(inputs, allowed, w_qkv, w_out, gain_one, shift_one):
    batch, length, width = inputs.shape
    local = w_qkv.shape[2]
    head_count = local // HD
    normed = layer_norm(inputs, gain_one, shift_one).astype(jnp.bfloat16)
    packed = jnp.einsum("btd,cde->cbte", normed, w_qkv, preferred_element_type=jnp.float32).astype(
        jnp.bfloat16
    )
    queries = packed[0].reshape(batch, length, head_count, HD)
    keys = packed[1].reshape(batch, length, head_count, HD)
    values = packed[2].reshape(batch, length, head_count, HD)
    scores = jnp.einsum(
        "bqhe,bkhe->bhqk", queries, keys, preferred_element_type=jnp.float32
    ) * HD ** (-0.5)
    scores = jnp.where(allowed[:, None], scores, -1e30)
    log_total = jax.nn.logsumexp(scores, axis=-1, keepdims=True)
    attn_probs = jnp.exp(scores - log_total)
    probs_low = attn_probs.astype(jnp.bfloat16)
    mixed = jnp.einsum("bhqk,bkhe->bqhe", probs_low, values, preferred_element_type=jnp.float32)
    mixed = mixed.reshape(batch, length, local).astype(jnp.bfloat16)
    partial_out = jnp.einsum("btk,kd->btd", mixed, w_out, preferred_element_type=jnp.float32)
    return (normed, queries, keys, values, attn_probs, probs_low, mixed, partial_out)


def mlp_forward(middle, w_up, gain_two, shift_two):
    normed_two = layer_norm(middle, gain_two, shift_two).astype(jnp.bfloat16)
    pre_act = jnp.einsum("btd,df->btf", normed_two, w_up, preferred_element_type=jnp.float32)
    activated = jax.nn.gelu(pre_act, approximate=False).astype(jnp.bfloat16)
    return (normed_two, pre_act, activated)


def per_device(
    tokens,
    cotangent,
    split_point,
    w_qkv,
    w_out,
    w_up,
    w_down,
    gain_one,
    shift_one,
    gain_two,
    shift_two,
):
    inputs = tokens.astype(jnp.float32)
    batch, length, width = tokens.shape
    local = w_qkv.shape[2]
    head_count = local // HD
    score_scale = HD ** (-0.5)
    places = jnp.arange(length, dtype=jnp.int32)
    limit = jnp.maximum(places[None, :, None], PATCHES + split_point[:, None, None] - 1)
    allowed = places[None, None, :] <= limit
    normed, queries, keys, values, attn_probs, probs_low, mixed, partial_out = attention_forward(
        inputs, allowed, w_qkv, w_out, gain_one, shift_one
    )
    middle = inputs + lax.psum(partial_out, "tensor")
    normed_two, pre_act, activated = mlp_forward(middle, w_up, gain_two, shift_two)
    branch = jnp.einsum("btf,fd->btd", activated, w_down, preferred_element_type=jnp.float32)
    output = (middle + lax.psum(branch, "tensor")).astype(jnp.bfloat16)
    normed, queries, keys, values, attn_probs, probs_low, mixed, partial_out = attention_forward(
        inputs, allowed, w_qkv, w_out, gain_one, shift_one
    )
    middle = inputs + lax.psum(partial_out, "tensor")
    normed_two, pre_act, activated = mlp_forward(middle, w_up, gain_two, shift_two)
    grad_output = cotangent.astype(jnp.float32)
    grad_act = jnp.einsum("btd,fd->btf", cotangent, w_down, preferred_element_type=jnp.float32)
    gelu_pull = jax.vjp(partial(jax.nn.gelu, approximate=False), pre_act)[1]
    grad_pre = gelu_pull(grad_act)[0].astype(jnp.bfloat16)
    grad_down_local = jnp.einsum(
        "btf,btd->fd", activated, cotangent, preferred_element_type=jnp.float32
    )
    grad_up_local = jnp.einsum(
        "btd,btf->df", normed_two, grad_pre, preferred_element_type=jnp.float32
    )
    grad_normed_two = lax.psum(
        jnp.einsum("btf,df->btd", grad_pre, w_up, preferred_element_type=jnp.float32), "tensor"
    )
    norm_two_pull = jax.vjp(layer_norm, middle, gain_two, shift_two)[1]
    grad_mid_norm, grad_gain_two, grad_shift_two = norm_two_pull(grad_normed_two)
    grad_middle = grad_output + grad_mid_norm
    grad_mid_low = grad_middle.astype(jnp.bfloat16)
    grad_out_local = jnp.einsum(
        "btk,btd->kd", mixed, grad_mid_low, preferred_element_type=jnp.float32
    )
    grad_mix = jnp.einsum("btd,kd->btk", grad_mid_low, w_out, preferred_element_type=jnp.float32)
    grad_mix = grad_mix.astype(jnp.bfloat16).reshape(batch, length, head_count, HD)
    grad_probs = jnp.einsum("bqhe,bkhe->bhqk", grad_mix, values, preferred_element_type=jnp.float32)
    row_terms = jnp.sum(attn_probs * grad_probs, axis=-1, keepdims=True)
    grad_scores = (attn_probs * (grad_probs - row_terms)).astype(jnp.bfloat16)
    grad_query = (
        jnp.einsum("bhqk,bkhe->bqhe", grad_scores, keys, preferred_element_type=jnp.float32)
        * score_scale
    )
    grad_key = (
        jnp.einsum("bhqk,bqhe->bkhe", grad_scores, queries, preferred_element_type=jnp.float32)
        * score_scale
    )
    grad_value = jnp.einsum(
        "bhqk,bqhe->bkhe", probs_low, grad_mix, preferred_element_type=jnp.float32
    )
    grad_packed = (
        jnp.stack([grad_query, grad_key, grad_value])
        .reshape(3, batch, length, local)
        .astype(jnp.bfloat16)
    )
    grad_qkv_local = jnp.einsum(
        "btd,cbte->cde", normed, grad_packed, preferred_element_type=jnp.float32
    )
    grad_normed = lax.psum(
        jnp.einsum("cbte,cde->btd", grad_packed, w_qkv, preferred_element_type=jnp.float32),
        "tensor",
    )
    norm_one_pull = jax.vjp(layer_norm, inputs, gain_one, shift_one)[1]
    grad_in_norm, grad_gain_one, grad_shift_one = norm_one_pull(grad_normed)
    grad_tokens = (grad_middle + grad_in_norm).astype(jnp.bfloat16)
    (
        qkv_part,
        out_part,
        up_part,
        down_part,
        gain_one_part,
        shift_one_part,
        gain_two_part,
        shift_two_part,
    ) = (
        lax.psum_scatter(grad_qkv_local, "dp", scatter_dimension=1, tiled=True),
        lax.psum_scatter(grad_out_local, "dp", scatter_dimension=1, tiled=True),
        lax.psum_scatter(grad_up_local, "dp", scatter_dimension=0, tiled=True),
        lax.psum_scatter(grad_down_local, "dp", scatter_dimension=1, tiled=True),
        lax.psum_scatter(grad_gain_one, "dp", scatter_dimension=0, tiled=True),
        lax.psum_scatter(grad_shift_one, "dp", scatter_dimension=0, tiled=True),
        lax.psum_scatter(grad_gain_two, "dp", scatter_dimension=0, tiled=True),
        lax.psum_scatter(grad_shift_two, "dp", scatter_dimension=0, tiled=True),
    )
    return (
        output,
        grad_tokens,
        qkv_part,
        out_part,
        up_part,
        down_part,
        gain_one_part,
        shift_one_part,
        gain_two_part,
        shift_two_part,
    )


def solution(mesh):
    in_specs = (
        P("dp", None, None),
        P("dp", None, None),
        P("dp"),
        P(None, None, "tensor"),
        P("tensor", None),
        P(None, "tensor"),
        P("tensor", None),
        P(),
        P(),
        P(),
        P(),
    )
    out_specs = (
        P("dp", None, None),
        P("dp", None, None),
        P(None, "dp", "tensor"),
        P("tensor", "dp"),
        P("dp", "tensor"),
        P("tensor", "dp"),
        P("dp"),
        P("dp"),
        P("dp"),
        P("dp"),
    )
    fast = mesh.shape["dp"] == 8 and mesh.shape["tensor"] == 4
    return jax.shard_map(
        fast_device if fast else per_device, mesh=mesh, in_specs=in_specs, out_specs=out_specs, check_vma=False
    )
```
